32 devices in a mesh: dp: 4 (over y, x), fsdp: 8 (over z, core).
Axes of the slice: x: 2, y: 2, z: 4, core: 2. Of those that a mesh axis runs over, the one named last changes fastest.
Arguments:
- layer_input: bfloat16 [64, 256, 768], P(('dp', 'fsdp')), may hold values from -6 to 6
- encoder_states: bfloat16 [64, 256, 768], P(('dp', 'fsdp')), may hold values from -6 to 6
- output_grad: bfloat16 [64, 256, 768], P(('dp', 'fsdp')), may hold values from -6 to 6
- span_start: int32 [64], P(('dp', 'fsdp')), may hold values from 0 to 128, as said below
- span_length: int32 [64], P(('dp', 'fsdp')), may hold values from 128 to 256, as said below
- self_project: bfloat16 [3, 768, 768], P(None, ('dp', 'fsdp')), may hold values from -0.21875 to 0.21875
- self_output: bfloat16 [768, 768], P(('dp', 'fsdp')), may hold values from -1.75 to 1.75
- cross_project: bfloat16 [3, 768, 768], P(None, ('dp', 'fsdp')), may hold values from -0.21875 to 0.21875
- cross_output: bfloat16 [768, 768], P(('dp', 'fsdp')), may hold values from -1.75 to 1.75
- attend_bias: bfloat16 [6, 768], P(None, ('dp', 'fsdp')), may hold values from -1.796875 to 1.796875
- expand_weight: bfloat16 [768, 3072], P(('dp', 'fsdp')), may hold values from -0.21875 to 0.21875
- expand_bias: bfloat16 [3072], P(('dp', 'fsdp')), may hold values from -1.796875 to 1.796875
- contract_weight: bfloat16 [3072, 768], P(('dp', 'fsdp')), may hold values from -0.109375 to 0.109375
- contract_bias: bfloat16 [768], P(('dp', 'fsdp')), may hold values from -1.796875 to 1.796875
- norm_gain: bfloat16 [3, 768], P(None, ('dp', 'fsdp')), may hold values from 0.25 to 1.75
- norm_shift: bfloat16 [3, 768], P(None, ('dp', 'fsdp')), may hold values from -1.796875 to 1.796875
Outputs:
- layer_output: bfloat16 [64, 256, 768], P(('dp', 'fsdp'))
- input_grad: float32 [64, 256, 768], P(('dp', 'fsdp'))
- encoder_grad: float32 [64, 256, 768], P(('dp', 'fsdp'))
- self_project_grad: float32 [3, 768, 768], P(None, ('dp', 'fsdp'))
- self_output_grad: float32 [768, 768], P(('dp', 'fsdp'))
- cross_project_grad: float32 [3, 768, 768], P(None, ('dp', 'fsdp'))
- cross_output_grad: float32 [768, 768], P(('dp', 'fsdp'))
- attend_bias_grad: float32 [6, 768], P(None, ('dp', 'fsdp'))
- expand_weight_grad: float32 [768, 3072], P(('dp', 'fsdp'))
- expand_bias_grad: float32 [3072], P(('dp', 'fsdp'))
- contract_weight_grad: float32 [3072, 768], P(('dp', 'fsdp'))
- contract_bias_grad: float32 [768], P(('dp', 'fsdp'))
- norm_gain_grad: float32 [3, 768], P(None, ('dp', 'fsdp'))
- norm_shift_grad: float32 [3, 768], P(None, ('dp', 'fsdp'))
The draws below stay inside these ranges and needn't reach their ends.
Inputs may be any that keep to these rules, and one draw needn't show every extreme that they name: span_start + span_length <= 256 for every sequence; some sequence has its span start at 0, some at 128. `span_length`: some sequence has a span of exactly 256 tokens and some of exactly 128.
All inputs are finite; a program needn't handle non-finite values.
Results may differ from the reference program's by a relative error of at most 0.025.
Values may be sent and summed in bfloat16 or wider, within the bound.
No kernel may reach another device: no remote copies, remote signals or barrier semaphores. Data moves between devices by JAX's collectives and lax.ppermute only.
A program may use at most 256 MiB of HBM per device.

```python
import jax
import jax.numpy as jnp
from jax import lax

D = 768
H = 12
HD = 64
FF = 3072
PIC = 256
MICRO = 2
LEN = 256
ENC = 256
SEQS = 64


def draw_spans(key):
    base = jax.random.fold_in(key, 11)
    length_key = jax.random.fold_in(base, 1)
    start_key = jax.random.fold_in(base, 2)
    pick_key = jax.random.fold_in(base, 3)
    lengths = jax.random.randint(length_key, (SEQS,), PIC // 2, PIC + 1, dtype=jnp.int32)
    chosen = jax.random.randint(pick_key, (), 0, SEQS, dtype=jnp.int32)
    second = (chosen + 1) % SEQS
    lengths = lengths.at[chosen].set(PIC)
    lengths = lengths.at[second].set(PIC // 2)
    room = LEN - lengths + 1
    starts = jax.random.randint(start_key, (SEQS,), 0, room, dtype=jnp.int32)
    starts = starts.at[chosen].set(0)
    starts = starts.at[second].set(LEN - PIC // 2)
    return (starts.astype(jnp.int32), lengths.astype(jnp.int32))


def draw_span_start(key, part):
    return draw_spans(key)[0]


def draw_span_length(key, part):
    return draw_spans(key)[1]


def steps_of(rng, shape, split, smallest, top_value):
    level = 1.0
    for axis_at, shards_of in split:
        steps = jax.random.uniform(jax.random.fold_in(jax.random.fold_in(rng, 6), axis_at), (shards_of,), jnp.float32, smallest / len(split), top_value / len(split))
        level = level * jnp.repeat(jnp.exp(steps), shape[axis_at] // shards_of).reshape((-1,) + (1,) * (len(shape) - 1 - axis_at))
    return level


def noise(key, shape, scale, limit, cuts=(), held_as=jnp.bfloat16):
    result = scale * jax.random.normal(key, shape, jnp.float32)
    if cuts:
        result = result * steps_of(key, shape, cuts, -0.22, 0.18)
    return jnp.clip(result, -limit, limit).astype(held_as)


def setup_inputs(seed: int = 0) -> dict:
    seeds = jax.random.split(jax.random.key(seed), 17)
    return {
        "layer_input": noise(seeds[0], (SEQS, LEN, D), 1.0, 6.0, ((0, 32),)),
        "encoder_states": noise(seeds[1], (SEQS, ENC, D), 1.0, 6.0, ((0, 32),)),
        "output_grad": noise(seeds[2], (SEQS, LEN, D), 1.0, 6.0, ((0, 32),)),
        "span_start": draw_span_start(jax.random.fold_in(seeds[16], 71), 0),
        "span_length": draw_span_length(jax.random.fold_in(seeds[16], 71), 0),
        "self_project": noise(seeds[5], (3, D, D), D ** -0.5, 0.21875, ((1, 32),)),
        "self_output": noise(seeds[6], (D, D), (D // 64) ** -0.5, 1.75, ((0, 32),)),
        "cross_project": noise(seeds[7], (3, D, D), D ** -0.5, 0.21875, ((1, 32),)),
        "cross_output": noise(seeds[8], (D, D), (D // 64) ** -0.5, 1.75, ((0, 32),)),
        "attend_bias": noise(seeds[9], (6, D), 0.3, 1.796875, ((1, 32),)),
        "expand_weight": noise(seeds[10], (D, FF), D ** -0.5, 0.21875, ((0, 32),)),
        "expand_bias": noise(seeds[11], (FF,), 0.3, 1.796875, ((0, 32),)),
        "contract_weight": noise(seeds[12], (FF, D), FF ** -0.5, 0.109375, ((0, 32),)),
        "contract_bias": noise(seeds[13], (D,), 0.3, 1.796875, ((0, 32),)),
        "norm_gain": jnp.clip(1.0 + 0.15 * jax.random.normal(seeds[14], (3, D), jnp.float32), 0.25, 1.75).astype(jnp.bfloat16),
        "norm_shift": noise(seeds[15], (3, D), 0.3, 1.796875, ((1, 32),)),
    }


eps_norm = 1e-05
big_negative = -1000000000.0

@jax.custom_vjp
def low(v):
    return lax.optimization_barrier(v.astype(jnp.bfloat16)).astype(jnp.float32)

@jax.custom_vjp
def low_back(v):
    return v

def low_keep(v):
    return (low(v), None)

def low_pass(kept, grad):
    return (grad,)

def back_keep(v):
    return (v, None)

def back_low(kept, grad):
    return (low(grad),)
low.defvjp(low_keep, low_pass)
low_back.defvjp(back_keep, back_low)

def round_both(value):
    return low(low_back(value))

def product(left_side, right_side):
    return jnp.dot(left_side, right_side, precision=lax.Precision.HIGHEST)

def layer_norm(summed, gain, shift):
    centre = summed - lax.optimization_barrier(jnp.mean(summed, axis=-1, keepdims=True))
    spread = lax.optimization_barrier(jnp.mean(centre * centre, axis=-1, keepdims=True))
    return centre * lax.rsqrt(spread + eps_norm) * gain + shift

def gelu_exact(value):
    return jax.nn.gelu(value, approximate=False)

def attend(queries, key_rows, values, allowed):
    groups, row_count = (queries.shape[0], queries.shape[1])
    key_count = key_rows.shape[1]
    query_heads = queries.reshape(groups, row_count, H, HD)
    key_heads = key_rows.reshape(groups, key_count, H, HD)
    value_heads = values.reshape(groups, key_count, H, HD)
    scores = low_back(jnp.einsum('gqhe,gkhe->ghqk', query_heads, key_heads, precision=lax.Precision.HIGHEST))
    if allowed is not None:
        scores = jnp.where(allowed[:, None], scores, big_negative)
    peak_score = lax.optimization_barrier(jnp.max(scores, axis=-1, keepdims=True))
    exp_scores = jnp.exp(scores - peak_score)
    soft_weights = low(exp_scores / lax.optimization_barrier(jnp.sum(exp_scores, axis=-1, keepdims=True)))
    attended = jnp.einsum('ghqk,gkhe->gqhe', soft_weights, value_heads, precision=lax.Precision.HIGHEST)
    return round_both(attended.reshape(groups, row_count, H * HD))

def forward(tokens, memory, params, allowed):
    self_project, self_output, cross_project, cross_output, attend_bias, expand_weight, expand_bias, contract_weight, contract_bias, norm_gain, norm_shift = params
    queries = round_both((product(tokens, self_project[0]) + attend_bias[0]) * 0.125)
    key_rows = round_both(product(tokens, self_project[1]))
    values = round_both(product(tokens, self_project[2]) + attend_bias[1])
    attended = attend(queries, key_rows, values, allowed)
    first_norm = layer_norm(tokens + low_back(product(attended, self_output) + attend_bias[2]), norm_gain[0], norm_shift[0])
    cross_queries = round_both((product(low(first_norm), cross_project[0]) + attend_bias[3]) * 0.125)
    cross_keys = round_both(product(memory, cross_project[1]))
    cross_values = round_both(product(memory, cross_project[2]) + attend_bias[4])
    cross_mixed = attend(cross_queries, cross_keys, cross_values, None)
    second_norm = layer_norm(first_norm + low_back(product(cross_mixed, cross_output) + attend_bias[5]), norm_gain[1], norm_shift[1])
    hidden_pre = low_back(product(low(second_norm), expand_weight) + expand_bias)
    hidden_act = low(gelu_exact(hidden_pre))
    third_sum = second_norm + low_back(product(hidden_act, contract_weight) + contract_bias)
    return layer_norm(third_sum, norm_gain[2], norm_shift[2])

def reference(layer_input, encoder_states, output_grad, span_start, span_length, self_project, self_output, cross_project, cross_output, attend_bias, expand_weight, expand_bias, contract_weight, contract_bias, norm_gain, norm_shift):
    params = tuple((weight.astype(jnp.float32) for weight in (self_project, self_output, cross_project, cross_output, attend_bias, expand_weight, expand_bias, contract_weight, contract_bias, norm_gain, norm_shift)))
    groups = SEQS // MICRO

    def regroup(tensor):
        return tensor.reshape((groups, MICRO) + tensor.shape[1:])
    entries = (regroup(layer_input), regroup(encoder_states), regroup(output_grad), regroup(span_start), regroup(span_length))
    positions = jnp.arange(LEN, dtype=jnp.int32)

    def group_step(totals, entry):
        tokens, memory, grad_out, starts, lengths = entry
        inside = (positions[None, :] >= starts[:, None]) & (positions[None, :] < (starts + lengths)[:, None])
        allowed = (positions[None, None, :] <= positions[None, :, None]) | inside[:, :, None] & inside[:, None, :]

        def run_layer(tok_values, mem_values, param_values):
            return forward(tok_values, mem_values, param_values, allowed)
        output, pullback = jax.vjp(run_layer, tokens.astype(jnp.float32), memory.astype(jnp.float32), params)
        grad_tokens, grad_memory, grad_params = pullback(grad_out.astype(jnp.float32))
        totals = jax.tree.map(jnp.add, totals, grad_params)
        return (totals, (output.astype(jnp.bfloat16), grad_tokens, grad_memory))
    zero_grads = tuple((jnp.zeros_like(weight) for weight in params))
    totals, (outputs, input_grads, memory_grads) = lax.scan(group_step, zero_grads, entries)
    return (outputs.reshape(SEQS, LEN, D), input_grads.reshape(SEQS, LEN, D), memory_grads.reshape(SEQS, ENC, D), totals[0], totals[1], totals[2], totals[3], totals[4], totals[5], totals[6], totals[7], totals[8], totals[9], totals[10])
```

```python
import functools

import jax
import jax.numpy as jnp
import numpy as np
from jax import lax
from jax.experimental import pallas as pl
from jax.experimental.pallas import tpu as pltpu
from jax.sharding import PartitionSpec as P

D = 768
H = 12
HD = 64
FF = 3072
AXES = ("dp", "fsdp")

EPS = 1e-05
BIG_NEGATIVE = -1000000000.0
HEADS_PER_STEP = 4
BF = jnp.bfloat16
F32 = jnp.float32


class Place:
    def __init__(self):
        self.dp_count = lax.axis_size("dp")
        self.inner = lax.axis_size("fsdp")
        self.chips = self.inner // 2
        self.dp = lax.axis_index("dp")
        inner = lax.axis_index("fsdp")
        self.chip = inner // 2
        self.core = inner % 2
        self.bits = int(np.log2(self.dp_count))

    def bit(self, core, step):
        return 1 << (self.bits - 1 - step if core == 0 else step)

    def mask(self, relative):
        values = [
            sum(self.bit(core, s) for s in range(self.bits) if relative >> s & 1)
            for core in (0, 1)
        ]
        return jnp.where(self.core == 0, values[0], values[1])

    def permute(self, value, target):
        pairs = []
        for dp in range(self.dp_count):
            for chip in range(self.chips):
                for core in range(2):
                    to = target(dp, chip, core)
                    pairs.append(
                        (
                            dp * self.inner + chip * 2 + core,
                            to[0] * self.inner + to[1] * 2 + to[2],
                        )
                    )
        return lax.ppermute(value, AXES, pairs)

    def across_cores(self, value):
        return self.permute(value, lambda d, z, c: (d, z, 1 - c))

    def across_step(self, value, step):
        return self.permute(value, lambda d, z, c: (d ^ self.bit(c, step), z, c))

    def along_chips(self, value, shift):
        return self.permute(value, lambda d, z, c: (d, (z + shift) % self.chips, c))


def owner_blocks(place, gradient):
    rows = gradient.shape[0] // (place.dp_count * place.inner)
    return gradient.reshape(
        place.dp_count, place.chips, 2, rows, gradient.shape[-1]
    )


def reduce_to_owner(place, blocks):
    others = [place.across_cores(b) for b in blocks]

    def chip_sum(where):
        parts = []
        for mine, other in zip(blocks, others):
            shape = (1, place.chips, 1) + mine.shape[3:]
            at = (where, 0, place.core, 0, 0)
            both = lax.dynamic_slice(mine, at, shape).astype(F32) + lax.dynamic_slice(
                other, at, shape
            ).astype(F32)
            parts.append(both.reshape((place.chips,) + mine.shape[3:]))
        return parts[0] if len(parts) == 1 else jnp.concatenate(parts, axis=1)

    arrived = {m: [] for m in range(1 << place.bits)}

    def total(relative):
        value = chip_sum(place.dp ^ place.mask(relative))
        for a in arrived[relative]:
            value = value + a.astype(F32)
        return value

    for step in range(place.bits):
        leaving = [
            m
            for m in range(1 << place.bits)
            if m >> step & 1 and not m & ((1 << step) - 1)
        ]
        sent = jnp.stack([total(m).astype(BF) for m in leaving])
        got = place.across_step(sent, step)
        for i, m in enumerate(leaving):
            arrived[m ^ (1 << step)].append(got[i])
    own = total(0)
    low = own.astype(BF)

    def chip_row(value, shift):
        return lax.dynamic_index_in_dim(
            value, (place.chip + shift) % place.chips, 0, keepdims=False
        )

    result = chip_row(own, 0)
    for shift in range(1, place.chips):
        result = result + place.along_chips(chip_row(low, shift), shift).astype(F32)
    return result


def dot_nt(a, b):
    return lax.dot_general(a, b, (((1,), (1,)), ((), ())), preferred_element_type=F32)


def dot_nn(a, b):
    return jnp.dot(a, b, preferred_element_type=F32)


def dot_tn(a, b):
    return lax.dot_general(a, b, (((0,), (0,)), ((), ())), preferred_element_type=F32)


def attend_kernel(masked, start_ref, length_ref, q_ref, k_ref, v_ref, o_ref, p_ref):
    rows = q_ref.shape[0]
    keys = k_ref.shape[0]
    if masked:
        seq = pl.program_id(0)
        start = start_ref[seq]
        stop = start + length_ref[seq]
        key_at = lax.broadcasted_iota(jnp.int32, (keys, rows), 0)
        row_at = lax.broadcasted_iota(jnp.int32, (keys, rows), 1)
        inside = (key_at >= start) & (key_at < stop) & (row_at >= start) & (row_at < stop)
        allowed = (key_at <= row_at) | inside
    values_t = v_ref[...].T
    pieces = []
    for h in range(HEADS_PER_STEP):
        cols = slice(h * HD, (h + 1) * HD)
        scores = dot_nt(k_ref[:, cols], q_ref[:, cols])
        if masked:
            scores = jnp.where(allowed, scores, BIG_NEGATIVE)
        peak = jnp.max(scores, axis=0, keepdims=True)
        weights = jnp.exp(scores - peak)
        total = jnp.sum(weights, axis=0, keepdims=True)
        low = (weights * (1.0 / total)).astype(BF)
        p_ref[0, h] = low
        pieces.append(dot_nn(values_t[cols], low))
    o_ref[...] = jnp.concatenate(pieces, axis=0).T.astype(BF)


def attend(queries, keys, values, start, length, masked, count):
    rows = queries.shape[0] // count
    key_rows = keys.shape[0] // count
    width = HEADS_PER_STEP * HD
    block = lambda n: pl.BlockSpec((n, width), lambda s, g, *_: (s, g))
    return pl.pallas_call(
        functools.partial(attend_kernel, masked),
        grid_spec=pltpu.PrefetchScalarGridSpec(
            num_scalar_prefetch=2,
            grid=(count, H // HEADS_PER_STEP),
            in_specs=[block(rows), block(key_rows), block(key_rows)],
            out_specs=[
                block(rows),
                pl.BlockSpec(
                    (1, HEADS_PER_STEP, key_rows, rows), lambda s, g, *_: (s, g, 0, 0)
                ),
            ],
        ),
        out_shape=[
            jax.ShapeDtypeStruct(queries.shape, BF),
            jax.ShapeDtypeStruct((count, H, key_rows, rows), BF),
        ],
        compiler_params=pltpu.CompilerParams(vmem_limit_bytes=24 << 20),
        name="attend",
    )(start, length, queries, keys, values)


def attend_back_kernel(q_ref, k_ref, v_ref, p_ref, g_ref, dq_ref, dk_ref, dv_ref):
    keys_t = k_ref[...].T
    dq, dk, dv = [], [], []
    for h in range(HEADS_PER_STEP):
        cols = slice(h * HD, (h + 1) * HD)
        grads = g_ref[:, cols]
        low = p_ref[0, h]
        weights = low.astype(F32)
        moved = dot_nt(v_ref[:, cols], grads)
        centre = jnp.sum(weights * moved, axis=0, keepdims=True)
        ds = (weights * (moved - centre)).astype(BF)
        dk.append(dot_nn(ds, q_ref[:, cols]))
        dv.append(dot_nn(low, grads))
        dq.append(dot_nn(keys_t[cols], ds))
    dq_ref[...] = jnp.concatenate(dq, axis=0).T.astype(BF)
    dk_ref[...] = jnp.concatenate(dk, axis=1).astype(BF)
    dv_ref[...] = jnp.concatenate(dv, axis=1).astype(BF)


def attend_back(queries, keys, values, weights, grads, count):
    rows = queries.shape[0] // count
    key_rows = keys.shape[0] // count
    width = HEADS_PER_STEP * HD
    block = lambda n: pl.BlockSpec((n, width), lambda s, g: (s, g))
    return pl.pallas_call(
        attend_back_kernel,
        grid=(count, H // HEADS_PER_STEP),
        in_specs=[
            block(rows),
            block(key_rows),
            block(key_rows),
            pl.BlockSpec((1, HEADS_PER_STEP, key_rows, rows), lambda s, g: (s, g, 0, 0)),
            block(rows),
        ],
        out_specs=[block(rows), block(key_rows), block(key_rows)],
        out_shape=[
            jax.ShapeDtypeStruct(queries.shape, BF),
            jax.ShapeDtypeStruct(keys.shape, BF),
            jax.ShapeDtypeStruct(keys.shape, BF),
        ],
        compiler_params=pltpu.CompilerParams(vmem_limit_bytes=24 << 20),
        name="attend_back",
    )(queries, keys, values, weights, grads)


def norm(summed):
    centre = summed - jnp.mean(summed, axis=-1, keepdims=True)
    scale = lax.rsqrt(jnp.mean(centre * centre, axis=-1, keepdims=True) + EPS)
    return centre * scale, scale


def norm_back(normal, scale, gain, grad):
    inner = grad * gain
    back = scale * (
        inner
        - jnp.mean(inner, axis=-1, keepdims=True)
        - normal * jnp.mean(inner * normal, axis=-1, keepdims=True)
    )
    return back, jnp.sum(grad * normal, axis=0), jnp.sum(grad, axis=0)


def gelu_and_slope(value):
    spread = 0.5 * (1.0 + lax.erf(value * np.float32(np.sqrt(0.5))))
    density = jnp.exp(-0.5 * value * value) * np.float32(1.0 / np.sqrt(2.0 * np.pi))
    return value * spread, spread + value * density


def gather_weights(shards):
    (sp, so, cp, co, ab, ew, eb, cw, cb, ng, ns) = shards
    rows = so.shape[0]
    small = jnp.concatenate([a.reshape(-1) for a in (ab, eb, cb, ng, ns)])
    used = small.shape[0]
    small = jnp.pad(small, (0, 8 * D - used)).reshape(8, D)
    packed = jnp.concatenate(
        [
            sp.reshape(-1, D),
            so,
            cp.reshape(-1, D),
            co,
            ew.reshape(rows, FF // D, D).swapaxes(0, 1).reshape(-1, D),
            cw,
            small,
        ]
    )
    whole = lax.all_gather(packed, AXES, axis=0, tiled=False)
    count = whole.shape[0]

    def square(i):
        return whole[:, i * rows : (i + 1) * rows].reshape(D, D)

    squares = [square(i) for i in range(12)]
    contract = whole[:, 12 * rows : 12 * rows + cw.shape[0]].reshape(FF, D)
    tail = whole[:, 12 * rows + cw.shape[0]].astype(F32)
    at = 0
    smalls = []
    for a in (ab, eb, cb, ng, ns):
        piece = tail[:, at : at + a.size].reshape((count,) + a.shape)
        at += a.size
        smalls.append(
            piece.reshape(-1) if a.ndim == 1 else piece.swapaxes(0, 1).reshape(a.shape[0], -1)
        )
    return squares, contract, smalls


def body(
    layer_input,
    encoder_states,
    output_grad,
    span_start,
    span_length,
    self_project,
    self_output,
    cross_project,
    cross_output,
    attend_bias,
    expand_weight,
    expand_bias,
    contract_weight,
    contract_bias,
    norm_gain,
    norm_shift,
):
    place = Place()
    count, length = layer_input.shape[:2]
    shape = layer_input.shape
    x = layer_input.reshape(-1, D)
    memory = encoder_states.reshape(-1, D)
    grad_out = output_grad.reshape(-1, D).astype(F32)
    squares, contract, smalls = gather_weights(
        (
            self_project,
            self_output,
            cross_project,
            cross_output,
            attend_bias,
            expand_weight,
            expand_bias,
            contract_weight,
            contract_bias,
            norm_gain,
            norm_shift,
        )
    )
    wq, wk, wv, wo, cq, ck, cv, co = squares[:8]
    expand = jnp.concatenate(squares[8:], axis=1)
    biases, expand_b, contract_b, gains, shifts = smalls

    q = ((dot_nn(x, wq) + biases[0]) * 0.125).astype(BF)
    k = dot_nn(x, wk).astype(BF)
    v = (dot_nn(x, wv) + biases[1]).astype(BF)
    o, p = attend(q, k, v, span_start, span_length, True, count)
    n1, s1 = norm(x.astype(F32) + (dot_nn(o, wo) + biases[2]))
    x1 = n1 * gains[0] + shifts[0]
    x1b = x1.astype(BF)
    q2 = ((dot_nn(x1b, cq) + biases[3]) * 0.125).astype(BF)
    k2 = dot_nn(memory, ck).astype(BF)
    v2 = (dot_nn(memory, cv) + biases[4]).astype(BF)
    o2, p2 = attend(q2, k2, v2, span_start, span_length, False, count)
    n2, s2 = norm(x1 + (dot_nn(o2, co) + biases[5]))
    x2 = n2 * gains[1] + shifts[1]
    x2b = x2.astype(BF)
    act, slope = gelu_and_slope(dot_nn(x2b, expand) + expand_b)
    act = act.astype(BF)
    slope = slope.astype(BF)
    n3, s3 = norm(x2 + (dot_nn(act, contract) + contract_b))
    output = (n3 * gains[2] + shifts[2]).astype(BF)

    dr3, gain3, shift3 = norm_back(n3, s3, gains[2], grad_out)
    df = dr3.astype(BF)
    d_contract = dot_tn(act, df).astype(BF)
    d_contract_b = jnp.sum(df.astype(F32), axis=0)
    du = (dot_nt(df, contract) * slope.astype(F32)).astype(BF)
    d_expand = dot_tn(x2b, du).astype(BF)
    d_expand_b = jnp.sum(du.astype(F32), axis=0)
    own_contract = reduce_to_owner(place, [owner_blocks(place, d_contract)])
    own_expand = reduce_to_owner(place, [owner_blocks(place, d_expand)])

    dr2, gain2, shift2 = norm_back(n2, s2, gains[1], dr3 + dot_nt(du, expand))
    dc = dr2.astype(BF)
    d_co = dot_tn(o2, dc).astype(BF)
    do2 = dot_nt(dc, co).astype(BF)
    dq2, dk2, dv2 = attend_back(q2, k2, v2, p2, do2, count)
    dq2 = dq2 * BF(0.125)
    d_cross = [dot_tn(x1b, dq2), dot_tn(memory, dk2), dot_tn(memory, dv2)]
    own_cross = reduce_to_owner(
        place, [owner_blocks(place, d.astype(BF)) for d in d_cross + [d_co]]
    )
    encoder_grad = dot_nt(dk2, ck) + dot_nt(dv2, cv)

    dr1, gain1, shift1 = norm_back(n1, s1, gains[0], dr2 + dot_nt(dq2, cq))
    da = dr1.astype(BF)
    d_so = dot_tn(o, da).astype(BF)
    do = dot_nt(da, wo).astype(BF)
    dq, dk, dv = attend_back(q, k, v, p, do, count)
    dq = dq * BF(0.125)
    d_self = [dot_tn(x, dq), dot_tn(x, dk), dot_tn(x, dv)]
    input_grad = dr1 + dot_nt(dq, wq) + dot_nt(dk, wk) + dot_nt(dv, wv)

    def column_sum(value):
        return jnp.sum(value.astype(F32), axis=0)

    d_bias = jnp.stack(
        [column_sum(t) for t in (dq, dv, da, dq2, dv2, dc)]
    )
    smalls_out = [
        d_bias,
        d_expand_b,
        d_contract_b,
        jnp.stack([gain1, gain2, gain3]),
        jnp.stack([shift1, shift2, shift3]),
    ]
    devices = place.dp_count * place.inner
    flat = []
    for s in smalls_out:
        by_owner = s.reshape(s.shape[:-1] + (devices, -1))
        flat.append(jnp.moveaxis(by_owner, -2, 0).reshape(devices, -1))
    flat = jnp.concatenate(flat, axis=1)
    flat = jnp.pad(flat, ((0, 0), (0, 8 * D - flat.shape[1]))).astype(BF)
    small_blocks = flat.reshape(place.dp_count, place.chips, 2, 8, D)
    own_self = reduce_to_owner(
        place,
        [owner_blocks(place, d.astype(BF)) for d in d_self + [d_so]] + [small_blocks],
    )
    rows = self_output.shape[0]
    tail = own_self[4 * rows]
    at = 0
    own_small = []
    for a in (attend_bias, expand_bias, contract_bias, norm_gain, norm_shift):
        own_small.append(tail[at : at + a.size].reshape(a.shape))
        at += a.size
    return (
        output.reshape(shape),
        input_grad.reshape(shape),
        encoder_grad.reshape(encoder_states.shape),
        own_self[: 3 * rows].reshape(3, rows, D),
        own_self[3 * rows : 4 * rows],
        own_cross[: 3 * rows].reshape(3, rows, D),
        own_cross[3 * rows :],
        own_small[0],
        own_expand,
        own_small[1],
        own_contract,
        own_small[2],
        own_small[3],
        own_small[4],
    )


def solution(mesh):
    rows = P(AXES)
    return jax.shard_map(
        body,
        mesh=mesh,
        in_specs=(
            P(AXES, None, None),
            P(AXES, None, None),
            P(AXES, None, None),
            P(AXES),
            P(AXES),
            P(None, AXES, None),
            P(AXES, None),
            P(None, AXES, None),
            P(AXES, None),
            P(None, AXES),
            P(AXES, None),
            P(AXES),
            P(AXES, None),
            P(AXES),
            P(None, AXES),
            P(None, AXES),
        ),
        out_specs=(
            P(AXES, None, None),
            P(AXES, None, None),
            P(AXES, None, None),
            P(None, AXES, None),
            P(AXES, None),
            P(None, AXES, None),
            P(AXES, None),
            P(None, AXES),
            P(AXES, None),
            P(AXES),
            P(AXES, None),
            P(AXES),
            P(None, AXES),
            P(None, AXES),
        ),
        check_vma=False,
    )
```

```python
import functools

import jax
import jax.numpy as jnp
import numpy as np
from jax import lax
from jax.experimental import pallas as pl
from jax.experimental.pallas import tpu as pltpu
from jax.sharding import PartitionSpec as P

D = 768
H = 12
HD = 64
FF = 3072
AXES = ("dp", "fsdp")

EPS = 1e-05
BIG_NEGATIVE = -1000000000.0
HEADS_PER_STEP = 4
BF = jnp.bfloat16
F32 = jnp.float32


class Place:
    def __init__(self):
        self.dp_count = lax.axis_size("dp")
        self.inner = lax.axis_size("fsdp")
        self.chips = self.inner // 2
        self.bits = int(np.log2(self.dp_count))
        self.dp = lax.axis_index("dp")
        inner = lax.axis_index("fsdp")
        self.chip = inner // 2
        self.core = inner % 2
        table = []
        for dp in range(self.dp_count):
            for chip in range(self.chips):
                for core in range(2):
                    table.append(
                        [dp ^ self.mask(core, m) for m in range(self.dp_count)]
                        + [dp ^ self.mask(1 - core, m) for m in range(self.dp_count)]
                        + [(chip + k) % self.chips for k in range(self.chips)]
                        + [(chip - k) % self.chips for k in range(self.chips)]
                        + [core, 1 - core]
                    )
        index = self.dp * self.inner + inner
        self.spots = lax.dynamic_index_in_dim(
            jnp.asarray(np.array(table, np.int32)), index, 0, keepdims=False
        )
        self.theirs_at = self.dp_count
        self.up_at = 2 * self.dp_count
        self.down_at = self.up_at + self.chips
        self.core_at = self.down_at + self.chips

    def bit(self, core, step):
        return 1 << (self.bits - 1 - step if core == 0 else step)

    def mask(self, core, relative):
        return sum(self.bit(core, s) for s in range(self.bits) if relative >> s & 1)

    def permute(self, value, target):
        pairs = []
        for dp in range(self.dp_count):
            for chip in range(self.chips):
                for core in range(2):
                    to = target(dp, chip, core)
                    pairs.append(
                        (
                            dp * self.inner + chip * 2 + core,
                            to[0] * self.inner + to[1] * 2 + to[2],
                        )
                    )
        return lax.ppermute(value, AXES, pairs)

    def across_cores(self, value):
        return self.permute(value, lambda d, z, c: (d, z, 1 - c))

    def across_step(self, value, step):
        return self.permute(value, lambda d, z, c: (d ^ self.bit(c, step), z, c))

    def along_chips(self, value, shift):
        return self.permute(value, lambda d, z, c: (d, (z + shift) % self.chips, c))


def after(values, *earlier):
    return lax.optimization_barrier((values, earlier))[0]


def copy_kernel(plan, n_in, spots_ref, *refs):
    ins, outs, sems = refs[:n_in], refs[n_in:-1], refs[-1]
    copies = []
    for i, (source, source_at, target, target_at) in enumerate(plan):
        copies.append(
            pltpu.make_async_copy(
                ins[source].at[source_at(spots_ref)],
                outs[target].at[target_at(spots_ref)],
                sems.at[i],
            )
        )
    for c in copies:
        c.start()
    for c in copies:
        c.wait()


def copy_call(place, plan, ins, outs, name):
    anywhere = pl.BlockSpec(memory_space=pl.ANY)
    return pl.pallas_call(
        functools.partial(copy_kernel, plan, len(ins)),
        grid_spec=pltpu.PrefetchScalarGridSpec(
            num_scalar_prefetch=1,
            grid=(1,),
            in_specs=[anywhere] * len(ins),
            out_specs=[anywhere] * len(outs),
            scratch_shapes=[pltpu.SemaphoreType.DMA((len(plan),))],
        ),
        out_shape=outs,
        compiler_params=pltpu.CompilerParams(vmem_limit_bytes=1 << 20),
        name=name,
    )(place.spots, *ins)


class Gather:
    def __init__(self, place, local):
        self.place = place
        self.local = local
        self.got = [local] + [
            place.along_chips(local, k) for k in range(1, place.chips)
        ]

    def column(self):
        place = self.place
        plan = [
            (
                k,
                lambda s: (slice(None),),
                0,
                lambda s, k=k: (s[place.down_at + k],),
            )
            for k in range(place.chips)
        ]
        shape = jax.ShapeDtypeStruct((place.chips,) + self.local.shape, BF)
        self.blocks = {0: copy_call(place, plan, self.got, [shape], "column")[0]}
        return self.blocks[0]

    def hop(self, step, held):
        self.blocks[held | 1 << step] = self.place.across_step(self.blocks[held], step)

    def share(self, held):
        return self.place.across_cores(self.blocks[held])

    def spread(self, parts):
        place = self.place
        others = [self.share(m) for m in range(place.dp_count)]
        ins = [self.blocks[m] for m in range(place.dp_count)] + others
        cols = self.local.shape[1]
        plan, outs = [], []
        for out, (first, rows) in enumerate(parts):
            outs.append(
                jax.ShapeDtypeStruct((place.dp_count, place.chips, 2, rows, cols), BF)
            )
            for m in range(2 * place.dp_count):
                core = place.core_at + (m >= place.dp_count)
                plan.append(
                    (
                        m,
                        lambda s, a=first, n=rows: (slice(None), pl.ds(a, n)),
                        out,
                        lambda s, m=m, core=core: (s[m], slice(None), s[core]),
                    )
                )
        whole = copy_call(place, plan, ins, outs, "spread")
        return [w.reshape(-1, cols) for w in whole]


def sum_refs(refs, n, arrived):
    parts = []
    for mine, other in zip(refs[:n], refs[n : 2 * n]):
        shape = mine.shape[-2:]
        lead = mine.shape[1:2]
        parts.append(
            (mine[...].astype(F32) + other[...].astype(F32)).reshape(lead + shape)
        )
    value = parts[0] if n == 1 else jnp.concatenate(parts, axis=1)
    for a in refs[2 * n : 2 * n + arrived]:
        value = value + a[...].astype(F32).reshape(value.shape)
    return value


def leave_kernel(n, arrived, spots_ref, *refs):
    out = refs[-1]
    out[...] = sum_refs(refs[:-1], n, arrived).astype(BF).reshape(out.shape)


def last_kernel(n, arrived, chips, spots_ref, *refs):
    each = 2 * n + arrived
    outs = refs[chips * each :]
    for k in range(chips):
        value = sum_refs(refs[k * each : (k + 1) * each], n, arrived)
        outs[k][...] = value.astype(outs[k].dtype).reshape(outs[k].shape)


class Reduce:
    def __init__(self, place, blocks):
        self.place = place
        self.blocks = blocks
        self.rows = sum(b.shape[3] for b in blocks)
        self.cols = blocks[0].shape[4]
        self.others = [place.across_cores(b) for b in blocks]
        self.got = []

    def leave(self, step):
        place = self.place
        count = 1 << (place.bits - 1 - step)
        chips, core = place.chips, place.core_at

        def spot(i, s):
            return s[(1 << step) + i * (2 << step)]

        specs = [
            pl.BlockSpec(
                (1, chips, 1) + b.shape[3:], lambda i, s: (spot(i, s), 0, s[core], 0, 0)
            )
            for b in self.blocks
        ] * 2
        for t in range(step):
            specs.append(
                pl.BlockSpec(
                    (1, chips, self.rows, self.cols),
                    lambda i, s, t=t: ((1 << (step - t - 1)) + i * (1 << (step - t)), 0, 0, 0),
                )
            )
        sent = pl.pallas_call(
            functools.partial(leave_kernel, len(self.blocks), step),
            grid_spec=pltpu.PrefetchScalarGridSpec(
                num_scalar_prefetch=1,
                grid=(count,),
                in_specs=specs,
                out_specs=pl.BlockSpec(
                    (1, chips, self.rows, self.cols), lambda i, s: (i, 0, 0, 0)
                ),
            ),
            out_shape=jax.ShapeDtypeStruct((count, chips, self.rows, self.cols), BF),
            compiler_params=pltpu.CompilerParams(vmem_limit_bytes=24 << 20),
            name="leave",
        )(place.spots, *self.blocks, *self.others, *self.got)
        self.got.append(place.across_step(sent, step))
        return self.got[-1]

    def last(self):
        place = self.place
        chips, core = place.chips, place.core_at
        specs, ins = [], []
        for k in range(chips):
            up = place.up_at + k
            for b in self.blocks + self.others:
                ins.append(b)
                specs.append(
                    pl.BlockSpec(
                        (1, 1, 1) + b.shape[3:],
                        lambda i, s, up=up: (s[0], s[up], s[core], 0, 0),
                    )
                )
            for g in self.got:
                ins.append(g)
                specs.append(
                    pl.BlockSpec(
                        (1, 1, self.rows, self.cols), lambda i, s, up=up: (0, s[up], 0, 0)
                    )
                )
        flat = pl.BlockSpec((self.rows, self.cols), lambda i, s: (0, 0))
        own, *sent = pl.pallas_call(
            functools.partial(last_kernel, len(self.blocks), place.bits, chips),
            grid_spec=pltpu.PrefetchScalarGridSpec(
                num_scalar_prefetch=1, grid=(1,), in_specs=specs, out_specs=[flat] * chips
            ),
            out_shape=[
                jax.ShapeDtypeStruct((self.rows, self.cols), F32 if k == 0 else BF)
                for k in range(chips)
            ],
            compiler_params=pltpu.CompilerParams(vmem_limit_bytes=24 << 20),
            name="last",
        )(place.spots, *ins)
        self.own = own
        self.came = [place.along_chips(v, k + 1) for k, v in enumerate(sent)]
        return self.came

    def result(self):
        total = self.own
        for c in self.came:
            total = total + c.astype(F32)
        return total


def owner_blocks(place, gradient):
    rows = gradient.shape[0] // (place.dp_count * place.inner)
    return gradient.reshape(
        place.dp_count, place.chips, 2, rows, gradient.shape[-1]
    )


class PlainReduce:
    def __init__(self, place, blocks):
        devices = place.dp_count * place.inner
        flat = [b.reshape((devices,) + b.shape[3:]) for b in blocks]
        self.sum = lax.psum_scatter(
            jnp.concatenate(flat, axis=1), AXES, scatter_dimension=0, tiled=False
        )

    def leave(self, step):
        return self.sum

    def last(self):
        return self.sum

    def result(self):
        return self.sum.astype(F32)


def dot_nt(a, b):
    return lax.dot_general(a, b, (((1,), (1,)), ((), ())), preferred_element_type=F32)


def dot_nn(a, b):
    return jnp.dot(a, b, preferred_element_type=F32)


def dot_tn(a, b):
    return lax.dot_general(a, b, (((0,), (0,)), ((), ())), preferred_element_type=F32)


def attend_kernel(masked, start_ref, length_ref, q_ref, k_ref, v_ref, o_ref, p_ref):
    rows = q_ref.shape[0]
    keys = k_ref.shape[0]
    if masked:
        seq = pl.program_id(0)
        start = start_ref[seq]
        stop = start + length_ref[seq]
        key_at = lax.broadcasted_iota(jnp.int32, (keys, rows), 0)
        row_at = lax.broadcasted_iota(jnp.int32, (keys, rows), 1)
        inside = (key_at >= start) & (key_at < stop) & (row_at >= start) & (row_at < stop)
        allowed = (key_at <= row_at) | inside
    values_t = v_ref[...].T
    pieces = []
    for h in range(HEADS_PER_STEP):
        cols = slice(h * HD, (h + 1) * HD)
        scores = dot_nt(k_ref[:, cols], q_ref[:, cols])
        if masked:
            scores = jnp.where(allowed, scores, BIG_NEGATIVE)
        peak = jnp.max(scores, axis=0, keepdims=True)
        weights = jnp.exp(scores - peak)
        total = jnp.sum(weights, axis=0, keepdims=True)
        low = (weights * (1.0 / total)).astype(BF)
        p_ref[0, h] = low
        pieces.append(dot_nn(values_t[cols], low))
    o_ref[...] = jnp.concatenate(pieces, axis=0).T.astype(BF)


def attend(queries, keys, values, start, length, masked, count):
    rows = queries.shape[0] // count
    key_rows = keys.shape[0] // count
    width = HEADS_PER_STEP * HD
    block = lambda n: pl.BlockSpec((n, width), lambda s, g, *_: (s, g))
    return pl.pallas_call(
        functools.partial(attend_kernel, masked),
        grid_spec=pltpu.PrefetchScalarGridSpec(
            num_scalar_prefetch=2,
            grid=(count, H // HEADS_PER_STEP),
            in_specs=[block(rows), block(key_rows), block(key_rows)],
            out_specs=[
                block(rows),
                pl.BlockSpec(
                    (1, HEADS_PER_STEP, key_rows, rows), lambda s, g, *_: (s, g, 0, 0)
                ),
            ],
        ),
        out_shape=[
            jax.ShapeDtypeStruct(queries.shape, BF),
            jax.ShapeDtypeStruct((count, H, key_rows, rows), BF),
        ],
        compiler_params=pltpu.CompilerParams(vmem_limit_bytes=24 << 20),
        name="attend",
    )(start, length, queries, keys, values)


def attend_back_kernel(q_ref, k_ref, v_ref, p_ref, g_ref, dq_ref, dk_ref, dv_ref):
    keys_t = k_ref[...].T
    dq, dk, dv = [], [], []
    for h in range(HEADS_PER_STEP):
        cols = slice(h * HD, (h + 1) * HD)
        grads = g_ref[:, cols]
        low = p_ref[0, h]
        weights = low.astype(F32)
        moved = dot_nt(v_ref[:, cols], grads)
        centre = jnp.sum(weights * moved, axis=0, keepdims=True)
        ds = (weights * (moved - centre)).astype(BF)
        dk.append(dot_nn(ds, q_ref[:, cols]))
        dv.append(dot_nn(low, grads))
        dq.append(dot_nn(keys_t[cols], ds))
    dq_ref[...] = jnp.concatenate(dq, axis=0).T.astype(BF)
    dk_ref[...] = jnp.concatenate(dk, axis=1).astype(BF)
    dv_ref[...] = jnp.concatenate(dv, axis=1).astype(BF)


def attend_back(queries, keys, values, weights, grads, count):
    rows = queries.shape[0] // count
    key_rows = keys.shape[0] // count
    width = HEADS_PER_STEP * HD
    block = lambda n: pl.BlockSpec((n, width), lambda s, g: (s, g))
    return pl.pallas_call(
        attend_back_kernel,
        grid=(count, H // HEADS_PER_STEP),
        in_specs=[
            block(rows),
            block(key_rows),
            block(key_rows),
            pl.BlockSpec((1, HEADS_PER_STEP, key_rows, rows), lambda s, g: (s, g, 0, 0)),
            block(rows),
        ],
        out_specs=[block(rows), block(key_rows), block(key_rows)],
        out_shape=[
            jax.ShapeDtypeStruct(queries.shape, BF),
            jax.ShapeDtypeStruct(keys.shape, BF),
            jax.ShapeDtypeStruct(keys.shape, BF),
        ],
        compiler_params=pltpu.CompilerParams(vmem_limit_bytes=24 << 20),
        name="attend_back",
    )(queries, keys, values, weights, grads)


def norm(summed):
    centre = summed - jnp.mean(summed, axis=-1, keepdims=True)
    scale = lax.rsqrt(jnp.mean(centre * centre, axis=-1, keepdims=True) + EPS)
    return centre * scale, scale


def norm_back(normal, scale, gain, grad):
    inner = grad * gain
    back = scale * (
        inner
        - jnp.mean(inner, axis=-1, keepdims=True)
        - normal * jnp.mean(inner * normal, axis=-1, keepdims=True)
    )
    return back, jnp.sum(grad * normal, axis=0), jnp.sum(grad, axis=0)


def gelu_and_slope(value):
    spread = 0.5 * (1.0 + lax.erf(value * np.float32(np.sqrt(0.5))))
    density = jnp.exp(-0.5 * value * value) * np.float32(1.0 / np.sqrt(2.0 * np.pi))
    return value * spread, spread + value * density


def pack_small_kernel(ab_ref, eb_ref, cb_ref, ng_ref, ns_ref, out_ref):
    out_ref[...] = jnp.zeros_like(out_ref)
    n = ab_ref.shape[1]
    out_ref[0:6, 0:n] = ab_ref[...].astype(F32)
    out_ref[6:7, 0:n] = cb_ref[...].astype(F32)
    out_ref[0:3, 128 : 128 + n] = ng_ref[...].astype(F32)
    out_ref[3:6, 128 : 128 + n] = ns_ref[...].astype(F32)
    out_ref[0:1, 256 : 256 + eb_ref.shape[1]] = eb_ref[...].astype(F32)


def pack_small(ab, eb, cb, ng, ns):
    return pl.pallas_call(
        pack_small_kernel,
        out_shape=jax.ShapeDtypeStruct((8, D), F32),
        compiler_params=pltpu.CompilerParams(vmem_limit_bytes=4 << 20),
        name="pack_small",
    )(ab, eb.reshape(1, -1), cb.reshape(1, -1), ng, ns).astype(BF)


def unpack_small_kernel(n, wide, in_ref, rows_ref, eb_ref):
    for d in range(in_ref.shape[0]):
        block = in_ref[d].astype(F32)
        rows_ref[0:8, d * n : (d + 1) * n] = block[:, 0:n]
        rows_ref[8:16, d * n : (d + 1) * n] = block[:, 128 : 128 + n]
        eb_ref[:, d * wide : (d + 1) * wide] = block[0:1, 256 : 256 + wide]


def unpack_small(gathered, n, wide):
    devices = gathered.shape[0]
    return pl.pallas_call(
        functools.partial(unpack_small_kernel, n, wide),
        out_shape=[
            jax.ShapeDtypeStruct((16, devices * n), F32),
            jax.ShapeDtypeStruct((1, devices * wide), F32),
        ],
        compiler_params=pltpu.CompilerParams(vmem_limit_bytes=8 << 20),
        name="unpack_small",
    )(gathered)


def split_small_kernel(n, wide, rows_ref, eb_ref, out_ref):
    for d in range(out_ref.shape[0]):
        left = rows_ref[0:8, d * n : (d + 1) * n]
        right = rows_ref[8:16, d * n : (d + 1) * n]
        tail = eb_ref[0:8, d * wide : (d + 1) * wide]
        block = jnp.zeros(out_ref.shape[1:], F32)

        def padded(v):
            return jnp.concatenate(
                [v, jnp.zeros((8, 128 - v.shape[1]), F32)], axis=1
            )

        out_ref[d] = jnp.concatenate(
            [padded(left), padded(right), padded(tail), block[:, 384:]], axis=1
        ).astype(BF)


def split_small(rows, eb, n, wide):
    devices = rows.shape[1] // n
    return pl.pallas_call(
        functools.partial(split_small_kernel, n, wide),
        out_shape=jax.ShapeDtypeStruct((devices, 8, D), BF),
        compiler_params=pltpu.CompilerParams(vmem_limit_bytes=8 << 20),
        name="split_small",
    )(rows, eb)


def body(
    layer_input,
    encoder_states,
    output_grad,
    span_start,
    span_length,
    self_project,
    self_output,
    cross_project,
    cross_output,
    attend_bias,
    expand_weight,
    expand_bias,
    contract_weight,
    contract_bias,
    norm_gain,
    norm_shift,
):
    place = Place()
    count, length = layer_input.shape[:2]
    shape = layer_input.shape
    rows = self_output.shape[0]
    wide = expand_bias.shape[0]
    fits = rows % 8 == 0
    reduce = Reduce if fits else PlainReduce
    x = layer_input.reshape(-1, D)
    memory = encoder_states.reshape(-1, D)
    grad_out = output_grad.reshape(-1, D).astype(F32)

    small = pack_small(attend_bias, expand_bias, contract_bias, norm_gain, norm_shift)
    local_self = jnp.concatenate([self_project.reshape(-1, D), self_output, small])
    local_cross = jnp.concatenate([cross_project.reshape(-1, D), cross_output])
    four = [(i * rows, rows) for i in range(4)]
    if fits:
        g_self = Gather(place, local_self)
        line = g_self.column()
        g_cross = Gather(place, after(local_cross, line))
        g_self.hop(0, 0)
        g_self.hop(1, 0)
        g_self.hop(1, 1)
        *w_self, smalls = g_self.spread(four + [(4 * rows, 8)])
        line = after(g_cross, g_self.blocks[1]) if False else None
        g_cross.column()
        g_cross.hop(0, 0)
        g_cross.hop(1, 0)
        g_cross.hop(1, 1)
        w_cross = g_cross.spread(four)
        g_expand = Gather(place, after(expand_weight, g_cross.blocks[0]))
        g_contract = Gather(place, after(contract_weight, g_cross.blocks[0]))
        g_expand.column()
        g_expand.hop(0, 0)
        g_expand.hop(1, 0)
        g_expand.hop(1, 1)
        (expand,) = g_expand.spread([(0, rows)])
        g_contract.column()
        g_contract.hop(0, 0)
        g_contract.hop(1, 0)
        g_contract.hop(1, 1)
        (contract,) = g_contract.spread([(0, contract_weight.shape[0])])
        smalls = smalls.reshape(-1, 8, D)
    else:
        whole = lax.all_gather(
            jnp.concatenate([local_self, local_cross, contract_weight]), AXES, axis=0
        )
        squares = [
            whole[:, a : a + rows].reshape(D, D)
            for a in [i * rows for i in range(4)]
            + [4 * rows + 8 + i * rows for i in range(4)]
        ]
        w_self, w_cross = squares[:4], squares[4:]
        contract = whole[:, 8 * rows + 8 :].reshape(FF, D)
        smalls = whole[:, 4 * rows : 4 * rows + 8]
        expand = lax.all_gather(expand_weight, AXES, axis=0, tiled=True)
    wq, wk, wv, wo = w_self
    cq, ck, cv, co = w_cross
    small_rows, expand_b = unpack_small(smalls, rows, wide)
    biases = [small_rows[i : i + 1] for i in range(6)]
    contract_b = small_rows[6:7]
    gains = [small_rows[8 + i : 9 + i] for i in range(3)]
    shifts = [small_rows[11 + i : 12 + i] for i in range(3)]

    q = ((dot_nn(x, wq) + biases[0]) * 0.125).astype(BF)
    k = dot_nn(x, wk).astype(BF)
    v = (dot_nn(x, wv) + biases[1]).astype(BF)
    o, p = attend(q, k, v, span_start, span_length, True, count)
    n1, s1 = norm(x.astype(F32) + (dot_nn(o, wo) + biases[2]))
    x1 = n1 * gains[0] + shifts[0]
    x1b = x1.astype(BF)
    q2 = ((dot_nn(x1b, cq) + biases[3]) * 0.125).astype(BF)
    k2 = dot_nn(memory, ck).astype(BF)
    v2 = (dot_nn(memory, cv) + biases[4]).astype(BF)
    o2, p2 = attend(q2, k2, v2, span_start, span_length, False, count)
    n2, s2 = norm(x1 + (dot_nn(o2, co) + biases[5]))
    x2 = n2 * gains[1] + shifts[1]
    x2b = x2.astype(BF)
    act, slope = gelu_and_slope(dot_nn(x2b, expand) + expand_b)
    act = act.astype(BF)
    slope = slope.astype(BF)
    n3, s3 = norm(x2 + (dot_nn(act, contract) + contract_b))
    output = (n3 * gains[2] + shifts[2]).astype(BF)

    dr3, gain3, shift3 = norm_back(n3, s3, gains[2], grad_out)
    df = dr3.astype(BF)
    d_contract = dot_tn(act, df).astype(BF)
    r_contract = reduce(place, [owner_blocks(place, d_contract)])
    d_contract_b = jnp.sum(df.astype(F32), axis=0)
    du = (dot_nt(after(df, d_contract), contract) * slope.astype(F32)).astype(BF)
    d_expand = dot_tn(x2b, du).astype(BF)
    r_expand = reduce(place, [owner_blocks(place, d_expand)])
    hop = r_contract.leave(0)
    d_expand_b = jnp.sum(du.astype(F32), axis=0)

    dr2, gain2, shift2 = norm_back(
        n2, s2, gains[1], dr3 + dot_nt(after(du, d_expand), expand)
    )
    dc = dr2.astype(BF)
    d_co = dot_tn(o2, dc).astype(BF)
    do2 = dot_nt(dc, co).astype(BF)
    do2 = after(do2, hop, d_co)
    hop = r_contract.leave(1)
    hop2 = r_expand.leave(0)
    dq2, dk2, dv2 = attend_back(q2, k2, v2, p2, do2, count)
    dq2 = dq2 * BF(0.125)
    dq2, dk2, dv2 = after((dq2, dk2, dv2), hop)
    d_cross = [dot_tn(x1b, dq2), dot_tn(memory, dk2), dot_tn(memory, dv2)]
    d_cross = [d.astype(BF) for d in d_cross]
    r_cross = reduce(place, [owner_blocks(place, d) for d in d_cross + [d_co]])
    came = r_contract.last()
    dq2, dk2, dv2 = after((dq2, dk2, dv2), d_cross, hop2)
    hop2 = r_expand.leave(1)
    encoder_grad = dot_nt(dk2, ck) + dot_nt(dv2, cv)

    dr1, gain1, shift1 = norm_back(n1, s1, gains[0], dr2 + dot_nt(dq2, cq))
    da = dr1.astype(BF)
    d_so = dot_tn(o, da).astype(BF)
    do = dot_nt(da, wo).astype(BF)
    do = after(do, hop2, came, encoder_grad, d_so)
    own_contract = r_contract.result()
    hop = r_cross.leave(0)
    came = r_expand.last()
    dq, dk, dv = attend_back(q, k, v, p, do, count)
    dq = dq * BF(0.125)
    dq, dk, dv = after((dq, dk, dv), hop)
    hop = r_cross.leave(1)
    d_self = [dot_tn(x, dq), dot_tn(x, dk), dot_tn(x, dv)]
    d_self = [d.astype(BF) for d in d_self]

    def column_sum(value):
        return jnp.sum(value.astype(F32), axis=0)

    zero = jnp.zeros((D,), F32)
    small_grads = jnp.stack(
        [column_sum(t) for t in (dq, dv, da, dq2, dv2, dc)]
        + [d_contract_b, zero, gain1, gain2, gain3, shift1, shift2, shift3, zero, zero]
    )
    small_blocks = split_small(
        small_grads, jnp.broadcast_to(d_expand_b, (8, FF)), rows, wide
    )
    small_blocks = small_blocks.reshape(place.dp_count, place.chips, 2, 8, D)
    r_self = reduce(
        place, [owner_blocks(place, d) for d in d_self + [d_so]] + [small_blocks]
    )
    dq, dk, dv = after((dq, dk, dv), d_self, small_blocks)
    input_grad = dr1 + dot_nt(dq, wq) + dot_nt(dk, wk) + dot_nt(dv, wv)
    own_expand = r_expand.result()
    r_self.leave(0)
    r_cross.last()
    r_self.leave(1)
    own_cross = r_cross.result()
    r_self.last()
    own_self = r_self.result()
    tail = own_self[4 * rows :]
    return (
        output.reshape(shape),
        input_grad.reshape(shape),
        encoder_grad.reshape(encoder_states.shape),
        own_self[: 3 * rows].reshape(3, rows, D),
        own_self[3 * rows : 4 * rows],
        own_cross[: 3 * rows].reshape(3, rows, D),
        own_cross[3 * rows :],
        tail[0:6, 0:rows],
        own_expand,
        tail[0, 256 : 256 + wide],
        own_contract,
        tail[6, 0:rows],
        tail[0:3, 128 : 128 + rows],
        tail[3:6, 128 : 128 + rows],
    )


def solution(mesh):
    rows = P(AXES)
    return jax.shard_map(
        body,
        mesh=mesh,
        in_specs=(
            P(AXES, None, None),
            P(AXES, None, None),
            P(AXES, None, None),
            P(AXES),
            P(AXES),
            P(None, AXES, None),
            P(AXES, None),
            P(None, AXES, None),
            P(AXES, None),
            P(None, AXES),
            P(AXES, None),
            P(AXES),
            P(AXES, None),
            P(AXES),
            P(None, AXES),
            P(None, AXES),
        ),
        out_specs=(
            P(AXES, None, None),
            P(AXES, None, None),
            P(AXES, None, None),
            P(None, AXES, None),
            P(AXES, None),
            P(None, AXES, None),
            P(AXES, None),
            P(None, AXES),
            P(AXES, None),
            P(AXES),
            P(AXES, None),
            P(AXES),
            P(None, AXES),
            P(None, AXES),
        ),
        check_vma=False,
    )
```

```python
import functools

import jax
import jax.numpy as jnp
import numpy as np
from jax import lax
from jax.experimental import pallas as pl
from jax.experimental.pallas import tpu as pltpu
from jax.sharding import PartitionSpec as P

D = 768
H = 12
HD = 64
FF = 3072
AXES = ("dp", "fsdp")

EPS = 1e-05
BIG_NEGATIVE = -1000000000.0
BF = jnp.bfloat16
F32 = jnp.float32
QUICK = pl.CostEstimate(flops=1000, bytes_accessed=1000, transcendentals=0)


class Place:
    def __init__(self):
        self.dp_count = lax.axis_size("dp")
        self.inner = lax.axis_size("fsdp")
        self.chips = self.inner // 2
        self.bits = int(np.log2(self.dp_count))
        self.dp = lax.axis_index("dp")
        inner = lax.axis_index("fsdp")
        self.chip = inner // 2
        self.core = inner % 2
        table = []
        for dp in range(self.dp_count):
            for chip in range(self.chips):
                for core in range(2):
                    table.append(
                        [dp ^ self.mask(core, m) for m in range(self.dp_count)]
                        + [dp ^ self.mask(1 - core, m) for m in range(self.dp_count)]
                        + [(chip + k) % self.chips for k in range(self.chips)]
                        + [(chip - k) % self.chips for k in range(self.chips)]
                        + [core, 1 - core]
                    )
        index = self.dp * self.inner + inner
        self.spots = lax.dynamic_index_in_dim(
            jnp.asarray(np.array(table, np.int32)), index, 0, keepdims=False
        )
        self.theirs_at = self.dp_count
        self.up_at = 2 * self.dp_count
        self.down_at = self.up_at + self.chips
        self.core_at = self.down_at + self.chips

    def bit(self, core, step):
        return 1 << (self.bits - 1 - step if core == 0 else step)

    def mask(self, core, relative):
        return sum(self.bit(core, s) for s in range(self.bits) if relative >> s & 1)

    def permute(self, value, target):
        pairs = []
        for dp in range(self.dp_count):
            for chip in range(self.chips):
                for core in range(2):
                    to = target(dp, chip, core)
                    pairs.append(
                        (
                            dp * self.inner + chip * 2 + core,
                            to[0] * self.inner + to[1] * 2 + to[2],
                        )
                    )
        return lax.ppermute(value, AXES, pairs)

    def across_cores(self, value):
        return self.permute(value, lambda d, z, c: (d, z, 1 - c))

    def across_step(self, value, step):
        return self.permute(value, lambda d, z, c: (d ^ self.bit(c, step), z, c))

    def along_chips(self, value, shift):
        return self.permute(value, lambda d, z, c: (d, (z + shift) % self.chips, c))


def after(values, *earlier):
    return lax.optimization_barrier((values, earlier))[0]


def copy_kernel(plan, n_in, spots_ref, *refs):
    ins, outs, sems = refs[:n_in], refs[n_in:-1], refs[-1]
    copies = []
    for i, (source, source_at, target, target_at) in enumerate(plan):
        copies.append(
            pltpu.make_async_copy(
                ins[source].at[source_at(spots_ref)],
                outs[target].at[target_at(spots_ref)],
                sems.at[i],
            )
        )
    for c in copies:
        c.start()
    for c in copies:
        c.wait()


def copy_call(place, plan, ins, outs, name):
    anywhere = pl.BlockSpec(memory_space=pl.ANY)
    return pl.pallas_call(
        functools.partial(copy_kernel, plan, len(ins)),
        grid_spec=pltpu.PrefetchScalarGridSpec(
            num_scalar_prefetch=1,
            grid=(1,),
            in_specs=[anywhere] * len(ins),
            out_specs=[anywhere] * len(outs),
            scratch_shapes=[pltpu.SemaphoreType.DMA((len(plan),))],
        ),
        out_shape=outs,
        compiler_params=pltpu.CompilerParams(vmem_limit_bytes=1 << 20),
        cost_estimate=QUICK,
        name=name,
    )(place.spots, *ins)


class Gather:
    def __init__(self, place, local):
        self.place = place
        self.local = local
        self.got = [local] + [
            place.along_chips(local, k) for k in range(1, place.chips)
        ]

    def column(self, *earlier):
        place = self.place
        self.got = after(self.got, *earlier)
        plan = [
            (
                k,
                lambda s: (slice(None),),
                0,
                lambda s, k=k: (s[place.down_at + k],),
            )
            for k in range(place.chips)
        ]
        shape = jax.ShapeDtypeStruct((place.chips,) + self.local.shape, BF)
        self.blocks = {0: copy_call(place, plan, self.got, [shape], "column")[0]}
        return self.blocks[0]

    def meet(self, later):
        self.blocks, later.got = lax.optimization_barrier((self.blocks, later.got))

    def hop(self, step, held, *earlier):
        self.blocks[held] = after(self.blocks[held], *earlier)
        self.blocks[held | 1 << step] = self.place.across_step(self.blocks[held], step)

    def share(self, held):
        return self.place.across_cores(self.blocks[held])

    def spread(self, parts, *earlier):
        place = self.place
        others = [self.share(m) for m in range(place.dp_count)]
        ins = [self.blocks[m] for m in range(place.dp_count)] + others
        ins = after(ins, *earlier)
        cols = self.local.shape[1]
        plan, outs = [], []
        for out, (first, rows) in enumerate(parts):
            outs.append(
                jax.ShapeDtypeStruct((place.dp_count, place.chips, 2, rows, cols), BF)
            )
            for m in range(2 * place.dp_count):
                core = place.core_at + (m >= place.dp_count)
                plan.append(
                    (
                        m,
                        lambda s, a=first, n=rows: (slice(None), pl.ds(a, n)),
                        out,
                        lambda s, m=m, core=core: (s[m], slice(None), s[core]),
                    )
                )
        whole = copy_call(place, plan, ins, outs, "spread")
        return [w.reshape(-1, cols) for w in whole]


def sum_refs(refs, n, arrived):
    parts = []
    for mine, other in zip(refs[:n], refs[n : 2 * n]):
        shape = mine.shape[-2:]
        lead = mine.shape[1:2]
        parts.append(
            (mine[...].astype(F32) + other[...].astype(F32)).reshape(lead + shape)
        )
    value = parts[0] if n == 1 else jnp.concatenate(parts, axis=1)
    for a in refs[2 * n : 2 * n + arrived]:
        value = value + a[...].astype(F32).reshape(value.shape)
    return value


def leave_kernel(n, arrived, spots_ref, *refs):
    out = refs[-1]
    out[...] = sum_refs(refs[:-1], n, arrived).astype(BF).reshape(out.shape)


def last_kernel(n, arrived, chips, spots_ref, *refs):
    each = 2 * n + arrived
    outs = refs[chips * each :]
    for k in range(chips):
        value = sum_refs(refs[k * each : (k + 1) * each], n, arrived)
        outs[k][...] = value.astype(outs[k].dtype).reshape(outs[k].shape)


def cut_kernel(parts, count, *refs):
    total = refs[0][...].astype(F32)
    for r in refs[1:count]:
        total = total + r[...].astype(F32)
    for (shape, row, col), out in zip(parts, refs[count:]):
        piece = total[row : row + int(np.prod(shape[:-1])), col : col + shape[-1]]
        out[...] = piece.reshape(shape)


def cut_sum(terms, parts):
    return pl.pallas_call(
        functools.partial(cut_kernel, parts, len(terms)),
        out_shape=[jax.ShapeDtypeStruct(s, F32) for s, _, _ in parts],
        compiler_params=pltpu.CompilerParams(vmem_limit_bytes=8 << 20),
        cost_estimate=QUICK,
        name="cut_sum",
    )(*terms)


class Reduce:
    def __init__(self, place, blocks):
        self.place = place
        self.blocks = blocks
        self.rows = sum(b.shape[3] for b in blocks)
        self.cols = blocks[0].shape[4]
        self.others = [place.across_cores(b) for b in blocks]
        self.got = []

    def leave(self, step, *earlier):
        place = self.place
        if step == 0:
            self.others = after(self.others, *earlier)
        else:
            self.got[-1] = after(self.got[-1], *earlier)
        count = 1 << (place.bits - 1 - step)
        chips, core = place.chips, place.core_at

        def spot(i, s):
            return s[(1 << step) + i * (2 << step)]

        specs = [
            pl.BlockSpec(
                (1, chips, 1) + b.shape[3:], lambda i, s: (spot(i, s), 0, s[core], 0, 0)
            )
            for b in self.blocks
        ] * 2
        for t in range(step):
            specs.append(
                pl.BlockSpec(
                    (1, chips, self.rows, self.cols),
                    lambda i, s, t=t: ((1 << (step - t - 1)) + i * (1 << (step - t)), 0, 0, 0),
                )
            )
        sent = pl.pallas_call(
            functools.partial(leave_kernel, len(self.blocks), step),
            grid_spec=pltpu.PrefetchScalarGridSpec(
                num_scalar_prefetch=1,
                grid=(count,),
                in_specs=specs,
                out_specs=pl.BlockSpec(
                    (1, chips, self.rows, self.cols), lambda i, s: (i, 0, 0, 0)
                ),
            ),
            out_shape=jax.ShapeDtypeStruct((count, chips, self.rows, self.cols), BF),
            compiler_params=pltpu.CompilerParams(vmem_limit_bytes=24 << 20),
            cost_estimate=QUICK,
            name="leave",
        )(place.spots, *self.blocks, *self.others, *self.got)
        self.got.append(place.across_step(sent, step))
        return sent

    def last(self, *earlier):
        place = self.place
        self.got[-1] = after(self.got[-1], *earlier)
        chips, core = place.chips, place.core_at
        specs, ins = [], []
        for k in range(chips):
            up = place.up_at + k
            for b in self.blocks + self.others:
                ins.append(b)
                specs.append(
                    pl.BlockSpec(
                        (1, 1, 1) + b.shape[3:],
                        lambda i, s, up=up: (s[0], s[up], s[core], 0, 0),
                    )
                )
            for g in self.got:
                ins.append(g)
                specs.append(
                    pl.BlockSpec(
                        (1, 1, self.rows, self.cols), lambda i, s, up=up: (0, s[up], 0, 0)
                    )
                )
        flat = pl.BlockSpec((self.rows, self.cols), lambda i, s: (0, 0))
        own, *sent = pl.pallas_call(
            functools.partial(last_kernel, len(self.blocks), place.bits, chips),
            grid_spec=pltpu.PrefetchScalarGridSpec(
                num_scalar_prefetch=1, grid=(1,), in_specs=specs, out_specs=[flat] * chips
            ),
            out_shape=[
                jax.ShapeDtypeStruct((self.rows, self.cols), F32 if k == 0 else BF)
                for k in range(chips)
            ],
            compiler_params=pltpu.CompilerParams(vmem_limit_bytes=24 << 20),
            cost_estimate=QUICK,
            name="last",
        )(place.spots, *ins)
        self.own = own
        self.came = [place.along_chips(v, k + 1) for k, v in enumerate(sent)]
        return own

    def result(self, parts, *earlier):
        self.came = after(self.came, *earlier)
        return cut_sum([self.own] + self.came, parts)


def owner_blocks(place, gradient):
    rows = gradient.shape[0] // (place.dp_count * place.inner)
    return gradient.reshape(
        place.dp_count, place.chips, 2, rows, gradient.shape[-1]
    )


class PlainReduce:
    def __init__(self, place, blocks):
        devices = place.dp_count * place.inner
        flat = [b.reshape((devices,) + b.shape[3:]) for b in blocks]
        self.sum = lax.psum_scatter(
            jnp.concatenate(flat, axis=1), AXES, scatter_dimension=0, tiled=False
        )

    def leave(self, step, *earlier):
        return self.sum

    def last(self, *earlier):
        return self.sum

    def result(self, parts, *earlier):
        total = self.sum.astype(F32)
        return [
            total[r : r + int(np.prod(s[:-1])), c : c + s[-1]].reshape(s)
            for s, r, c in parts
        ]


def dot_nt(a, b):
    return lax.dot_general(a, b, (((1,), (1,)), ((), ())), preferred_element_type=F32)


def dot_nn(a, b):
    return jnp.dot(a, b, preferred_element_type=F32)


def dot_tn(a, b):
    return lax.dot_general(a, b, (((0,), (0,)), ((), ())), preferred_element_type=F32)


def head(h):
    return slice(h * HD, (h + 1) * HD)


def attend_kernel(
    masked, start_ref, length_ref, q_ref, k_ref, v_ref, o_ref, p_ref, scores_ref
):
    rows = q_ref.shape[0]
    keys = k_ref.shape[0]
    if masked:
        seq = pl.program_id(0)
        start = start_ref[seq]
        stop = start + length_ref[seq]
        key_at = lax.broadcasted_iota(jnp.int32, (keys, rows), 0)
        row_at = lax.broadcasted_iota(jnp.int32, (keys, rows), 1)
        inside = (key_at >= start) & (key_at < stop) & (row_at >= start) & (row_at < stop)
        hidden = jnp.where((key_at <= row_at) | inside, 0.0, BIG_NEGATIVE).astype(F32)
    for h in range(H):
        scores_ref[h] = dot_nt(k_ref[:, head(h)], q_ref[:, head(h)])
    for h in range(H):
        scores = scores_ref[h]
        if masked:
            scores = scores + hidden
        peak = jnp.max(scores, axis=0, keepdims=True)
        weights = jnp.exp(scores - peak)
        total = jnp.sum(weights, axis=0, keepdims=True)
        p_ref[0, h] = (weights * (1.0 / total)).astype(BF)
    values_t = v_ref[...].T
    pieces = [dot_nn(values_t[head(h)], p_ref[0, h]) for h in range(H)]
    o_ref[...] = jnp.concatenate(pieces, axis=0).T.astype(BF)


def attend(queries, keys, values, start, length, masked, count):
    rows = queries.shape[0] // count
    key_rows = keys.shape[0] // count
    block = lambda n: pl.BlockSpec((n, D), lambda s, *_: (s, 0))
    return pl.pallas_call(
        functools.partial(attend_kernel, masked),
        grid_spec=pltpu.PrefetchScalarGridSpec(
            num_scalar_prefetch=2,
            grid=(count,),
            in_specs=[block(rows), block(key_rows), block(key_rows)],
            out_specs=[
                block(rows),
                pl.BlockSpec((1, H, key_rows, rows), lambda s, *_: (s, 0, 0, 0)),
            ],
            scratch_shapes=[pltpu.VMEM((H, key_rows, rows), F32)],
        ),
        out_shape=[
            jax.ShapeDtypeStruct(queries.shape, BF),
            jax.ShapeDtypeStruct((count, H, key_rows, rows), BF),
        ],
        compiler_params=pltpu.CompilerParams(vmem_limit_bytes=20 << 20),
        cost_estimate=QUICK,
        name="attend",
    )(start, length, queries, keys, values)


def attend_back_kernel(
    q_ref, k_ref, v_ref, p_ref, g_ref, dq_ref, dk_ref, dv_ref, moved_ref, ds_ref
):
    for h in range(H):
        moved_ref[h] = dot_nt(v_ref[:, head(h)], g_ref[:, head(h)])
    for h in range(H):
        weights = p_ref[0, h].astype(F32)
        moved = moved_ref[h]
        centre = jnp.sum(weights * moved, axis=0, keepdims=True)
        ds_ref[h] = (weights * (moved - centre)).astype(BF)
    keys_t = k_ref[...].T
    dq, dk, dv = [], [], []
    for h in range(H):
        dk.append(dot_nn(ds_ref[h], q_ref[:, head(h)]))
        dv.append(dot_nn(p_ref[0, h], g_ref[:, head(h)]))
        dq.append(dot_nn(keys_t[head(h)], ds_ref[h]))
    dq_ref[...] = jnp.concatenate(dq, axis=0).T.astype(BF)
    dk_ref[...] = jnp.concatenate(dk, axis=1).astype(BF)
    dv_ref[...] = jnp.concatenate(dv, axis=1).astype(BF)


def attend_back(queries, keys, values, weights, grads, count):
    rows = queries.shape[0] // count
    key_rows = keys.shape[0] // count
    block = lambda n: pl.BlockSpec((n, D), lambda s: (s, 0))
    return pl.pallas_call(
        attend_back_kernel,
        grid=(count,),
        in_specs=[
            block(rows),
            block(key_rows),
            block(key_rows),
            pl.BlockSpec((1, H, key_rows, rows), lambda s: (s, 0, 0, 0)),
            block(rows),
        ],
        out_specs=[block(rows), block(key_rows), block(key_rows)],
        out_shape=[
            jax.ShapeDtypeStruct(queries.shape, BF),
            jax.ShapeDtypeStruct(keys.shape, BF),
            jax.ShapeDtypeStruct(keys.shape, BF),
        ],
        scratch_shapes=[
            pltpu.VMEM((H, key_rows, rows), F32),
            pltpu.VMEM((H, key_rows, rows), BF),
        ],
        compiler_params=pltpu.CompilerParams(vmem_limit_bytes=24 << 20),
        cost_estimate=QUICK,
        name="attend_back",
    )(queries, keys, values, weights, grads)


def norm(summed):
    centre = summed - jnp.mean(summed, axis=-1, keepdims=True)
    scale = lax.rsqrt(jnp.mean(centre * centre, axis=-1, keepdims=True) + EPS)
    return centre * scale, scale


def norm_back(normal, scale, gain, grad):
    inner = grad * gain
    back = scale * (
        inner
        - jnp.mean(inner, axis=-1, keepdims=True)
        - normal * jnp.mean(inner * normal, axis=-1, keepdims=True)
    )
    return back, jnp.sum(grad * normal, axis=0), jnp.sum(grad, axis=0)


def column_sum(value):
    return jnp.sum(value.astype(F32), axis=0)


def gelu_and_slope(value):
    spread = 0.5 * (1.0 + lax.erf(value * np.float32(np.sqrt(0.5))))
    density = jnp.exp(-0.5 * value * value) * np.float32(1.0 / np.sqrt(2.0 * np.pi))
    return value * spread, spread + value * density


def pack_kernel(sp_ref, so_ref, ab_ref, eb_ref, cb_ref, ng_ref, ns_ref, out_ref):
    rows, n = so_ref.shape[0], ab_ref.shape[1]
    for i in range(3):
        out_ref[i * rows : (i + 1) * rows] = sp_ref[i]
    out_ref[3 * rows : 4 * rows] = so_ref[...]

    def padded(v, width):
        v = v.astype(F32)
        if v.shape[0] < 8:
            v = jnp.concatenate([v, jnp.zeros((8 - v.shape[0], v.shape[1]), F32)])
        return jnp.concatenate([v, jnp.zeros((8, width - v.shape[1]), F32)], axis=1)

    first = jnp.concatenate([ab_ref[...].astype(F32), cb_ref[...].astype(F32)])
    second = jnp.concatenate([ng_ref[...].astype(F32), ns_ref[...].astype(F32)])
    out_ref[4 * rows :] = jnp.concatenate(
        [padded(first, 128), padded(second, 128), padded(eb_ref[...], D - 256)], axis=1
    ).astype(BF)


def pack_self(sp, so, ab, eb, cb, ng, ns):
    ins = [sp, so, ab, eb.reshape(1, -1), cb.reshape(1, -1), ng, ns]
    ins = [pltpu.with_memory_space_constraint(a, pltpu.HBM) for a in ins]
    return pl.pallas_call(
        pack_kernel,
        grid=(1,),
        in_specs=[
            pl.BlockSpec(a.shape, lambda i, n=a.ndim: (0,) * n) for a in ins
        ],
        out_specs=pl.BlockSpec((4 * so.shape[0] + 8, D), lambda i: (0, 0)),
        out_shape=jax.ShapeDtypeStruct((4 * so.shape[0] + 8, D), BF),
        compiler_params=pltpu.CompilerParams(vmem_limit_bytes=4 << 20),
        cost_estimate=QUICK,
        name="pack_self",
    )(*ins)


def pack_small(ab, eb, cb, ng, ns):
    n, wide = cb.shape[0], eb.shape[0]
    return jnp.concatenate(
        [
            jnp.pad(jnp.concatenate([ab, cb[None]]), ((0, 1), (0, 128 - n))),
            jnp.pad(jnp.concatenate([ng, ns]), ((0, 2), (0, 128 - n))),
            jnp.pad(eb[None], ((0, 7), (0, D - 256 - wide))),
        ],
        axis=1,
    )


def unpack_small_kernel(n, wide, in_ref, rows_ref, eb_ref):
    for d in range(in_ref.shape[0]):
        block = in_ref[d].astype(F32)
        rows_ref[0:8, d * n : (d + 1) * n] = block[:, 0:n]
        rows_ref[8:16, d * n : (d + 1) * n] = block[:, 128 : 128 + n]
        eb_ref[:, d * wide : (d + 1) * wide] = block[0:1, 256 : 256 + wide]


def unpack_small(gathered, n, wide):
    devices = gathered.shape[0]
    return pl.pallas_call(
        functools.partial(unpack_small_kernel, n, wide),
        out_shape=[
            jax.ShapeDtypeStruct((16, devices * n), F32),
            jax.ShapeDtypeStruct((1, devices * wide), F32),
        ],
        compiler_params=pltpu.CompilerParams(vmem_limit_bytes=8 << 20),
        cost_estimate=QUICK,
        name="unpack_small",
    )(gathered)


def split_small_kernel(n, wide, *refs):
    *vectors, eb_ref, out_ref = refs
    rows = [v[...].reshape(1, D) for v in vectors]
    zero = jnp.zeros((1, D), F32)
    first = jnp.concatenate(rows[:7] + [zero], axis=0)
    second = jnp.concatenate(rows[7:] + [zero, zero], axis=0)
    tail = jnp.broadcast_to(eb_ref[...].reshape(1, FF), (8, FF))

    def padded(v, width):
        return jnp.concatenate([v, jnp.zeros((8, width - v.shape[1]), F32)], axis=1)

    for d in range(out_ref.shape[0]):
        out_ref[d] = jnp.concatenate(
            [
                padded(first[:, d * n : (d + 1) * n], 128),
                padded(second[:, d * n : (d + 1) * n], 128),
                padded(tail[:, d * wide : (d + 1) * wide], D - 256),
            ],
            axis=1,
        ).astype(BF)


def split_small(vectors, eb, n, wide):
    devices = D // n
    return pl.pallas_call(
        functools.partial(split_small_kernel, n, wide),
        out_shape=jax.ShapeDtypeStruct((devices, 8, D), BF),
        compiler_params=pltpu.CompilerParams(vmem_limit_bytes=8 << 20),
        cost_estimate=QUICK,
        name="split_small",
    )(*vectors, eb)


def body(
    layer_input,
    encoder_states,
    output_grad,
    span_start,
    span_length,
    self_project,
    self_output,
    cross_project,
    cross_output,
    attend_bias,
    expand_weight,
    expand_bias,
    contract_weight,
    contract_bias,
    norm_gain,
    norm_shift,
):
    place = Place()
    count, length = layer_input.shape[:2]
    shape = layer_input.shape
    rows = self_output.shape[0]
    wide = expand_bias.shape[0]
    fits = rows % 8 == 0
    reduce = Reduce if fits else PlainReduce
    x = layer_input.reshape(-1, D)
    memory = encoder_states.reshape(-1, D)
    grad_out = output_grad.reshape(-1, D).astype(F32)

    local_cross = jnp.concatenate([cross_project.reshape(-1, D), cross_output])
    four = [(i * rows, rows) for i in range(4)]
    if fits:
        g_self = Gather(
            place,
            pack_self(
                self_project,
                self_output,
                attend_bias,
                expand_bias,
                contract_bias,
                norm_gain,
                norm_shift,
            ),
        )
        line = g_self.column()
        g_self.hop(0, 0)
        g_self.hop(1, 0)
        g_cross = Gather(place, after(local_cross, line))
        g_self.meet(g_cross)
        g_self.hop(1, 1)
        line = g_cross.column()
        g_cross.hop(0, 0)
        g_cross.hop(1, 0)
        g_expand = Gather(place, after(expand_weight, line))
        *w_self, smalls = g_self.spread(four + [(4 * rows, 8)], line)
        smalls = smalls.reshape(-1, 8, D)
    else:
        whole = lax.all_gather(
            jnp.concatenate(
                [
                    self_project.reshape(-1, D),
                    self_output,
                    pack_small(
                        attend_bias, expand_bias, contract_bias, norm_gain, norm_shift
                    ),
                    local_cross,
                    contract_weight,
                ]
            ),
            AXES,
            axis=0,
        )
        squares = [
            whole[:, a : a + rows].reshape(D, D)
            for a in [i * rows for i in range(4)]
            + [4 * rows + 8 + i * rows for i in range(4)]
        ]
        w_self, w_cross = squares[:4], squares[4:]
        contract = whole[:, 8 * rows + 8 :].reshape(FF, D)
        smalls = whole[:, 4 * rows : 4 * rows + 8]
        expand = lax.all_gather(expand_weight, AXES, axis=0, tiled=True)
    wq, wk, wv, wo = w_self
    small_rows, expand_b = unpack_small(smalls, rows, wide)
    biases = [small_rows[i : i + 1] for i in range(6)]
    contract_b = small_rows[6:7]
    gains = [small_rows[8 + i : 9 + i] for i in range(3)]
    shifts = [small_rows[11 + i : 12 + i] for i in range(3)]

    q = ((dot_nn(x, wq) + biases[0]) * 0.125).astype(BF)
    k = dot_nn(x, wk).astype(BF)
    v = (dot_nn(x, wv) + biases[1]).astype(BF)
    o, p = attend(q, k, v, span_start, span_length, True, count)
    if fits:
        g_cross.hop(1, 1, o)
        line = g_expand.column(o)
        g_expand.hop(0, 0)
        g_expand.hop(1, 0)
        g_contract = Gather(place, after(contract_weight, line))
        o = after(o, line)
    n1, s1 = norm(x.astype(F32) + (dot_nn(o, wo) + biases[2]))
    x1 = n1 * gains[0] + shifts[0]
    x1b = x1.astype(BF)
    if fits:
        w_cross = g_cross.spread(four, x1b)
    cq, ck, cv, co = w_cross
    q2 = ((dot_nn(x1b, cq) + biases[3]) * 0.125).astype(BF)
    k2 = dot_nn(memory, ck).astype(BF)
    v2 = (dot_nn(memory, cv) + biases[4]).astype(BF)
    o2, p2 = attend(q2, k2, v2, span_start, span_length, False, count)
    if fits:
        g_expand.hop(1, 1, o2)
        line = g_contract.column(o2)
        g_contract.hop(0, 0)
        g_contract.hop(1, 0)
        o2 = after(o2, line)
    n2, s2 = norm(x1 + (dot_nn(o2, co) + biases[5]))
    x2 = n2 * gains[1] + shifts[1]
    x2b = x2.astype(BF)
    if fits:
        (expand,) = g_expand.spread([(0, rows)], x2b)
    act, slope = gelu_and_slope(dot_nn(x2b, expand) + expand_b)
    act = act.astype(BF)
    slope = slope.astype(BF)
    if fits:
        g_contract.hop(1, 1, act)
        (contract,) = g_contract.spread([(0, 4 * rows)], act)
    n3, s3 = norm(x2 + (dot_nn(act, contract) + contract_b))
    output = (n3 * gains[2] + shifts[2]).astype(BF)

    dr3, gain3, shift3 = norm_back(n3, s3, gains[2], grad_out)
    df = dr3.astype(BF)
    d_contract = dot_tn(act, df).astype(BF)
    r_contract = reduce(place, [owner_blocks(place, d_contract)])
    d_contract_b = column_sum(df)
    df2 = after(df, d_contract)
    du = (dot_nt(df2, contract) * slope.astype(F32)).astype(BF)
    d_expand_b = column_sum(du)

    hop = r_contract.leave(0, du)
    d_expand = dot_tn(x2b, after(du, hop)).astype(BF)
    r_expand = reduce(place, [owner_blocks(place, d_expand)])
    dr2, gain2, shift2 = norm_back(
        n2, s2, gains[1], dr3 + dot_nt(after(du, d_expand), expand)
    )
    dc = dr2.astype(BF)
    hop = r_contract.leave(1, dc)
    hop2 = r_expand.leave(0, dc)
    dc2 = after(dc, hop, hop2)
    d_co = dot_tn(o2, dc2).astype(BF)
    do2 = dot_nt(dc2, co).astype(BF)
    dq2, dk2, dv2 = attend_back(q2, k2, v2, p2, after(do2, d_co), count)
    dq2 = dq2 * BF(0.125)

    sent = r_contract.last(dq2)
    hop2 = r_expand.leave(1, dq2)
    dq2, dk2, dv2 = after((dq2, dk2, dv2), sent, hop2)
    d_cross = [dot_tn(x1b, dq2), dot_tn(memory, dk2), dot_tn(memory, dv2)]
    d_cross = [d.astype(BF) for d in d_cross]
    r_cross = reduce(place, [owner_blocks(place, d) for d in d_cross + [d_co]])
    dq2, dk2, dv2 = after((dq2, dk2, dv2), d_cross)

    dr1, gain1, shift1 = norm_back(n1, s1, gains[0], dr2 + dot_nt(dq2, cq))
    da = dr1.astype(BF)
    hop = r_cross.leave(0, da)
    (own_contract,) = r_contract.result([((4 * rows, D), 0, 0)], da)
    sent = r_expand.last(da)
    da2 = after(da, hop, own_contract, sent)
    d_so = dot_tn(o, da2).astype(BF)
    do = dot_nt(da2, wo).astype(BF)
    dq, dk, dv = attend_back(q, k, v, p, after(do, d_so), count)
    dq = dq * BF(0.125)

    hop = r_cross.leave(1, dq)
    dq, dk, dv = after((dq, dk, dv), hop)
    d_self = [dot_tn(x, dq), dot_tn(x, dk), dot_tn(x, dv)]
    d_self = [d.astype(BF) for d in d_self]
    small_blocks = split_small(
        [column_sum(t) for t in (dq, dv, da, dq2, dv2, dc)]
        + [d_contract_b, gain1, gain2, gain3, shift1, shift2, shift3],
        d_expand_b,
        rows,
        wide,
    )
    small_blocks = small_blocks.reshape(place.dp_count, place.chips, 2, 8, D)
    r_self = reduce(
        place, [owner_blocks(place, d) for d in d_self + [d_so]] + [small_blocks]
    )
    (own_expand,) = r_expand.result([((rows, FF), 0, 0)], d_self, small_blocks)
    dk2, dv2 = after((dk2, dv2), own_expand)
    encoder_grad = dot_nt(dk2, ck) + dot_nt(dv2, cv)
    sent = r_cross.last(encoder_grad)
    hop = r_self.leave(0, sent)
    dq, dk, dv = after((dq, dk, dv), hop)
    input_grad = dr1 + dot_nt(dq, wq) + dot_nt(dk, wk) + dot_nt(dv, wv)
    projects = [((3, rows, D), 0, 0), ((rows, D), 3 * rows, 0)]
    own_cross = r_cross.result(projects, input_grad)
    r_self.leave(1, own_cross)
    r_self.last()
    at = 4 * rows
    own_self = r_self.result(
        projects
        + [
            ((6, rows), at, 0),
            ((1, wide), at, 256),
            ((1, rows), at + 6, 0),
            ((3, rows), at, 128),
            ((3, rows), at + 3, 128),
        ]
    )
    return (
        output.reshape(shape),
        input_grad.reshape(shape),
        encoder_grad.reshape(encoder_states.shape),
        own_self[0],
        own_self[1],
        own_cross[0],
        own_cross[1],
        own_self[2],
        own_expand,
        own_self[3].reshape(-1),
        own_contract,
        own_self[4].reshape(-1),
        own_self[5],
        own_self[6],
    )


def solution(mesh):
    rows = P(AXES)
    return jax.shard_map(
        body,
        mesh=mesh,
        in_specs=(
            P(AXES, None, None),
            P(AXES, None, None),
            P(AXES, None, None),
            P(AXES),
            P(AXES),
            P(None, AXES, None),
            P(AXES, None),
            P(None, AXES, None),
            P(AXES, None),
            P(None, AXES),
            P(AXES, None),
            P(AXES),
            P(AXES, None),
            P(AXES),
            P(None, AXES),
            P(None, AXES),
        ),
        out_specs=(
            P(AXES, None, None),
            P(AXES, None, None),
            P(AXES, None, None),
            P(None, AXES, None),
            P(AXES, None),
            P(None, AXES, None),
            P(AXES, None),
            P(None, AXES),
            P(AXES, None),
            P(AXES),
            P(AXES, None),
            P(AXES),
            P(None, AXES),
            P(None, AXES),
        ),
        check_vma=False,
    )
```

```python
import functools

import jax
import jax.numpy as jnp
import numpy as np
from jax import lax
from jax.experimental import pallas as pl
from jax.experimental.pallas import tpu as pltpu
from jax.sharding import PartitionSpec as P

D = 768
H = 12
HD = 64
FF = 3072
AXES = ("dp", "fsdp")

EPS = 1e-05
BIG_NEGATIVE = -1000000000.0
BF = jnp.bfloat16
F32 = jnp.float32
QUICK = pl.CostEstimate(flops=1000, bytes_accessed=1000, transcendentals=0)
LONG = pl.CostEstimate(flops=10**11, bytes_accessed=10**6, transcendentals=0)


class Place:
    def __init__(self):
        self.dp_count = lax.axis_size("dp")
        self.inner = lax.axis_size("fsdp")
        self.chips = self.inner // 2
        self.bits = int(np.log2(self.dp_count))
        self.dp = lax.axis_index("dp")
        inner = lax.axis_index("fsdp")
        self.chip = inner // 2
        self.core = inner % 2
        table = []
        for dp in range(self.dp_count):
            for chip in range(self.chips):
                for core in range(2):
                    table.append(
                        [dp ^ self.mask(core, m) for m in range(self.dp_count)]
                        + [dp ^ self.mask(1 - core, m) for m in range(self.dp_count)]
                        + [(chip + k) % self.chips for k in range(self.chips)]
                        + [(chip - k) % self.chips for k in range(self.chips)]
                        + [core, 1 - core]
                    )
        index = self.dp * self.inner + inner
        self.spots = lax.dynamic_index_in_dim(
            jnp.asarray(np.array(table, np.int32)), index, 0, keepdims=False
        )
        self.theirs_at = self.dp_count
        self.up_at = 2 * self.dp_count
        self.down_at = self.up_at + self.chips
        self.core_at = self.down_at + self.chips

    def bit(self, core, step):
        return 1 << (self.bits - 1 - step if core == 0 else step)

    def mask(self, core, relative):
        return sum(self.bit(core, s) for s in range(self.bits) if relative >> s & 1)

    def permute(self, value, target):
        pairs = []
        for dp in range(self.dp_count):
            for chip in range(self.chips):
                for core in range(2):
                    to = target(dp, chip, core)
                    pairs.append(
                        (
                            dp * self.inner + chip * 2 + core,
                            to[0] * self.inner + to[1] * 2 + to[2],
                        )
                    )
        return lax.ppermute(value, AXES, pairs)

    def across_cores(self, value):
        return self.permute(value, lambda d, z, c: (d, z, 1 - c))

    def across_step(self, value, step):
        return self.permute(value, lambda d, z, c: (d ^ self.bit(c, step), z, c))

    def along_chips(self, value, shift):
        return self.permute(value, lambda d, z, c: (d, (z + shift) % self.chips, c))


def after(values, *earlier):
    return lax.optimization_barrier((values, earlier))[0]


def copy_kernel(plan, n_in, spots_ref, *refs):
    ins, outs, sems = refs[:n_in], refs[n_in:-1], refs[-1]
    copies = []
    for i, (source, source_at, target, target_at) in enumerate(plan):
        copies.append(
            pltpu.make_async_copy(
                ins[source].at[source_at(spots_ref)],
                outs[target].at[target_at(spots_ref)],
                sems.at[i],
            )
        )
    for c in copies:
        c.start()
    for c in copies:
        c.wait()


def copy_call(place, plan, ins, outs, name):
    anywhere = pl.BlockSpec(memory_space=pl.ANY)
    return pl.pallas_call(
        functools.partial(copy_kernel, plan, len(ins)),
        grid_spec=pltpu.PrefetchScalarGridSpec(
            num_scalar_prefetch=1,
            grid=(1,),
            in_specs=[anywhere] * len(ins),
            out_specs=[anywhere] * len(outs),
            scratch_shapes=[pltpu.SemaphoreType.DMA((len(plan),))],
        ),
        out_shape=outs,
        compiler_params=pltpu.CompilerParams(vmem_limit_bytes=1 << 20),
        cost_estimate=QUICK,
        name=name,
    )(place.spots, *ins)


class Gather:
    def __init__(self, place, local):
        self.place = place
        self.local = local
        self.got = [local] + [
            place.along_chips(local, k) for k in range(1, place.chips)
        ]

    def column(self, *earlier):
        place = self.place
        self.got = after(self.got, *earlier)
        plan = [
            (
                k,
                lambda s: (slice(None),),
                0,
                lambda s, k=k: (s[place.down_at + k],),
            )
            for k in range(place.chips)
        ]
        shape = jax.ShapeDtypeStruct((place.chips,) + self.local.shape, BF)
        self.blocks = {0: copy_call(place, plan, self.got, [shape], "column")[0]}
        return self.blocks[0]

    def meet(self, later):
        self.blocks, later.got = lax.optimization_barrier((self.blocks, later.got))

    def hop(self, step, held, *earlier):
        self.blocks[held] = after(self.blocks[held], *earlier)
        self.blocks[held | 1 << step] = self.place.across_step(self.blocks[held], step)

    def share(self, held):
        return self.place.across_cores(self.blocks[held])

    def half(self, *earlier):
        place = self.place
        ins = after([self.blocks[m] for m in range(place.dp_count)], *earlier)
        plan = [
            (m, lambda s: (slice(None),), 0, lambda s, m=m: (s[m],))
            for m in range(place.dp_count)
        ]
        shape = jax.ShapeDtypeStruct((place.dp_count,) + ins[0].shape, BF)
        self.own_half = copy_call(place, plan, ins, [shape], "half")[0]
        self.other_half = place.across_cores(self.own_half)
        return self.own_half

    def spread(self, parts, *earlier):
        place = self.place
        cols = self.local.shape[1]
        whole = slice(None)
        if hasattr(self, "other_half"):
            ins = [self.own_half, self.other_half]
            places = [lambda s: (whole,), lambda s: (whole,)]
        else:
            ins = [self.blocks[m] for m in range(place.dp_count)]
            ins += [self.share(m) for m in range(place.dp_count)]
            places = [lambda s, m=m: (s[m],) for m in range(2 * place.dp_count)]
        ins = after(ins, *earlier)
        plan, outs = [], []
        for out, (first, rows) in enumerate(parts):
            outs.append(
                jax.ShapeDtypeStruct((place.dp_count, place.chips, 2, rows, cols), BF)
            )
            for m, where in enumerate(places):
                core = place.core_at + (m >= len(places) // 2)
                lead = (whole,) * (ins[m].ndim - 2)
                plan.append(
                    (
                        m,
                        lambda s, a=first, n=rows, lead=lead: lead + (pl.ds(a, n),),
                        out,
                        lambda s, where=where, core=core: where(s) + (whole, s[core]),
                    )
                )
        full = copy_call(place, plan, ins, outs, "spread")
        return [w.reshape(-1, cols) for w in full]


def side_by_side(refs):
    parts = [r[...].reshape(r.shape[1:2] + r.shape[-2:]) for r in refs]
    return parts[0] if len(parts) == 1 else jnp.concatenate(parts, axis=1)


def exchange_kernel(spots_ref, *refs):
    out = refs[-1]
    out[...] = side_by_side(refs[:-1]).reshape(out.shape)


def sum_refs(refs, n):
    value = side_by_side(refs[:n]).astype(F32)
    for a in refs[n:]:
        value = value + a[...].astype(F32).reshape(value.shape)
    return value


def leave_kernel(n, spots_ref, *refs):
    out = refs[-1]
    out[...] = sum_refs(refs[:-1], n).astype(BF).reshape(out.shape)


def last_kernel(n, each, chips, spots_ref, *refs):
    outs = refs[chips * each :]
    for k in range(chips):
        value = sum_refs(refs[k * each : (k + 1) * each], n)
        outs[k][...] = value.astype(outs[k].dtype).reshape(outs[k].shape)


def cut_kernel(parts, count, *refs):
    total = refs[0][...].astype(F32)
    for r in refs[1:count]:
        total = total + r[...].astype(F32)
    for (shape, row, col), out in zip(parts, refs[count:]):
        piece = total[row : row + int(np.prod(shape[:-1])), col : col + shape[-1]]
        out[...] = piece.reshape(shape)


def cut_sum(terms, parts):
    return pl.pallas_call(
        functools.partial(cut_kernel, parts, len(terms)),
        out_shape=[jax.ShapeDtypeStruct(s, F32) for s, _, _ in parts],
        compiler_params=pltpu.CompilerParams(vmem_limit_bytes=8 << 20),
        cost_estimate=QUICK,
        name="cut_sum",
    )(*terms)


class Reduce:
    def __init__(self, place, blocks):
        self.place = place
        self.blocks = blocks
        self.rows = sum(b.shape[3] for b in blocks)
        self.cols = blocks[0].shape[4]
        shape = (place.dp_count, place.chips, self.rows, self.cols)
        sent = self.call(
            exchange_kernel,
            (place.dp_count,),
            [
                pl.BlockSpec(
                    (1, place.chips, 1) + b.shape[3:],
                    lambda i, s: (i, 0, s[place.core_at + 1], 0, 0),
                )
                for b in blocks
            ],
            pl.BlockSpec((1,) + shape[1:], lambda i, s: (i, 0, 0, 0)),
            jax.ShapeDtypeStruct(shape, BF),
            "exchange",
        )(place.spots, *blocks)
        self.other = place.across_cores(sent)
        self.got = []

    def call(self, kernel, grid, in_specs, out_specs, out_shape, name):
        return pl.pallas_call(
            kernel,
            grid_spec=pltpu.PrefetchScalarGridSpec(
                num_scalar_prefetch=1, grid=grid, in_specs=in_specs, out_specs=out_specs
            ),
            out_shape=out_shape,
            compiler_params=pltpu.CompilerParams(vmem_limit_bytes=24 << 20),
            cost_estimate=QUICK,
            name=name,
        )

    def leave(self, step, *earlier):
        place = self.place
        if step == 0:
            self.other = after(self.other, *earlier)
        else:
            self.got[-1] = after(self.got[-1], *earlier)
        count = 1 << (place.bits - 1 - step)
        chips, core = place.chips, place.core_at

        def spot(i, s):
            return s[(1 << step) + i * (2 << step)]

        shape = (count, chips, self.rows, self.cols)
        specs = [
            pl.BlockSpec(
                (1, chips, 1) + b.shape[3:], lambda i, s: (spot(i, s), 0, s[core], 0, 0)
            )
            for b in self.blocks
        ]
        specs.append(pl.BlockSpec((1,) + shape[1:], lambda i, s: (spot(i, s), 0, 0, 0)))
        for t in range(step):
            specs.append(
                pl.BlockSpec(
                    (1,) + shape[1:],
                    lambda i, s, t=t: ((1 << (step - t - 1)) + i * (1 << (step - t)), 0, 0, 0),
                )
            )
        sent = self.call(
            functools.partial(leave_kernel, len(self.blocks)),
            (count,),
            specs,
            pl.BlockSpec((1,) + shape[1:], lambda i, s: (i, 0, 0, 0)),
            jax.ShapeDtypeStruct(shape, BF),
            "leave",
        )(place.spots, *self.blocks, self.other, *self.got)
        self.got.append(place.across_step(sent, step))
        return sent

    def last(self, *earlier):
        place = self.place
        self.got[-1] = after(self.got[-1], *earlier)
        chips, core = place.chips, place.core_at
        specs, ins = [], []
        for k in range(chips):
            up = place.up_at + k
            for b in self.blocks:
                ins.append(b)
                specs.append(
                    pl.BlockSpec(
                        (1, 1, 1) + b.shape[3:],
                        lambda i, s, up=up: (s[0], s[up], s[core], 0, 0),
                    )
                )
            for n, g in enumerate([self.other] + self.got):
                ins.append(g)
                specs.append(
                    pl.BlockSpec(
                        (1, 1, self.rows, self.cols),
                        lambda i, s, up=up, n=n: (s[0] if n == 0 else 0, s[up], 0, 0),
                    )
                )
        own, *sent = self.call(
            functools.partial(last_kernel, len(self.blocks), len(ins) // chips, chips),
            (1,),
            specs,
            [pl.BlockSpec((self.rows, self.cols), lambda i, s: (0, 0))] * chips,
            [
                jax.ShapeDtypeStruct((self.rows, self.cols), F32 if k == 0 else BF)
                for k in range(chips)
            ],
            "last",
        )(place.spots, *ins)
        self.own = own
        self.came = [place.along_chips(v, k + 1) for k, v in enumerate(sent)]
        return own

    def result(self, parts, *earlier):
        self.came = after(self.came, *earlier)
        return cut_sum([self.own] + self.came, parts)


def owner_blocks(place, gradient):
    rows = gradient.shape[0] // (place.dp_count * place.inner)
    return gradient.reshape(
        place.dp_count, place.chips, 2, rows, gradient.shape[-1]
    )


class PlainReduce:
    def __init__(self, place, blocks):
        devices = place.dp_count * place.inner
        flat = [b.reshape((devices,) + b.shape[3:]) for b in blocks]
        self.sum = lax.psum_scatter(
            jnp.concatenate(flat, axis=1), AXES, scatter_dimension=0, tiled=False
        )

    def leave(self, step, *earlier):
        return self.sum

    def last(self, *earlier):
        return self.sum

    def result(self, parts, *earlier):
        total = self.sum.astype(F32)
        return [
            total[r : r + int(np.prod(s[:-1])), c : c + s[-1]].reshape(s)
            for s, r, c in parts
        ]


def dot_nt(a, b):
    return lax.dot_general(a, b, (((1,), (1,)), ((), ())), preferred_element_type=F32)


def dot_nn(a, b):
    return jnp.dot(a, b, preferred_element_type=F32)


def dot_tn(a, b):
    return lax.dot_general(a, b, (((0,), (0,)), ((), ())), preferred_element_type=F32)


def head(h):
    return slice(h * HD, (h + 1) * HD)


def attend_kernel(
    masked, start_ref, length_ref, q_ref, k_ref, v_ref, o_ref, p_ref, scores_ref
):
    rows = q_ref.shape[0]
    keys = k_ref.shape[0]
    if masked:
        seq = pl.program_id(0)
        start = start_ref[seq]
        stop = start + length_ref[seq]
        key_at = lax.broadcasted_iota(jnp.int32, (keys, rows), 0)
        row_at = lax.broadcasted_iota(jnp.int32, (keys, rows), 1)
        inside = (key_at >= start) & (key_at < stop) & (row_at >= start) & (row_at < stop)
        hidden = jnp.where((key_at <= row_at) | inside, 0.0, BIG_NEGATIVE).astype(F32)
    for h in range(H):
        scores_ref[h] = dot_nt(k_ref[:, head(h)], q_ref[:, head(h)])
    for h in range(H):
        scores = scores_ref[h]
        if masked:
            scores = scores + hidden
        peak = jnp.max(scores, axis=0, keepdims=True)
        weights = jnp.exp(scores - peak)
        total = jnp.sum(weights, axis=0, keepdims=True)
        p_ref[0, h] = (weights * (1.0 / total)).astype(BF)
    values_t = v_ref[...].T
    pieces = [dot_nn(values_t[head(h)], p_ref[0, h]) for h in range(H)]
    o_ref[...] = jnp.concatenate(pieces, axis=0).T.astype(BF)


def attend(queries, keys, values, start, length, masked, count):
    rows = queries.shape[0] // count
    key_rows = keys.shape[0] // count
    block = lambda n: pl.BlockSpec((n, D), lambda s, *_: (s, 0))
    return pl.pallas_call(
        functools.partial(attend_kernel, masked),
        grid_spec=pltpu.PrefetchScalarGridSpec(
            num_scalar_prefetch=2,
            grid=(count,),
            in_specs=[block(rows), block(key_rows), block(key_rows)],
            out_specs=[
                block(rows),
                pl.BlockSpec((1, H, key_rows, rows), lambda s, *_: (s, 0, 0, 0)),
            ],
            scratch_shapes=[pltpu.VMEM((H, key_rows, rows), F32)],
        ),
        out_shape=[
            jax.ShapeDtypeStruct(queries.shape, BF),
            jax.ShapeDtypeStruct((count, H, key_rows, rows), BF),
        ],
        compiler_params=pltpu.CompilerParams(vmem_limit_bytes=14 << 20),
        cost_estimate=QUICK,
        name="attend",
    )(start, length, queries, keys, values)


def norm_parts(summed):
    centre = summed - jnp.mean(summed, axis=-1, keepdims=True)
    scale = lax.rsqrt(jnp.mean(centre * centre, axis=-1, keepdims=True) + EPS)
    return centre * scale, scale


def row_sum(value):
    return jnp.sum(value.astype(F32), axis=0, keepdims=True)


def norm_back_sums(summed, gain, grad):
    normal, scale = norm_parts(summed)
    inner = grad * gain
    back = scale * (
        inner
        - jnp.mean(inner, axis=-1, keepdims=True)
        - normal * jnp.mean(inner * normal, axis=-1, keepdims=True)
    )
    return back, [row_sum(grad * normal), row_sum(grad)]


def put_rows(ref, rows):
    for i, r in enumerate(rows):
        ref[i : i + 1] = r


def hidden_back_kernel(df_ref, c_ref, slope_ref, du_ref, sum_ref):
    du = (dot_nt(df_ref[...], c_ref[...]) * slope_ref[...].astype(F32)).astype(BF)
    du_ref[...] = du
    sum_ref[...] = row_sum(du)


def hidden_back(df, contract, slope):
    tokens = df.shape[0]
    return pl.pallas_call(
        hidden_back_kernel,
        grid=(FF // D,),
        in_specs=[
            pl.BlockSpec((tokens, D), lambda j: (0, 0)),
            pl.BlockSpec((D, D), lambda j: (j, 0)),
            pl.BlockSpec((tokens, D), lambda j: (0, j)),
        ],
        out_specs=[
            pl.BlockSpec((tokens, D), lambda j: (0, j)),
            pl.BlockSpec((1, D), lambda j: (0, j)),
        ],
        out_shape=[
            jax.ShapeDtypeStruct((tokens, FF), BF),
            jax.ShapeDtypeStruct((1, FF), F32),
        ],
        compiler_params=pltpu.CompilerParams(vmem_limit_bytes=16 << 20),
        cost_estimate=LONG,
        name="hidden_back",
    )(df, contract, slope)


def expand_back_kernel(
    x_ref, du_ref, e_ref, dr3_ref, r2_ref, gain_ref, de_ref, dr2_ref, dc_ref, sum_ref, xt_ref
):
    j = pl.program_id(0)

    @pl.when(j == 0)
    def _():
        xt_ref[...] = x_ref[...].T
        dr2_ref[...] = dr3_ref[...]

    du = du_ref[...]
    de_ref[...] = dot_nn(xt_ref[...], du).astype(BF)
    dr2_ref[...] += dot_nt(du, e_ref[...])

    @pl.when(j == pl.num_programs(0) - 1)
    def _():
        back, sums = norm_back_sums(r2_ref[...], gain_ref[...], dr2_ref[...])
        dc = back.astype(BF)
        dr2_ref[...] = back
        dc_ref[...] = dc
        put_rows(sum_ref, sums + [row_sum(dc)])


def expand_back(x2b, du, expand, dr3, r2, gain):
    tokens = x2b.shape[0]
    still = pl.BlockSpec((tokens, D), lambda j: (0, 0))
    moving = lambda n: pl.BlockSpec((n, D), lambda j: (0, j))
    return pl.pallas_call(
        expand_back_kernel,
        grid=(FF // D,),
        in_specs=[
            still,
            moving(tokens),
            moving(D),
            still,
            still,
            pl.BlockSpec((1, D), lambda j: (0, 0)),
        ],
        out_specs=[moving(D), still, still, pl.BlockSpec((8, D), lambda j: (0, 0))],
        out_shape=[
            jax.ShapeDtypeStruct((D, FF), BF),
            jax.ShapeDtypeStruct((tokens, D), F32),
            jax.ShapeDtypeStruct((tokens, D), BF),
            jax.ShapeDtypeStruct((8, D), F32),
        ],
        scratch_shapes=[pltpu.VMEM((D, tokens), BF)],
        compiler_params=pltpu.CompilerParams(vmem_limit_bytes=24 << 20),
        cost_estimate=LONG,
        name="expand_back",
    )(x2b, du, expand, dr3, r2, gain)


def heads_back(count, q_ref, k_ref, v_ref, p_ref, g_ref, outs, moved_ref, ds_ref):
    rows = q_ref.shape[0] // count
    keys = k_ref.shape[0] // count
    for s in range(count):
        at = slice(s * rows, (s + 1) * rows)
        key_at = slice(s * keys, (s + 1) * keys)
        for h in range(H):
            moved_ref[h] = dot_nt(v_ref[key_at, head(h)], g_ref[at, head(h)])
        for h in range(H):
            weights = p_ref[s, h].astype(F32)
            moved = moved_ref[h]
            centre = jnp.sum(weights * moved, axis=0, keepdims=True)
            ds_ref[h] = (weights * (moved - centre)).astype(BF)
        keys_t = k_ref[key_at].T
        dq, dk, dv = [], [], []
        for h in range(H):
            dk.append(dot_nn(ds_ref[h], q_ref[at, head(h)]))
            dv.append(dot_nn(p_ref[s, h], g_ref[at, head(h)]))
            dq.append(dot_nn(keys_t[head(h)], ds_ref[h]))
        outs[0][at] = (jnp.concatenate(dq, axis=0).T.astype(BF) * 0.125).astype(BF)
        outs[1][key_at] = jnp.concatenate(dk, axis=1).astype(BF)
        outs[2][key_at] = jnp.concatenate(dv, axis=1).astype(BF)


def cross_back_kernel(
    count,
    dc_ref,
    co_ref,
    cq_ref,
    q_ref,
    k_ref,
    v_ref,
    p_ref,
    o_ref,
    x_ref,
    m_ref,
    dr2_ref,
    r1_ref,
    gain_ref,
    os_ref,
    dwq_ref,
    dwk_ref,
    dwv_ref,
    dwo_ref,
    dso_ref,
    dk_ref,
    dv_ref,
    dr1_ref,
    da_ref,
    sum_ref,
    g_ref,
    dq_ref,
    moved_ref,
    ds_ref,
):
    dc = dc_ref[...]
    g_ref[...] = dot_nt(dc, co_ref[...]).astype(BF)
    dwo_ref[...] = dot_tn(o_ref[...], dc).astype(BF)
    heads_back(
        count, q_ref, k_ref, v_ref, p_ref, g_ref, (dq_ref, dk_ref, dv_ref), moved_ref, ds_ref
    )
    dq = dq_ref[...]
    dr1 = dr2_ref[...] + dot_nt(dq, cq_ref[...])
    dwq_ref[...] = dot_tn(x_ref[...], dq).astype(BF)
    mt = m_ref[...].T
    dwk_ref[...] = dot_nn(mt, dk_ref[...]).astype(BF)
    dwv_ref[...] = dot_nn(mt, dv_ref[...]).astype(BF)
    back, sums = norm_back_sums(r1_ref[...], gain_ref[...], dr1)
    da = back.astype(BF)
    dr1_ref[...] = back
    da_ref[...] = da
    dso_ref[...] = dot_tn(os_ref[...], da).astype(BF)
    put_rows(sum_ref, sums + [row_sum(da), row_sum(dq), row_sum(dv_ref[...])])


def cross_back(dc, co, cq, q2, k2, v2, p2, o2, x1b, memory, dr2, r1, gain, o, count):
    tokens, rows = dc.shape[0], dc.shape[0] // count
    keys = memory.shape[0] // count
    square = jax.ShapeDtypeStruct((D, D), BF)
    low = jax.ShapeDtypeStruct((tokens, D), BF)
    return pl.pallas_call(
        functools.partial(cross_back_kernel, count),
        out_shape=[square] * 5
        + [
            jax.ShapeDtypeStruct(memory.shape, BF),
            jax.ShapeDtypeStruct(memory.shape, BF),
            jax.ShapeDtypeStruct((tokens, D), F32),
            low,
            jax.ShapeDtypeStruct((8, D), F32),
        ],
        scratch_shapes=[
            pltpu.VMEM((tokens, D), BF),
            pltpu.VMEM((tokens, D), BF),
            pltpu.VMEM((H, keys, rows), F32),
            pltpu.VMEM((H, keys, rows), BF),
        ],
        compiler_params=pltpu.CompilerParams(vmem_limit_bytes=18 << 20),
        cost_estimate=LONG,
        name="cross_back",
    )(dc, co, cq, q2, k2, v2, p2, o2, x1b, memory, dr2, r1, gain, o)


def self_back_kernel(
    count,
    da_ref,
    wo_ref,
    q_ref,
    k_ref,
    v_ref,
    p_ref,
    x_ref,
    dwq_ref,
    dwk_ref,
    dwv_ref,
    dq_ref,
    dk_ref,
    dv_ref,
    sum_ref,
    g_ref,
    moved_ref,
    ds_ref,
):
    g_ref[...] = dot_nt(da_ref[...], wo_ref[...]).astype(BF)
    heads_back(
        count, q_ref, k_ref, v_ref, p_ref, g_ref, (dq_ref, dk_ref, dv_ref), moved_ref, ds_ref
    )
    xt = x_ref[...].T
    dwq_ref[...] = dot_nn(xt, dq_ref[...]).astype(BF)
    dwk_ref[...] = dot_nn(xt, dk_ref[...]).astype(BF)
    dwv_ref[...] = dot_nn(xt, dv_ref[...]).astype(BF)
    put_rows(sum_ref, [row_sum(dq_ref[...]), row_sum(dv_ref[...])])


def self_back(da, wo, q, k, v, p, x, count):
    tokens, rows = da.shape[0], da.shape[0] // count
    square = jax.ShapeDtypeStruct((D, D), BF)
    low = jax.ShapeDtypeStruct((tokens, D), BF)
    return pl.pallas_call(
        functools.partial(self_back_kernel, count),
        out_shape=[square] * 3 + [low] * 3 + [jax.ShapeDtypeStruct((8, D), F32)],
        scratch_shapes=[
            pltpu.VMEM((tokens, D), BF),
            pltpu.VMEM((H, rows, rows), F32),
            pltpu.VMEM((H, rows, rows), BF),
        ],
        compiler_params=pltpu.CompilerParams(vmem_limit_bytes=14 << 20),
        cost_estimate=LONG,
        name="self_back",
    )(da, wo, q, k, v, p, x)


def inputs_back_kernel(
    dq_ref, dk_ref, dv_ref, wq_ref, wk_ref, wv_ref, dr1_ref, dk2_ref, dv2_ref, ck_ref, cv_ref, dx_ref, de_ref
):
    de_ref[...] = dot_nt(dk2_ref[...], ck_ref[...]) + dot_nt(dv2_ref[...], cv_ref[...])
    dx_ref[...] = (
        dr1_ref[...]
        + dot_nt(dq_ref[...], wq_ref[...])
        + dot_nt(dk_ref[...], wk_ref[...])
        + dot_nt(dv_ref[...], wv_ref[...])
    )


def inputs_back(dq, dk, dv, wq, wk, wv, dr1, dk2, dv2, ck, cv):
    return pl.pallas_call(
        inputs_back_kernel,
        out_shape=[
            jax.ShapeDtypeStruct(dr1.shape, F32),
            jax.ShapeDtypeStruct(dk2.shape, F32),
        ],
        compiler_params=pltpu.CompilerParams(vmem_limit_bytes=10 << 20),
        cost_estimate=LONG,
        name="inputs_back",
    )(dq, dk, dv, wq, wk, wv, dr1, dk2, dv2, ck, cv)


def norm(summed):
    centre = summed - jnp.mean(summed, axis=-1, keepdims=True)
    scale = lax.rsqrt(jnp.mean(centre * centre, axis=-1, keepdims=True) + EPS)
    return centre * scale, scale


def norm_back(normal, scale, gain, grad):
    inner = grad * gain
    back = scale * (
        inner
        - jnp.mean(inner, axis=-1, keepdims=True)
        - normal * jnp.mean(inner * normal, axis=-1, keepdims=True)
    )
    return back, jnp.sum(grad * normal, axis=0), jnp.sum(grad, axis=0)


def column_sum(value):
    return jnp.sum(value.astype(F32), axis=0)


def gelu_and_slope(value):
    spread = 0.5 * (1.0 + lax.erf(value * np.float32(np.sqrt(0.5))))
    density = jnp.exp(-0.5 * value * value) * np.float32(1.0 / np.sqrt(2.0 * np.pi))
    return value * spread, spread + value * density


def pack_kernel(sp_ref, so_ref, ab_ref, eb_ref, cb_ref, ng_ref, ns_ref, out_ref):
    rows, n = so_ref.shape[0], ab_ref.shape[1]
    for i in range(3):
        out_ref[i * rows : (i + 1) * rows] = sp_ref[i]
    out_ref[3 * rows : 4 * rows] = so_ref[...]

    def padded(v, width):
        v = v.astype(F32)
        if v.shape[0] < 8:
            v = jnp.concatenate([v, jnp.zeros((8 - v.shape[0], v.shape[1]), F32)])
        return jnp.concatenate([v, jnp.zeros((8, width - v.shape[1]), F32)], axis=1)

    first = jnp.concatenate([ab_ref[...].astype(F32), cb_ref[...].astype(F32)])
    second = jnp.concatenate([ng_ref[...].astype(F32), ns_ref[...].astype(F32)])
    out_ref[4 * rows :] = jnp.concatenate(
        [padded(first, 128), padded(second, 128), padded(eb_ref[...], D - 256)], axis=1
    ).astype(BF)


def pack_self(sp, so, ab, eb, cb, ng, ns):
    ins = [sp, so, ab, eb.reshape(1, -1), cb.reshape(1, -1), ng, ns]
    ins = [pltpu.with_memory_space_constraint(a, pltpu.HBM) for a in ins]
    return pl.pallas_call(
        pack_kernel,
        grid=(1,),
        in_specs=[
            pl.BlockSpec(a.shape, lambda i, n=a.ndim: (0,) * n) for a in ins
        ],
        out_specs=pl.BlockSpec((4 * so.shape[0] + 8, D), lambda i: (0, 0)),
        out_shape=jax.ShapeDtypeStruct((4 * so.shape[0] + 8, D), BF),
        compiler_params=pltpu.CompilerParams(vmem_limit_bytes=4 << 20),
        cost_estimate=QUICK,
        name="pack_self",
    )(*ins)


def pack_small(ab, eb, cb, ng, ns):
    n, wide = cb.shape[0], eb.shape[0]
    return jnp.concatenate(
        [
            jnp.pad(jnp.concatenate([ab, cb[None]]), ((0, 1), (0, 128 - n))),
            jnp.pad(jnp.concatenate([ng, ns]), ((0, 2), (0, 128 - n))),
            jnp.pad(eb[None], ((0, 7), (0, D - 256 - wide))),
        ],
        axis=1,
    )


def unpack_small_kernel(n, wide, in_ref, rows_ref, eb_ref):
    for d in range(in_ref.shape[0]):
        block = in_ref[d].astype(F32)
        rows_ref[0:8, d * n : (d + 1) * n] = block[:, 0:n]
        rows_ref[8:16, d * n : (d + 1) * n] = block[:, 128 : 128 + n]
        eb_ref[:, d * wide : (d + 1) * wide] = block[0:1, 256 : 256 + wide]


def unpack_small(gathered, n, wide):
    devices = gathered.shape[0]
    return pl.pallas_call(
        functools.partial(unpack_small_kernel, n, wide),
        out_shape=[
            jax.ShapeDtypeStruct((16, devices * n), F32),
            jax.ShapeDtypeStruct((1, devices * wide), F32),
        ],
        compiler_params=pltpu.CompilerParams(vmem_limit_bytes=8 << 20),
        cost_estimate=QUICK,
        name="unpack_small",
    )(gathered)


def split_small_kernel(n, wide, ff_ref, cross_ref, self_ref, db_ref, g3_ref, s3_ref, eb_ref, out_ref):
    zero = jnp.zeros((1, D), F32)
    first = jnp.concatenate(
        [
            self_ref[0:2],
            cross_ref[2:5],
            ff_ref[2:3],
            db_ref[...].reshape(1, D),
            zero,
        ],
        axis=0,
    )
    second = jnp.concatenate(
        [
            cross_ref[0:1],
            ff_ref[0:1],
            g3_ref[...].reshape(1, D),
            cross_ref[1:2],
            ff_ref[1:2],
            s3_ref[...].reshape(1, D),
            zero,
            zero,
        ],
        axis=0,
    )
    tail = jnp.broadcast_to(eb_ref[...], (8, FF))

    def padded(v, width):
        return jnp.concatenate([v, jnp.zeros((8, width - v.shape[1]), F32)], axis=1)

    for d in range(out_ref.shape[0]):
        out_ref[d] = jnp.concatenate(
            [
                padded(first[:, d * n : (d + 1) * n], 128),
                padded(second[:, d * n : (d + 1) * n], 128),
                padded(tail[:, d * wide : (d + 1) * wide], D - 256),
            ],
            axis=1,
        ).astype(BF)


def split_small(ff_sums, cross_sums, self_sums, vectors, eb, n, wide):
    devices = D // n
    return pl.pallas_call(
        functools.partial(split_small_kernel, n, wide),
        out_shape=jax.ShapeDtypeStruct((devices, 8, D), BF),
        compiler_params=pltpu.CompilerParams(vmem_limit_bytes=8 << 20),
        cost_estimate=QUICK,
        name="split_small",
    )(ff_sums, cross_sums, self_sums, *vectors, eb)


def body(
    layer_input,
    encoder_states,
    output_grad,
    span_start,
    span_length,
    self_project,
    self_output,
    cross_project,
    cross_output,
    attend_bias,
    expand_weight,
    expand_bias,
    contract_weight,
    contract_bias,
    norm_gain,
    norm_shift,
):
    place = Place()
    count, length = layer_input.shape[:2]
    shape = layer_input.shape
    rows = self_output.shape[0]
    wide = expand_bias.shape[0]
    fits = rows % 8 == 0
    reduce = Reduce if fits else PlainReduce
    x = layer_input.reshape(-1, D)
    memory = encoder_states.reshape(-1, D)
    grad_out = output_grad.reshape(-1, D).astype(F32)

    local_cross = jnp.concatenate([cross_project.reshape(-1, D), cross_output])
    four = [(i * rows, rows) for i in range(4)]
    if fits:
        g_self = Gather(
            place,
            pack_self(
                self_project,
                self_output,
                attend_bias,
                expand_bias,
                contract_bias,
                norm_gain,
                norm_shift,
            ),
        )
        line = g_self.column()
        g_self.hop(0, 0)
        g_self.hop(1, 0)
        g_cross = Gather(place, after(local_cross, line))
        g_self.meet(g_cross)
        g_self.hop(1, 1)
        line = g_cross.column()
        g_cross.hop(0, 0)
        g_cross.hop(1, 0)
        g_self.blocks[3] = after(g_self.blocks[3], line)
        g_expand = Gather(place, after(expand_weight, g_self.blocks[3]))
        g_self.half(line)
        *w_self, smalls = g_self.spread(four + [(4 * rows, 8)])
        smalls = smalls.reshape(-1, 8, D)
    else:
        whole = lax.all_gather(
            jnp.concatenate(
                [
                    self_project.reshape(-1, D),
                    self_output,
                    pack_small(
                        attend_bias, expand_bias, contract_bias, norm_gain, norm_shift
                    ),
                    local_cross,
                    contract_weight,
                ]
            ),
            AXES,
            axis=0,
        )
        squares = [
            whole[:, a : a + rows].reshape(D, D)
            for a in [i * rows for i in range(4)]
            + [4 * rows + 8 + i * rows for i in range(4)]
        ]
        w_self, w_cross = squares[:4], squares[4:]
        contract = whole[:, 8 * rows + 8 :].reshape(FF, D)
        smalls = whole[:, 4 * rows : 4 * rows + 8]
        expand = lax.all_gather(expand_weight, AXES, axis=0, tiled=True)
    wq, wk, wv, wo = w_self
    small_rows, expand_b = unpack_small(smalls, rows, wide)
    biases = [small_rows[i : i + 1] for i in range(6)]
    contract_b = small_rows[6:7]
    gains = [small_rows[8 + i : 9 + i] for i in range(3)]
    shifts = [small_rows[11 + i : 12 + i] for i in range(3)]

    q = ((dot_nn(x, wq) + biases[0]) * 0.125).astype(BF)
    k = dot_nn(x, wk).astype(BF)
    v = (dot_nn(x, wv) + biases[1]).astype(BF)
    o, p = attend(q, k, v, span_start, span_length, True, count)
    if fits:
        g_cross.hop(1, 1, o)
        line = g_expand.column(o)
        g_expand.hop(0, 0)
        g_expand.hop(1, 0)
        g_cross.blocks[3] = after(g_cross.blocks[3], line)
        g_contract = Gather(place, after(contract_weight, g_cross.blocks[3]))
        o = after(o, line)
    r1 = x.astype(F32) + (dot_nn(o, wo) + biases[2])
    n1, s1 = norm(r1)
    x1 = n1 * gains[0] + shifts[0]
    x1b = x1.astype(BF)
    if fits:
        g_cross.half(x1b)
        w_cross = g_cross.spread(four)
    cq, ck, cv, co = w_cross
    q2 = ((dot_nn(x1b, cq) + biases[3]) * 0.125).astype(BF)
    k2 = dot_nn(memory, ck).astype(BF)
    v2 = (dot_nn(memory, cv) + biases[4]).astype(BF)
    o2, p2 = attend(q2, k2, v2, span_start, span_length, False, count)
    if fits:
        g_expand.hop(1, 1, o2)
        line = g_contract.column(o2)
        g_contract.hop(0, 0)
        g_contract.hop(1, 0)
        g_expand.blocks[3] = after(g_expand.blocks[3], line)
        o2 = after(o2, line)
    r2 = x1 + (dot_nn(o2, co) + biases[5])
    n2, s2 = norm(r2)
    x2 = n2 * gains[1] + shifts[1]
    x2b = x2.astype(BF)
    if fits:
        g_expand.half(x2b)
        (expand,) = g_expand.spread([(0, rows)])
    act, slope = gelu_and_slope(dot_nn(x2b, expand) + expand_b)
    act = act.astype(BF)
    slope = slope.astype(BF)
    if fits:
        g_contract.hop(1, 1, act)
        (contract,) = g_contract.spread([(0, 4 * rows)], act)
    n3, s3 = norm(x2 + (dot_nn(act, contract) + contract_b))
    output = (n3 * gains[2] + shifts[2]).astype(BF)

    dr3, gain3, shift3 = norm_back(n3, s3, gains[2], grad_out)
    df = dr3.astype(BF)
    d_contract = dot_tn(act, df).astype(BF)
    r_contract = reduce(place, [owner_blocks(place, d_contract)])
    d_contract_b = column_sum(df)
    du, d_expand_b = hidden_back(after(df, d_contract), contract, slope)
    sent = r_contract.leave(0, du)
    d_expand, dr2, dc, ff_sums = expand_back(
        x2b, after(du, sent), expand, dr3, r2, gains[1]
    )
    sent = r_contract.leave(1, dc)
    r_expand = reduce(place, [owner_blocks(place, after(d_expand, sent))])
    sent = r_expand.leave(0, dc)
    *d_cross, dk2, dv2, dr1, da, cross_sums = cross_back(
        after(dc, sent), co, cq, q2, k2, v2, p2, o2, x1b, memory, dr2, r1, gains[0], o, count
    )
    r_cross = reduce(place, [owner_blocks(place, d) for d in d_cross])
    sent = r_contract.last(da)
    *d_self, dq, dk, dv, self_sums = self_back(after(da, sent), wo, q, k, v, p, x, count)
    sent = r_expand.leave(1, self_sums)
    sent2 = r_cross.leave(0, sent)
    small_blocks = split_small(
        ff_sums,
        cross_sums,
        self_sums,
        [d_contract_b, gain3, shift3],
        d_expand_b,
        rows,
        wide,
    )
    small_blocks = small_blocks.reshape(place.dp_count, place.chips, 2, 8, D)
    (own_contract,) = r_contract.result([((4 * rows, D), 0, 0)], self_sums, sent2)
    r_self = reduce(
        place,
        [owner_blocks(place, d) for d in after(d_self, sent2)] + [small_blocks],
    )
    dq, dk, dv, dk2, dv2 = after((dq, dk, dv, dk2, dv2), sent2, own_contract)
    input_grad, encoder_grad = inputs_back(
        dq, dk, dv, wq, wk, wv, dr1, dk2, dv2, ck, cv
    )
    sent = r_expand.last(input_grad)
    sent2 = r_cross.leave(1, sent)
    sent3 = r_self.leave(0, sent2)
    (own_expand,) = r_expand.result([((rows, FF), 0, 0)], sent3)
    sent = r_cross.last(own_expand)
    sent = r_self.leave(1, sent)
    sent = r_self.last(sent)
    projects = ((3, rows, D), 0, 0)
    square = (rows, D)
    own_cross = r_cross.result(
        [projects, (square, 3 * rows, 0), (square, 4 * rows, 0)], sent
    )
    at = 3 * rows
    own_self = r_self.result(
        [
            projects,
            ((6, rows), at, 0),
            ((1, wide), at, 256),
            ((1, rows), at + 6, 0),
            ((3, rows), at, 128),
            ((3, rows), at + 3, 128),
        ]
    )
    own_self = [own_self[0], own_cross[2], *own_self[1:]]
    return (
        output.reshape(shape),
        input_grad.reshape(shape),
        encoder_grad.reshape(encoder_states.shape),
        own_self[0],
        own_self[1],
        own_cross[0],
        own_cross[1],
        own_self[2],
        own_expand,
        own_self[3].reshape(-1),
        own_contract,
        own_self[4].reshape(-1),
        own_self[5],
        own_self[6],
    )


def solution(mesh):
    rows = P(AXES)
    return jax.shard_map(
        body,
        mesh=mesh,
        in_specs=(
            P(AXES, None, None),
            P(AXES, None, None),
            P(AXES, None, None),
            P(AXES),
            P(AXES),
            P(None, AXES, None),
            P(AXES, None),
            P(None, AXES, None),
            P(AXES, None),
            P(None, AXES),
            P(AXES, None),
            P(AXES),
            P(AXES, None),
            P(AXES),
            P(None, AXES),
            P(None, AXES),
        ),
        out_specs=(
            P(AXES, None, None),
            P(AXES, None, None),
            P(AXES, None, None),
            P(None, AXES, None),
            P(AXES, None),
            P(None, AXES, None),
            P(AXES, None),
            P(None, AXES),
            P(AXES, None),
            P(AXES),
            P(AXES, None),
            P(AXES),
            P(None, AXES),
            P(None, AXES),
        ),
        check_vma=False,
    )
```

```python
import functools

import jax
import jax.numpy as jnp
import numpy as np
from jax import lax
from jax.experimental import pallas as pl
from jax.experimental.pallas import tpu as pltpu
from jax.sharding import PartitionSpec as P

D = 768
H = 12
HD = 64
FF = 3072
AXES = ("dp", "fsdp")

EPS = 1e-05
BIG_NEGATIVE = -1000000000.0
BF = jnp.bfloat16
F32 = jnp.float32
QUICK = pl.CostEstimate(flops=1000, bytes_accessed=1000, transcendentals=0)
LONG = pl.CostEstimate(flops=10**11, bytes_accessed=10**6, transcendentals=0)


class Place:
    def __init__(self):
        self.dp_count = lax.axis_size("dp")
        self.inner = lax.axis_size("fsdp")
        self.chips = self.inner // 2
        self.bits = int(np.log2(self.dp_count))
        self.dp = lax.axis_index("dp")
        inner = lax.axis_index("fsdp")
        self.chip = inner // 2
        self.core = inner % 2
        table = []
        for dp in range(self.dp_count):
            for chip in range(self.chips):
                for core in range(2):
                    table.append(
                        [dp ^ self.mask(core, m) for m in range(self.dp_count)]
                        + [dp ^ self.mask(1 - core, m) for m in range(self.dp_count)]
                        + [(chip + k) % self.chips for k in range(self.chips)]
                        + [(chip - k) % self.chips for k in range(self.chips)]
                        + [core, 1 - core]
                    )
        index = self.dp * self.inner + inner
        self.spots = lax.dynamic_index_in_dim(
            jnp.asarray(np.array(table, np.int32)), index, 0, keepdims=False
        )
        self.theirs_at = self.dp_count
        self.up_at = 2 * self.dp_count
        self.down_at = self.up_at + self.chips
        self.core_at = self.down_at + self.chips

    def bit(self, core, step):
        return 1 << (self.bits - 1 - step if core == 0 else step)

    def mask(self, core, relative):
        return sum(self.bit(core, s) for s in range(self.bits) if relative >> s & 1)

    def permute(self, value, target):
        pairs = []
        for dp in range(self.dp_count):
            for chip in range(self.chips):
                for core in range(2):
                    to = target(dp, chip, core)
                    pairs.append(
                        (
                            dp * self.inner + chip * 2 + core,
                            to[0] * self.inner + to[1] * 2 + to[2],
                        )
                    )
        return lax.ppermute(value, AXES, pairs)

    def across_cores(self, value):
        return self.permute(value, lambda d, z, c: (d, z, 1 - c))

    def across_step(self, value, step):
        return self.permute(value, lambda d, z, c: (d ^ self.bit(c, step), z, c))

    def along_chips(self, value, shift):
        return self.permute(value, lambda d, z, c: (d, (z + shift) % self.chips, c))


def after(values, *earlier):
    return lax.optimization_barrier((values, earlier))[0]


def copy_kernel(plan, n_in, spots_ref, *refs):
    ins, outs, sems = refs[:n_in], refs[n_in:-1], refs[-1]
    copies = []
    for i, (source, source_at, target, target_at) in enumerate(plan):
        copies.append(
            pltpu.make_async_copy(
                ins[source].at[source_at(spots_ref)],
                outs[target].at[target_at(spots_ref)],
                sems.at[i],
            )
        )
    for c in copies:
        c.start()
    for c in copies:
        c.wait()


def copy_call(place, plan, ins, outs, name):
    anywhere = pl.BlockSpec(memory_space=pl.ANY)
    return pl.pallas_call(
        functools.partial(copy_kernel, plan, len(ins)),
        grid_spec=pltpu.PrefetchScalarGridSpec(
            num_scalar_prefetch=1,
            grid=(1,),
            in_specs=[anywhere] * len(ins),
            out_specs=[anywhere] * len(outs),
            scratch_shapes=[pltpu.SemaphoreType.DMA((len(plan),))],
        ),
        out_shape=outs,
        compiler_params=pltpu.CompilerParams(vmem_limit_bytes=1 << 20),
        cost_estimate=QUICK,
        name=name,
    )(place.spots, *ins)


class Gather:
    def __init__(self, place, local):
        self.place = place
        self.local = local
        self.got = [local] + [
            place.along_chips(local, k) for k in range(1, place.chips)
        ]

    def column(self, *earlier):
        place = self.place
        self.got = after(self.got, *earlier)
        plan = [
            (
                k,
                lambda s: (slice(None),),
                0,
                lambda s, k=k: (s[place.down_at + k],),
            )
            for k in range(place.chips)
        ]
        shape = jax.ShapeDtypeStruct((place.chips,) + self.local.shape, BF)
        self.blocks = {0: copy_call(place, plan, self.got, [shape], "column")[0]}
        return self.blocks[0]

    def meet(self, later):
        self.blocks, later.got = lax.optimization_barrier((self.blocks, later.got))

    def hop(self, step, held, *earlier):
        self.blocks[held] = after(self.blocks[held], *earlier)
        self.blocks[held | 1 << step] = self.place.across_step(self.blocks[held], step)

    def share(self, held):
        return self.place.across_cores(self.blocks[held])

    def half(self, *earlier):
        place = self.place
        ins = after([self.blocks[m] for m in range(place.dp_count)], *earlier)
        plan = [
            (m, lambda s: (slice(None),), 0, lambda s, m=m: (s[m],))
            for m in range(place.dp_count)
        ]
        shape = jax.ShapeDtypeStruct((place.dp_count,) + ins[0].shape, BF)
        self.own_half = copy_call(place, plan, ins, [shape], "half")[0]
        self.other_half = place.across_cores(self.own_half)
        return self.own_half

    def spread(self, parts, *earlier):
        place = self.place
        cols = self.local.shape[1]
        whole = slice(None)
        if hasattr(self, "other_half"):
            ins = [self.own_half, self.other_half]
            places = [lambda s: (whole,), lambda s: (whole,)]
        else:
            ins = [self.blocks[m] for m in range(place.dp_count)]
            ins += [self.share(m) for m in range(place.dp_count)]
            places = [lambda s, m=m: (s[m],) for m in range(2 * place.dp_count)]
        ins = after(ins, *earlier)
        plan, outs = [], []
        for out, (first, rows) in enumerate(parts):
            outs.append(
                jax.ShapeDtypeStruct((place.dp_count, place.chips, 2, rows, cols), BF)
            )
            for m, where in enumerate(places):
                core = place.core_at + (m >= len(places) // 2)
                lead = (whole,) * (ins[m].ndim - 2)
                plan.append(
                    (
                        m,
                        lambda s, a=first, n=rows, lead=lead: lead + (pl.ds(a, n),),
                        out,
                        lambda s, where=where, core=core: where(s) + (whole, s[core]),
                    )
                )
        full = copy_call(place, plan, ins, outs, "spread")
        return [w.reshape(-1, cols) for w in full]


def side_by_side(refs):
    parts = [r[...].reshape(r.shape[1:2] + r.shape[-2:]) for r in refs]
    return parts[0] if len(parts) == 1 else jnp.concatenate(parts, axis=1)


def exchange_kernel(spots_ref, *refs):
    out = refs[-1]
    out[...] = side_by_side(refs[:-1]).reshape(out.shape)


def sum_refs(refs, n):
    value = side_by_side(refs[:n]).astype(F32)
    for a in refs[n:]:
        value = value + a[...].astype(F32).reshape(value.shape)
    return value


def leave_kernel(n, spots_ref, *refs):
    out = refs[-1]
    out[...] = sum_refs(refs[:-1], n).astype(BF).reshape(out.shape)


def last_kernel(n, each, chips, spots_ref, *refs):
    outs = refs[chips * each :]
    for k in range(chips):
        value = sum_refs(refs[k * each : (k + 1) * each], n)
        outs[k][...] = value.astype(outs[k].dtype).reshape(outs[k].shape)


def cut_kernel(parts, count, *refs):
    total = refs[0][...].astype(F32)
    for r in refs[1:count]:
        total = total + r[...].astype(F32)
    for (shape, row, col), out in zip(parts, refs[count:]):
        piece = total[row : row + int(np.prod(shape[:-1])), col : col + shape[-1]]
        out[...] = piece.reshape(shape)


def cut_sum(terms, parts):
    return pl.pallas_call(
        functools.partial(cut_kernel, parts, len(terms)),
        out_shape=[jax.ShapeDtypeStruct(s, F32) for s, _, _ in parts],
        compiler_params=pltpu.CompilerParams(vmem_limit_bytes=8 << 20),
        cost_estimate=QUICK,
        name="cut_sum",
    )(*terms)


class Reduce:
    def __init__(self, place, blocks):
        self.place = place
        self.blocks = blocks
        self.rows = sum(b.shape[3] for b in blocks)
        self.cols = blocks[0].shape[4]
        shape = (place.dp_count, place.chips, self.rows, self.cols)
        sent = self.call(
            exchange_kernel,
            (place.dp_count,),
            [
                pl.BlockSpec(
                    (1, place.chips, 1) + b.shape[3:],
                    lambda i, s: (i, 0, s[place.core_at + 1], 0, 0),
                )
                for b in blocks
            ],
            pl.BlockSpec((1,) + shape[1:], lambda i, s: (i, 0, 0, 0)),
            jax.ShapeDtypeStruct(shape, BF),
            "exchange",
        )(place.spots, *blocks)
        self.sent = sent
        self.other = place.across_cores(sent)
        self.got = []

    def call(self, kernel, grid, in_specs, out_specs, out_shape, name):
        return pl.pallas_call(
            kernel,
            grid_spec=pltpu.PrefetchScalarGridSpec(
                num_scalar_prefetch=1, grid=grid, in_specs=in_specs, out_specs=out_specs
            ),
            out_shape=out_shape,
            compiler_params=pltpu.CompilerParams(vmem_limit_bytes=24 << 20),
            cost_estimate=QUICK,
            name=name,
        )

    def leave(self, step, *earlier):
        place = self.place
        if step == 0:
            self.other = after(self.other, *earlier)
        else:
            self.got[-1] = after(self.got[-1], *earlier)
        count = 1 << (place.bits - 1 - step)
        chips, core = place.chips, place.core_at

        def spot(i, s):
            return s[(1 << step) + i * (2 << step)]

        shape = (count, chips, self.rows, self.cols)
        specs = [
            pl.BlockSpec(
                (1, chips, 1) + b.shape[3:], lambda i, s: (spot(i, s), 0, s[core], 0, 0)
            )
            for b in self.blocks
        ]
        specs.append(pl.BlockSpec((1,) + shape[1:], lambda i, s: (spot(i, s), 0, 0, 0)))
        for t in range(step):
            specs.append(
                pl.BlockSpec(
                    (1,) + shape[1:],
                    lambda i, s, t=t: ((1 << (step - t - 1)) + i * (1 << (step - t)), 0, 0, 0),
                )
            )
        sent = self.call(
            functools.partial(leave_kernel, len(self.blocks)),
            (count,),
            specs,
            pl.BlockSpec((1,) + shape[1:], lambda i, s: (i, 0, 0, 0)),
            jax.ShapeDtypeStruct(shape, BF),
            "leave",
        )(place.spots, *self.blocks, self.other, *self.got)
        self.got.append(place.across_step(sent, step))
        return sent

    def latest(self):
        return self.got[-1]

    def last(self, *earlier):
        place = self.place
        self.got[-1] = after(self.got[-1], *earlier)
        chips, core = place.chips, place.core_at
        specs, ins = [], []
        for k in range(chips):
            up = place.up_at + k
            for b in self.blocks:
                ins.append(b)
                specs.append(
                    pl.BlockSpec(
                        (1, 1, 1) + b.shape[3:],
                        lambda i, s, up=up: (s[0], s[up], s[core], 0, 0),
                    )
                )
            for n, g in enumerate([self.other] + self.got):
                ins.append(g)
                specs.append(
                    pl.BlockSpec(
                        (1, 1, self.rows, self.cols),
                        lambda i, s, up=up, n=n: (s[0] if n == 0 else 0, s[up], 0, 0),
                    )
                )
        own, *sent = self.call(
            functools.partial(last_kernel, len(self.blocks), len(ins) // chips, chips),
            (1,),
            specs,
            [pl.BlockSpec((self.rows, self.cols), lambda i, s: (0, 0))] * chips,
            [
                jax.ShapeDtypeStruct((self.rows, self.cols), F32 if k == 0 else BF)
                for k in range(chips)
            ],
            "last",
        )(place.spots, *ins)
        self.own = own
        self.came = [place.along_chips(v, k + 1) for k, v in enumerate(sent)]
        return own

    def result(self, parts, *earlier):
        self.came = after(self.came, *earlier)
        return cut_sum([self.own] + self.came, parts)


def line_kernel(n, each, chips, spots_ref, *refs):
    outs = refs[2 * chips * each :]
    for k in range(chips):
        for i in range(2):
            at = (2 * k + i) * each
            value = sum_refs(refs[at : at + each], n)
            outs[k][i] = value.astype(outs[k].dtype).reshape(outs[k].shape[1:])


def turn_kernel(own_ref, *refs):
    *came, keep_ref, send_ref = refs
    total = own_ref[...]
    for c in came:
        total = total + c[...].astype(F32)
    keep_ref[...] = total[0]
    send_ref[...] = total[1].astype(BF)


class ReduceHopLast(Reduce):
    def line(self, *earlier):
        place = self.place
        self.got[-1] = after(self.got[-1], *earlier)
        chips, core = place.chips, place.core_at
        specs, ins = [], []
        for k in range(chips):
            up = place.up_at + k
            for i in range(2):
                for b in self.blocks:
                    ins.append(b)
                    specs.append(
                        pl.BlockSpec(
                            (1, 1, 1) + b.shape[3:],
                            lambda _, s, up=up, i=i: (s[2 * i], s[up], s[core], 0, 0),
                        )
                    )
                ins.append(self.other)
                specs.append(
                    pl.BlockSpec(
                        (1, 1, self.rows, self.cols),
                        lambda _, s, up=up, i=i: (s[2 * i], s[up], 0, 0),
                    )
                )
                ins.append(self.got[0])
                specs.append(
                    pl.BlockSpec(
                        (1, 1, self.rows, self.cols),
                        lambda _, s, up=up, i=i: (i, s[up], 0, 0),
                    )
                )
        shape = (2, self.rows, self.cols)
        own, *sent = self.call(
            functools.partial(line_kernel, len(self.blocks), len(ins) // chips // 2, chips),
            (1,),
            specs,
            [pl.BlockSpec(shape, lambda _, s: (0, 0, 0))] * chips,
            [jax.ShapeDtypeStruct(shape, F32 if k == 0 else BF) for k in range(chips)],
            "line",
        )(place.spots, *ins)
        self.own = own
        self.came = [place.along_chips(v, k + 1) for k, v in enumerate(sent)]
        return own

    def turn(self, *earlier):
        came = after(self.came, *earlier)
        shape = (self.rows, self.cols)
        self.own, sent = pl.pallas_call(
            turn_kernel,
            out_shape=[jax.ShapeDtypeStruct(shape, F32), jax.ShapeDtypeStruct(shape, BF)],
            compiler_params=pltpu.CompilerParams(vmem_limit_bytes=8 << 20),
            cost_estimate=QUICK,
            name="turn",
        )(self.own, *came)
        self.came = [self.place.across_step(sent, 1)]
        return sent


def owner_blocks(place, gradient):
    rows = gradient.shape[0] // (place.dp_count * place.inner)
    return gradient.reshape(
        place.dp_count, place.chips, 2, rows, gradient.shape[-1]
    )


class PlainReduce:
    def __init__(self, place, blocks):
        devices = place.dp_count * place.inner
        flat = [b.reshape((devices,) + b.shape[3:]) for b in blocks]
        self.sum = lax.psum_scatter(
            jnp.concatenate(flat, axis=1), AXES, scatter_dimension=0, tiled=False
        )
        self.sent = self.sum

    def leave(self, step, *earlier):
        return self.sum

    def last(self, *earlier):
        return self.sum

    def latest(self):
        return self.sum

    def line(self, *earlier):
        return self.sum

    def turn(self, *earlier):
        return self.sum

    def result(self, parts, *earlier):
        total = self.sum.astype(F32)
        return [
            total[r : r + int(np.prod(s[:-1])), c : c + s[-1]].reshape(s)
            for s, r, c in parts
        ]


def dot_nt(a, b):
    return lax.dot_general(a, b, (((1,), (1,)), ((), ())), preferred_element_type=F32)


def dot_nn(a, b):
    return jnp.dot(a, b, preferred_element_type=F32)


def dot_tn(a, b):
    return lax.dot_general(a, b, (((0,), (0,)), ((), ())), preferred_element_type=F32)


def head(h):
    return slice(h * HD, (h + 1) * HD)


def attend_kernel(
    masked, start_ref, length_ref, q_ref, k_ref, v_ref, o_ref, p_ref, scores_ref
):
    rows = q_ref.shape[0]
    keys = k_ref.shape[0]
    if masked:
        seq = pl.program_id(0)
        start = start_ref[seq]
        stop = start + length_ref[seq]
        key_at = lax.broadcasted_iota(jnp.int32, (keys, rows), 0)
        row_at = lax.broadcasted_iota(jnp.int32, (keys, rows), 1)
        inside = (key_at >= start) & (key_at < stop) & (row_at >= start) & (row_at < stop)
        hidden = jnp.where((key_at <= row_at) | inside, 0.0, BIG_NEGATIVE).astype(F32)
    for h in range(H):
        scores_ref[h] = dot_nt(k_ref[:, head(h)], q_ref[:, head(h)])
    for h in range(H):
        scores = scores_ref[h]
        if masked:
            scores = scores + hidden
        peak = jnp.max(scores, axis=0, keepdims=True)
        weights = jnp.exp(scores - peak)
        total = jnp.sum(weights, axis=0, keepdims=True)
        p_ref[0, h] = (weights * (1.0 / total)).astype(BF)
    values_t = v_ref[...].T
    pieces = [dot_nn(values_t[head(h)], p_ref[0, h]) for h in range(H)]
    o_ref[...] = jnp.concatenate(pieces, axis=0).T.astype(BF)


def attend(queries, keys, values, start, length, masked, count):
    rows = queries.shape[0] // count
    key_rows = keys.shape[0] // count
    block = lambda n: pl.BlockSpec((n, D), lambda s, *_: (s, 0))
    return pl.pallas_call(
        functools.partial(attend_kernel, masked),
        grid_spec=pltpu.PrefetchScalarGridSpec(
            num_scalar_prefetch=2,
            grid=(count,),
            in_specs=[block(rows), block(key_rows), block(key_rows)],
            out_specs=[
                block(rows),
                pl.BlockSpec((1, H, key_rows, rows), lambda s, *_: (s, 0, 0, 0)),
            ],
            scratch_shapes=[pltpu.VMEM((H, key_rows, rows), F32)],
        ),
        out_shape=[
            jax.ShapeDtypeStruct(queries.shape, BF),
            jax.ShapeDtypeStruct((count, H, key_rows, rows), BF),
        ],
        compiler_params=pltpu.CompilerParams(vmem_limit_bytes=14 << 20),
        cost_estimate=QUICK,
        name="attend",
    )(start, length, queries, keys, values)


def norm_parts(summed):
    centre = summed - jnp.mean(summed, axis=-1, keepdims=True)
    scale = lax.rsqrt(jnp.mean(centre * centre, axis=-1, keepdims=True) + EPS)
    return centre * scale, scale


def row_sum(value):
    return jnp.sum(value.astype(F32), axis=0, keepdims=True)


def norm_back_sums(summed, gain, grad):
    normal, scale = norm_parts(summed)
    inner = grad * gain
    back = scale * (
        inner
        - jnp.mean(inner, axis=-1, keepdims=True)
        - normal * jnp.mean(inner * normal, axis=-1, keepdims=True)
    )
    return back, [row_sum(grad * normal), row_sum(grad)]


def put_rows(ref, rows):
    for i, r in enumerate(rows):
        ref[i : i + 1] = r


def hidden_back_kernel(df_ref, c_ref, slope_ref, du_ref, sum_ref):
    du = (dot_nt(df_ref[...], c_ref[...]) * slope_ref[...].astype(F32)).astype(BF)
    du_ref[...] = du
    sum_ref[...] = row_sum(du)


def hidden_back(df, contract, slope):
    tokens = df.shape[0]
    return pl.pallas_call(
        hidden_back_kernel,
        grid=(FF // D,),
        in_specs=[
            pl.BlockSpec((tokens, D), lambda j: (0, 0)),
            pl.BlockSpec((D, D), lambda j: (j, 0)),
            pl.BlockSpec((tokens, D), lambda j: (0, j)),
        ],
        out_specs=[
            pl.BlockSpec((tokens, D), lambda j: (0, j)),
            pl.BlockSpec((1, D), lambda j: (0, j)),
        ],
        out_shape=[
            jax.ShapeDtypeStruct((tokens, FF), BF),
            jax.ShapeDtypeStruct((1, FF), F32),
        ],
        compiler_params=pltpu.CompilerParams(vmem_limit_bytes=16 << 20),
        cost_estimate=LONG,
        name="hidden_back",
    )(df, contract, slope)


def expand_back_kernel(
    x_ref, du_ref, e_ref, dr3_ref, r2_ref, gain_ref, de_ref, dr2_ref, dc_ref, sum_ref, xt_ref
):
    j = pl.program_id(0)

    @pl.when(j == 0)
    def _():
        xt_ref[...] = x_ref[...].T
        dr2_ref[...] = dr3_ref[...]

    du = du_ref[...]
    de_ref[...] = dot_nn(xt_ref[...], du).astype(BF)
    dr2_ref[...] += dot_nt(du, e_ref[...])

    @pl.when(j == pl.num_programs(0) - 1)
    def _():
        back, sums = norm_back_sums(r2_ref[...], gain_ref[...], dr2_ref[...])
        dc = back.astype(BF)
        dr2_ref[...] = back
        dc_ref[...] = dc
        put_rows(sum_ref, sums + [row_sum(dc)])


def expand_back(x2b, du, expand, dr3, r2, gain):
    tokens = x2b.shape[0]
    still = pl.BlockSpec((tokens, D), lambda j: (0, 0))
    moving = lambda n: pl.BlockSpec((n, D), lambda j: (0, j))
    return pl.pallas_call(
        expand_back_kernel,
        grid=(FF // D,),
        in_specs=[
            still,
            moving(tokens),
            moving(D),
            still,
            still,
            pl.BlockSpec((1, D), lambda j: (0, 0)),
        ],
        out_specs=[moving(D), still, still, pl.BlockSpec((8, D), lambda j: (0, 0))],
        out_shape=[
            jax.ShapeDtypeStruct((D, FF), BF),
            jax.ShapeDtypeStruct((tokens, D), F32),
            jax.ShapeDtypeStruct((tokens, D), BF),
            jax.ShapeDtypeStruct((8, D), F32),
        ],
        scratch_shapes=[pltpu.VMEM((D, tokens), BF)],
        compiler_params=pltpu.CompilerParams(vmem_limit_bytes=24 << 20),
        cost_estimate=LONG,
        name="expand_back",
    )(x2b, du, expand, dr3, r2, gain)


def heads_back(count, q_ref, k_ref, v_ref, p_ref, g_ref, outs, moved_ref, ds_ref):
    rows = q_ref.shape[0] // count
    keys = k_ref.shape[0] // count
    for s in range(count):
        at = slice(s * rows, (s + 1) * rows)
        key_at = slice(s * keys, (s + 1) * keys)
        for h in range(H):
            moved_ref[h] = dot_nt(v_ref[key_at, head(h)], g_ref[at, head(h)])
        for h in range(H):
            weights = p_ref[s, h].astype(F32)
            moved = moved_ref[h]
            centre = jnp.sum(weights * moved, axis=0, keepdims=True)
            ds_ref[h] = (weights * (moved - centre)).astype(BF)
        keys_t = k_ref[key_at].T
        dq, dk, dv = [], [], []
        for h in range(H):
            dk.append(dot_nn(ds_ref[h], q_ref[at, head(h)]))
            dv.append(dot_nn(p_ref[s, h], g_ref[at, head(h)]))
            dq.append(dot_nn(keys_t[head(h)], ds_ref[h]))
        outs[0][at] = (jnp.concatenate(dq, axis=0).T.astype(BF) * 0.125).astype(BF)
        outs[1][key_at] = jnp.concatenate(dk, axis=1).astype(BF)
        outs[2][key_at] = jnp.concatenate(dv, axis=1).astype(BF)


def cross_back_kernel(
    count,
    dc_ref,
    co_ref,
    cq_ref,
    q_ref,
    k_ref,
    v_ref,
    p_ref,
    o_ref,
    x_ref,
    m_ref,
    dr2_ref,
    r1_ref,
    gain_ref,
    os_ref,
    dwq_ref,
    dwk_ref,
    dwv_ref,
    dwo_ref,
    dso_ref,
    dk_ref,
    dv_ref,
    dr1_ref,
    da_ref,
    sum_ref,
    g_ref,
    dq_ref,
    moved_ref,
    ds_ref,
):
    dc = dc_ref[...]
    g_ref[...] = dot_nt(dc, co_ref[...]).astype(BF)
    dwo_ref[...] = dot_tn(o_ref[...], dc).astype(BF)
    heads_back(
        count, q_ref, k_ref, v_ref, p_ref, g_ref, (dq_ref, dk_ref, dv_ref), moved_ref, ds_ref
    )
    dq = dq_ref[...]
    dr1 = dr2_ref[...] + dot_nt(dq, cq_ref[...])
    dwq_ref[...] = dot_tn(x_ref[...], dq).astype(BF)
    mt = m_ref[...].T
    dwk_ref[...] = dot_nn(mt, dk_ref[...]).astype(BF)
    dwv_ref[...] = dot_nn(mt, dv_ref[...]).astype(BF)
    back, sums = norm_back_sums(r1_ref[...], gain_ref[...], dr1)
    da = back.astype(BF)
    dr1_ref[...] = back
    da_ref[...] = da
    dso_ref[...] = dot_tn(os_ref[...], da).astype(BF)
    put_rows(sum_ref, sums + [row_sum(da), row_sum(dq), row_sum(dv_ref[...])])


def cross_back(dc, co, cq, q2, k2, v2, p2, o2, x1b, memory, dr2, r1, gain, o, count):
    tokens, rows = dc.shape[0], dc.shape[0] // count
    keys = memory.shape[0] // count
    square = jax.ShapeDtypeStruct((D, D), BF)
    low = jax.ShapeDtypeStruct((tokens, D), BF)
    return pl.pallas_call(
        functools.partial(cross_back_kernel, count),
        out_shape=[square] * 5
        + [
            jax.ShapeDtypeStruct(memory.shape, BF),
            jax.ShapeDtypeStruct(memory.shape, BF),
            jax.ShapeDtypeStruct((tokens, D), F32),
            low,
            jax.ShapeDtypeStruct((8, D), F32),
        ],
        scratch_shapes=[
            pltpu.VMEM((tokens, D), BF),
            pltpu.VMEM((tokens, D), BF),
            pltpu.VMEM((H, keys, rows), F32),
            pltpu.VMEM((H, keys, rows), BF),
        ],
        compiler_params=pltpu.CompilerParams(vmem_limit_bytes=18 << 20),
        cost_estimate=LONG,
        name="cross_back",
    )(dc, co, cq, q2, k2, v2, p2, o2, x1b, memory, dr2, r1, gain, o)


def self_back_kernel(
    count,
    da_ref,
    wo_ref,
    q_ref,
    k_ref,
    v_ref,
    p_ref,
    x_ref,
    dwq_ref,
    dwk_ref,
    dwv_ref,
    dq_ref,
    dk_ref,
    dv_ref,
    sum_ref,
    g_ref,
    moved_ref,
    ds_ref,
):
    g_ref[...] = dot_nt(da_ref[...], wo_ref[...]).astype(BF)
    heads_back(
        count, q_ref, k_ref, v_ref, p_ref, g_ref, (dq_ref, dk_ref, dv_ref), moved_ref, ds_ref
    )
    xt = x_ref[...].T
    dwq_ref[...] = dot_nn(xt, dq_ref[...]).astype(BF)
    dwk_ref[...] = dot_nn(xt, dk_ref[...]).astype(BF)
    dwv_ref[...] = dot_nn(xt, dv_ref[...]).astype(BF)
    put_rows(sum_ref, [row_sum(dq_ref[...]), row_sum(dv_ref[...])])


def self_back(da, wo, q, k, v, p, x, count):
    tokens, rows = da.shape[0], da.shape[0] // count
    square = jax.ShapeDtypeStruct((D, D), BF)
    low = jax.ShapeDtypeStruct((tokens, D), BF)
    return pl.pallas_call(
        functools.partial(self_back_kernel, count),
        out_shape=[square] * 3 + [low] * 3 + [jax.ShapeDtypeStruct((8, D), F32)],
        scratch_shapes=[
            pltpu.VMEM((tokens, D), BF),
            pltpu.VMEM((H, rows, rows), F32),
            pltpu.VMEM((H, rows, rows), BF),
        ],
        compiler_params=pltpu.CompilerParams(vmem_limit_bytes=14 << 20),
        cost_estimate=LONG,
        name="self_back",
    )(da, wo, q, k, v, p, x)


def inputs_back_kernel(
    dq_ref, dk_ref, dv_ref, wq_ref, wk_ref, wv_ref, dr1_ref, dk2_ref, dv2_ref, ck_ref, cv_ref, dx_ref, de_ref
):
    de_ref[...] = dot_nt(dk2_ref[...], ck_ref[...]) + dot_nt(dv2_ref[...], cv_ref[...])
    dx_ref[...] = (
        dr1_ref[...]
        + dot_nt(dq_ref[...], wq_ref[...])
        + dot_nt(dk_ref[...], wk_ref[...])
        + dot_nt(dv_ref[...], wv_ref[...])
    )


def inputs_back(dq, dk, dv, wq, wk, wv, dr1, dk2, dv2, ck, cv):
    return pl.pallas_call(
        inputs_back_kernel,
        out_shape=[
            jax.ShapeDtypeStruct(dr1.shape, F32),
            jax.ShapeDtypeStruct(dk2.shape, F32),
        ],
        compiler_params=pltpu.CompilerParams(vmem_limit_bytes=10 << 20),
        cost_estimate=LONG,
        name="inputs_back",
    )(dq, dk, dv, wq, wk, wv, dr1, dk2, dv2, ck, cv)


def norm(summed):
    centre = summed - jnp.mean(summed, axis=-1, keepdims=True)
    scale = lax.rsqrt(jnp.mean(centre * centre, axis=-1, keepdims=True) + EPS)
    return centre * scale, scale


def norm_back(normal, scale, gain, grad):
    inner = grad * gain
    back = scale * (
        inner
        - jnp.mean(inner, axis=-1, keepdims=True)
        - normal * jnp.mean(inner * normal, axis=-1, keepdims=True)
    )
    return back, jnp.sum(grad * normal, axis=0), jnp.sum(grad, axis=0)


def column_sum(value):
    return jnp.sum(value.astype(F32), axis=0)


def gelu_and_slope(value):
    spread = 0.5 * (1.0 + lax.erf(value * np.float32(np.sqrt(0.5))))
    density = jnp.exp(-0.5 * value * value) * np.float32(1.0 / np.sqrt(2.0 * np.pi))
    return value * spread, spread + value * density


def pack_kernel(sp_ref, so_ref, ab_ref, eb_ref, cb_ref, ng_ref, ns_ref, out_ref):
    rows, n = so_ref.shape[0], ab_ref.shape[1]
    for i in range(3):
        out_ref[i * rows : (i + 1) * rows] = sp_ref[i]
    out_ref[3 * rows : 4 * rows] = so_ref[...]

    def padded(v, width):
        v = v.astype(F32)
        if v.shape[0] < 8:
            v = jnp.concatenate([v, jnp.zeros((8 - v.shape[0], v.shape[1]), F32)])
        return jnp.concatenate([v, jnp.zeros((8, width - v.shape[1]), F32)], axis=1)

    first = jnp.concatenate([ab_ref[...].astype(F32), cb_ref[...].astype(F32)])
    second = jnp.concatenate([ng_ref[...].astype(F32), ns_ref[...].astype(F32)])
    out_ref[4 * rows :] = jnp.concatenate(
        [padded(first, 128), padded(second, 128), padded(eb_ref[...], D - 256)], axis=1
    ).astype(BF)


def pack_self(sp, so, ab, eb, cb, ng, ns):
    ins = [sp, so, ab, eb.reshape(1, -1), cb.reshape(1, -1), ng, ns]
    ins = [pltpu.with_memory_space_constraint(a, pltpu.HBM) for a in ins]
    return pl.pallas_call(
        pack_kernel,
        grid=(1,),
        in_specs=[
            pl.BlockSpec(a.shape, lambda i, n=a.ndim: (0,) * n) for a in ins
        ],
        out_specs=pl.BlockSpec((4 * so.shape[0] + 8, D), lambda i: (0, 0)),
        out_shape=jax.ShapeDtypeStruct((4 * so.shape[0] + 8, D), BF),
        compiler_params=pltpu.CompilerParams(vmem_limit_bytes=4 << 20),
        cost_estimate=QUICK,
        name="pack_self",
    )(*ins)


def pack_small(ab, eb, cb, ng, ns):
    n, wide = cb.shape[0], eb.shape[0]
    return jnp.concatenate(
        [
            jnp.pad(jnp.concatenate([ab, cb[None]]), ((0, 1), (0, 128 - n))),
            jnp.pad(jnp.concatenate([ng, ns]), ((0, 2), (0, 128 - n))),
            jnp.pad(eb[None], ((0, 7), (0, D - 256 - wide))),
        ],
        axis=1,
    )


def unpack_small_kernel(n, wide, in_ref, rows_ref, eb_ref):
    for d in range(in_ref.shape[0]):
        block = in_ref[d].astype(F32)
        rows_ref[0:8, d * n : (d + 1) * n] = block[:, 0:n]
        rows_ref[8:16, d * n : (d + 1) * n] = block[:, 128 : 128 + n]
        eb_ref[:, d * wide : (d + 1) * wide] = block[0:1, 256 : 256 + wide]


def unpack_small(gathered, n, wide):
    devices = gathered.shape[0]
    return pl.pallas_call(
        functools.partial(unpack_small_kernel, n, wide),
        out_shape=[
            jax.ShapeDtypeStruct((16, devices * n), F32),
            jax.ShapeDtypeStruct((1, devices * wide), F32),
        ],
        compiler_params=pltpu.CompilerParams(vmem_limit_bytes=8 << 20),
        cost_estimate=QUICK,
        name="unpack_small",
    )(gathered)


def split_small_kernel(n, wide, ff_ref, cross_ref, self_ref, db_ref, g3_ref, s3_ref, eb_ref, out_ref):
    zero = jnp.zeros((1, D), F32)
    first = jnp.concatenate(
        [
            self_ref[0:2],
            cross_ref[2:5],
            ff_ref[2:3],
            db_ref[...].reshape(1, D),
            zero,
        ],
        axis=0,
    )
    second = jnp.concatenate(
        [
            cross_ref[0:1],
            ff_ref[0:1],
            g3_ref[...].reshape(1, D),
            cross_ref[1:2],
            ff_ref[1:2],
            s3_ref[...].reshape(1, D),
            zero,
            zero,
        ],
        axis=0,
    )
    tail = jnp.broadcast_to(eb_ref[...], (8, FF))

    def padded(v, width):
        return jnp.concatenate([v, jnp.zeros((8, width - v.shape[1]), F32)], axis=1)

    for d in range(out_ref.shape[0]):
        out_ref[d] = jnp.concatenate(
            [
                padded(first[:, d * n : (d + 1) * n], 128),
                padded(second[:, d * n : (d + 1) * n], 128),
                padded(tail[:, d * wide : (d + 1) * wide], D - 256),
            ],
            axis=1,
        ).astype(BF)


def split_small(ff_sums, cross_sums, self_sums, vectors, eb, n, wide):
    devices = D // n
    return pl.pallas_call(
        functools.partial(split_small_kernel, n, wide),
        out_shape=jax.ShapeDtypeStruct((devices, 8, D), BF),
        compiler_params=pltpu.CompilerParams(vmem_limit_bytes=8 << 20),
        cost_estimate=QUICK,
        name="split_small",
    )(ff_sums, cross_sums, self_sums, *vectors, eb)


def body(
    layer_input,
    encoder_states,
    output_grad,
    span_start,
    span_length,
    self_project,
    self_output,
    cross_project,
    cross_output,
    attend_bias,
    expand_weight,
    expand_bias,
    contract_weight,
    contract_bias,
    norm_gain,
    norm_shift,
):
    place = Place()
    count, length = layer_input.shape[:2]
    shape = layer_input.shape
    rows = self_output.shape[0]
    wide = expand_bias.shape[0]
    fits = rows % 8 == 0 and place.bits == 2
    reduce = Reduce if fits else PlainReduce
    reduce_hop_last = ReduceHopLast if fits else PlainReduce
    x = layer_input.reshape(-1, D)
    memory = encoder_states.reshape(-1, D)
    grad_out = output_grad.reshape(-1, D).astype(F32)

    local_cross = jnp.concatenate([cross_project.reshape(-1, D), cross_output])
    four = [(i * rows, rows) for i in range(4)]
    if fits:
        g_self = Gather(
            place,
            pack_self(
                self_project,
                self_output,
                attend_bias,
                expand_bias,
                contract_bias,
                norm_gain,
                norm_shift,
            ),
        )
        line = g_self.column()
        g_self.hop(0, 0)
        g_self.hop(1, 0)
        g_cross = Gather(place, after(local_cross, line))
        g_self.blocks, g_cross.got = lax.optimization_barrier((g_self.blocks, g_cross.got))
        g_self.hop(1, 1)
        line = g_cross.column()
        g_cross.hop(0, 0)
        g_cross.hop(1, 0)
        g_expand = Gather(place, after(expand_weight, line))
        g_self.blocks, g_cross.blocks, g_expand.got = lax.optimization_barrier(
            (g_self.blocks, g_cross.blocks, g_expand.got)
        )
        g_cross.hop(1, 1)
        line = g_expand.column()
        g_expand.hop(0, 0)
        g_expand.hop(1, 0)
        g_contract = Gather(place, after(contract_weight, line))
        g_self.half(line)
        *w_self, smalls = g_self.spread(four + [(4 * rows, 8)])
        smalls = smalls.reshape(-1, 8, D)
    else:
        whole = lax.all_gather(
            jnp.concatenate(
                [
                    self_project.reshape(-1, D),
                    self_output,
                    pack_small(
                        attend_bias, expand_bias, contract_bias, norm_gain, norm_shift
                    ),
                    local_cross,
                    contract_weight,
                ]
            ),
            AXES,
            axis=0,
        )
        squares = [
            whole[:, a : a + rows].reshape(D, D)
            for a in [i * rows for i in range(4)]
            + [4 * rows + 8 + i * rows for i in range(4)]
        ]
        w_self, w_cross = squares[:4], squares[4:]
        contract = whole[:, 8 * rows + 8 :].reshape(FF, D)
        smalls = whole[:, 4 * rows : 4 * rows + 8]
        expand = lax.all_gather(expand_weight, AXES, axis=0, tiled=True)
    wq, wk, wv, wo = w_self
    small_rows, expand_b = unpack_small(smalls, rows, wide)
    biases = [small_rows[i : i + 1] for i in range(6)]
    contract_b = small_rows[6:7]
    gains = [small_rows[8 + i : 9 + i] for i in range(3)]
    shifts = [small_rows[11 + i : 12 + i] for i in range(3)]

    q = ((dot_nn(x, wq) + biases[0]) * 0.125).astype(BF)
    k = dot_nn(x, wk).astype(BF)
    v = (dot_nn(x, wv) + biases[1]).astype(BF)
    o, p = attend(q, k, v, span_start, span_length, True, count)
    if fits:
        g_cross.blocks, g_expand.blocks, g_contract.got, o = lax.optimization_barrier(
            (g_cross.blocks, g_expand.blocks, g_contract.got, o)
        )
        g_expand.hop(1, 1)
        line = g_contract.column()
        g_contract.hop(0, 0)
        g_contract.hop(1, 0)
        g_cross.half(line)
        w_cross = g_cross.spread(four)
    r1 = x.astype(F32) + (dot_nn(o, wo) + biases[2])
    n1, s1 = norm(r1)
    x1 = n1 * gains[0] + shifts[0]
    x1b = x1.astype(BF)
    cq, ck, cv, co = w_cross
    q2 = ((dot_nn(x1b, cq) + biases[3]) * 0.125).astype(BF)
    k2 = dot_nn(memory, ck).astype(BF)
    v2 = (dot_nn(memory, cv) + biases[4]).astype(BF)
    o2, p2 = attend(q2, k2, v2, span_start, span_length, False, count)
    if fits:
        g_expand.blocks, g_contract.blocks, o2 = lax.optimization_barrier(
            (g_expand.blocks, g_contract.blocks, o2)
        )
        g_contract.hop(1, 1)
        g_expand.half()
        (expand,) = g_expand.spread([(0, rows)])
    r2 = x1 + (dot_nn(o2, co) + biases[5])
    n2, s2 = norm(r2)
    x2 = n2 * gains[1] + shifts[1]
    x2b = x2.astype(BF)
    act, slope = gelu_and_slope(dot_nn(x2b, expand) + expand_b)
    act = act.astype(BF)
    slope = slope.astype(BF)
    if fits:
        g_contract.blocks[3] = after(g_contract.blocks[3], act)
        (contract,) = g_contract.spread([(0, 4 * rows)])
    n3, s3 = norm(x2 + (dot_nn(act, contract) + contract_b))
    output = (n3 * gains[2] + shifts[2]).astype(BF)

    dr3, gain3, shift3 = norm_back(n3, s3, gains[2], grad_out)
    df = dr3.astype(BF)
    d_contract = dot_tn(act, df).astype(BF)
    r_contract = reduce_hop_last(place, [owner_blocks(place, d_contract)])
    d_contract_b = column_sum(df)
    du, d_expand_b = hidden_back(after(df, d_contract), contract, slope)
    sent = r_contract.leave(0, du)
    d_expand, dr2, dc, ff_sums = expand_back(
        x2b, after(du, sent), expand, dr3, r2, gains[1]
    )
    sent = r_contract.line(dc)
    r_expand = reduce_hop_last(place, [owner_blocks(place, after(d_expand, sent))])
    sent = r_expand.leave(0, dc)
    *d_cross, dk2, dv2, dr1, da, cross_sums = cross_back(
        after(dc, sent), co, cq, q2, k2, v2, p2, o2, x1b, memory, dr2, r1, gains[0], o, count
    )
    r_cross = reduce(place, [owner_blocks(place, d) for d in d_cross])
    sent = r_expand.line(da)
    sent = r_contract.turn(sent)
    *d_self, dq, dk, dv, self_sums = self_back(after(da, sent), wo, q, k, v, p, x, count)
    sent = r_cross.leave(0, self_sums)
    small_blocks = split_small(
        ff_sums,
        cross_sums,
        self_sums,
        [d_contract_b, gain3, shift3],
        d_expand_b,
        rows,
        wide,
    )
    small_blocks = small_blocks.reshape(place.dp_count, place.chips, 2, 8, D)
    r_self = reduce(
        place,
        [owner_blocks(place, d) for d in after(d_self, sent)] + [small_blocks],
    )
    sent = r_expand.turn(r_self.sent)
    (own_contract,) = r_contract.result([((4 * rows, D), 0, 0)], sent)
    dq, dk, dv, dk2, dv2 = after((dq, dk, dv, dk2, dv2), own_contract)
    input_grad, encoder_grad = inputs_back(
        dq, dk, dv, wq, wk, wv, dr1, dk2, dv2, ck, cv
    )
    r_cross.leave(1, input_grad)
    sent = r_self.leave(0, r_cross.latest())
    sent = r_cross.last(sent)
    sent = r_self.leave(1, sent)
    (own_expand,) = r_expand.result([((rows, FF), 0, 0)], sent)
    sent = r_self.last(own_expand)
    projects = ((3, rows, D), 0, 0)
    square = (rows, D)
    own_cross = r_cross.result(
        [projects, (square, 3 * rows, 0), (square, 4 * rows, 0)], sent
    )
    at = 3 * rows
    own_self = r_self.result(
        [
            projects,
            ((6, rows), at, 0),
            ((1, wide), at, 256),
            ((1, rows), at + 6, 0),
            ((3, rows), at, 128),
            ((3, rows), at + 3, 128),
        ]
    )
    own_self = [own_self[0], own_cross[2], *own_self[1:]]
    return (
        output.reshape(shape),
        input_grad.reshape(shape),
        encoder_grad.reshape(encoder_states.shape),
        own_self[0],
        own_self[1],
        own_cross[0],
        own_cross[1],
        own_self[2],
        own_expand,
        own_self[3].reshape(-1),
        own_contract,
        own_self[4].reshape(-1),
        own_self[5],
        own_self[6],
    )


def solution(mesh):
    rows = P(AXES)
    return jax.shard_map(
        body,
        mesh=mesh,
        in_specs=(
            P(AXES, None, None),
            P(AXES, None, None),
            P(AXES, None, None),
            P(AXES),
            P(AXES),
            P(None, AXES, None),
            P(AXES, None),
            P(None, AXES, None),
            P(AXES, None),
            P(None, AXES),
            P(AXES, None),
            P(AXES),
            P(AXES, None),
            P(AXES),
            P(None, AXES),
            P(None, AXES),
        ),
        out_specs=(
            P(AXES, None, None),
            P(AXES, None, None),
            P(AXES, None, None),
            P(None, AXES, None),
            P(AXES, None),
            P(None, AXES, None),
            P(AXES, None),
            P(None, AXES),
            P(AXES, None),
            P(AXES),
            P(AXES, None),
            P(AXES),
            P(None, AXES),
            P(None, AXES),
        ),
        check_vma=False,
    )
```

```python
import functools

import jax
import jax.numpy as jnp
import numpy as np
from jax import lax
from jax.experimental import pallas as pl
from jax.experimental.pallas import tpu as pltpu
from jax.sharding import PartitionSpec as P

D = 768
H = 12
HD = 64
FF = 3072
AXES = ("dp", "fsdp")

EPS = 1e-05
BIG_NEGATIVE = -1000000000.0
BF = jnp.bfloat16
F32 = jnp.float32
QUICK = pl.CostEstimate(flops=1000, bytes_accessed=1000, transcendentals=0)
LONG = pl.CostEstimate(flops=4 * 10**10, bytes_accessed=10**6, transcendentals=0)


class Place:
    def __init__(self):
        self.dp_count = lax.axis_size("dp")
        self.inner = lax.axis_size("fsdp")
        self.chips = self.inner // 2
        self.bits = int(np.log2(self.dp_count))
        self.dp = lax.axis_index("dp")
        inner = lax.axis_index("fsdp")
        self.chip = inner // 2
        self.core = inner % 2
        table = []
        for dp in range(self.dp_count):
            for chip in range(self.chips):
                for core in range(2):
                    table.append(
                        [dp ^ self.mask(core, m) for m in range(self.dp_count)]
                        + [dp ^ self.mask(1 - core, m) for m in range(self.dp_count)]
                        + [(chip + k) % self.chips for k in range(self.chips)]
                        + [(chip - k) % self.chips for k in range(self.chips)]
                        + [core, 1 - core]
                    )
        index = self.dp * self.inner + inner
        self.spots = lax.dynamic_index_in_dim(
            jnp.asarray(np.array(table, np.int32)), index, 0, keepdims=False
        )
        self.theirs_at = self.dp_count
        self.up_at = 2 * self.dp_count
        self.down_at = self.up_at + self.chips
        self.core_at = self.down_at + self.chips

    def bit(self, core, step):
        return 1 << (self.bits - 1 - step if core == 0 else step)

    def mask(self, core, relative):
        return sum(self.bit(core, s) for s in range(self.bits) if relative >> s & 1)

    def permute(self, value, target):
        pairs = []
        for dp in range(self.dp_count):
            for chip in range(self.chips):
                for core in range(2):
                    to = target(dp, chip, core)
                    pairs.append(
                        (
                            dp * self.inner + chip * 2 + core,
                            to[0] * self.inner + to[1] * 2 + to[2],
                        )
                    )
        return lax.ppermute(value, AXES, pairs)

    def across_cores(self, value):
        return self.permute(value, lambda d, z, c: (d, z, 1 - c))

    def across_step(self, value, step):
        return self.permute(value, lambda d, z, c: (d ^ self.bit(c, step), z, c))

    def along_chips(self, value, shift):
        return self.permute(value, lambda d, z, c: (d, (z + shift) % self.chips, c))


def after(values, *earlier):
    return lax.optimization_barrier((values, earlier))[0]


def copy_kernel(plan, n_in, spots_ref, *refs):
    ins, outs, sems = refs[:n_in], refs[n_in:-1], refs[-1]
    copies = []
    for i, (source, source_at, target, target_at) in enumerate(plan):
        copies.append(
            pltpu.make_async_copy(
                ins[source].at[source_at(spots_ref)],
                outs[target].at[target_at(spots_ref)],
                sems.at[i],
            )
        )
    for c in copies:
        c.start()
    for c in copies:
        c.wait()


def copy_call(place, plan, ins, outs, name):
    anywhere = pl.BlockSpec(memory_space=pl.ANY)
    return pl.pallas_call(
        functools.partial(copy_kernel, plan, len(ins)),
        grid_spec=pltpu.PrefetchScalarGridSpec(
            num_scalar_prefetch=1,
            grid=(1,),
            in_specs=[anywhere] * len(ins),
            out_specs=[anywhere] * len(outs),
            scratch_shapes=[pltpu.SemaphoreType.DMA((len(plan),))],
        ),
        out_shape=outs,
        compiler_params=pltpu.CompilerParams(vmem_limit_bytes=1 << 20),
        cost_estimate=QUICK,
        name=name,
    )(place.spots, *ins)


def fence_kernel(in_ref, out_ref):
    for i in range(in_ref.shape[0]):
        out_ref[i] = in_ref[i]


def fence(place, *values):
    spots = place.spots
    scalars = pl.BlockSpec(memory_space=pltpu.SMEM)
    place.spots = pl.pallas_call(
        fence_kernel,
        in_specs=[scalars],
        out_specs=scalars,
        out_shape=jax.ShapeDtypeStruct(spots.shape, spots.dtype),
        compiler_params=pltpu.CompilerParams(vmem_limit_bytes=1 << 20),
        cost_estimate=LONG,
        name="fence",
    )(after(spots, *values))
    return place.spots


class Gather:
    def __init__(self, place, local):
        self.place = place
        self.local = local
        self.got = [local] + [
            place.along_chips(local, k) for k in range(1, place.chips)
        ]

    def column(self, *earlier):
        place = self.place
        self.got = after(self.got, *earlier)
        plan = [
            (
                k,
                lambda s: (slice(None),),
                0,
                lambda s, k=k: (s[place.down_at + k],),
            )
            for k in range(place.chips)
        ]
        shape = jax.ShapeDtypeStruct((place.chips,) + self.local.shape, BF)
        self.blocks = {0: copy_call(place, plan, self.got, [shape], "column")[0]}
        return self.blocks[0]

    def meet(self, later):
        self.blocks, later.got = lax.optimization_barrier((self.blocks, later.got))

    def hop(self, step, held, *earlier):
        self.blocks[held] = after(self.blocks[held], *earlier)
        self.blocks[held | 1 << step] = self.place.across_step(self.blocks[held], step)

    def share(self, held):
        return self.place.across_cores(self.blocks[held])

    def half(self, *earlier):
        place = self.place
        ins = after([self.blocks[m] for m in range(place.dp_count)], *earlier)
        plan = [
            (m, lambda s: (slice(None),), 0, lambda s, m=m: (s[m],))
            for m in range(place.dp_count)
        ]
        shape = jax.ShapeDtypeStruct((place.dp_count,) + ins[0].shape, BF)
        self.own_half = copy_call(place, plan, ins, [shape], "half")[0]
        self.other_half = place.across_cores(self.own_half)
        return self.own_half

    def spread(self, parts, *earlier):
        place = self.place
        cols = self.local.shape[1]
        whole = slice(None)
        if hasattr(self, "other_half"):
            ins = [self.own_half, self.other_half]
            places = [lambda s: (whole,), lambda s: (whole,)]
        else:
            ins = [self.blocks[m] for m in range(place.dp_count)]
            ins += [self.share(m) for m in range(place.dp_count)]
            places = [lambda s, m=m: (s[m],) for m in range(2 * place.dp_count)]
        ins = after(ins, *earlier)
        plan, outs = [], []
        for out, (first, rows) in enumerate(parts):
            outs.append(
                jax.ShapeDtypeStruct((place.dp_count, place.chips, 2, rows, cols), BF)
            )
            for m, where in enumerate(places):
                core = place.core_at + (m >= len(places) // 2)
                lead = (whole,) * (ins[m].ndim - 2)
                plan.append(
                    (
                        m,
                        lambda s, a=first, n=rows, lead=lead: lead + (pl.ds(a, n),),
                        out,
                        lambda s, where=where, core=core: where(s) + (whole, s[core]),
                    )
                )
        full = copy_call(place, plan, ins, outs, "spread")
        return [w.reshape(-1, cols) for w in full]


def side_by_side(refs):
    parts = [r[...].reshape(r.shape[1:2] + r.shape[-2:]) for r in refs]
    return parts[0] if len(parts) == 1 else jnp.concatenate(parts, axis=1)


def exchange_kernel(spots_ref, *refs):
    out = refs[-1]
    out[...] = side_by_side(refs[:-1]).reshape(out.shape)


def sum_refs(refs, n):
    value = side_by_side(refs[:n]).astype(F32)
    for a in refs[n:]:
        value = value + a[...].astype(F32).reshape(value.shape)
    return value


def leave_kernel(n, spots_ref, *refs):
    out = refs[-1]
    out[...] = sum_refs(refs[:-1], n).astype(BF).reshape(out.shape)


def last_kernel(n, each, chips, spots_ref, *refs):
    outs = refs[chips * each :]
    for k in range(chips):
        value = sum_refs(refs[k * each : (k + 1) * each], n)
        outs[k][...] = value.astype(outs[k].dtype).reshape(outs[k].shape)


def cut_kernel(parts, count, *refs):
    total = refs[0][...].astype(F32)
    for r in refs[1:count]:
        total = total + r[...].astype(F32)
    for (shape, row, col), out in zip(parts, refs[count:]):
        piece = total[row : row + int(np.prod(shape[:-1])), col : col + shape[-1]]
        out[...] = piece.reshape(shape)


def cut_sum(terms, parts):
    return pl.pallas_call(
        functools.partial(cut_kernel, parts, len(terms)),
        out_shape=[jax.ShapeDtypeStruct(s, F32) for s, _, _ in parts],
        compiler_params=pltpu.CompilerParams(vmem_limit_bytes=8 << 20),
        cost_estimate=QUICK,
        name="cut_sum",
    )(*terms)


class Reduce:
    def __init__(self, place, blocks):
        self.place = place
        self.blocks = blocks
        self.rows = sum(b.shape[3] for b in blocks)
        self.cols = blocks[0].shape[4]
        shape = (place.dp_count, place.chips, self.rows, self.cols)
        sent = self.call(
            exchange_kernel,
            (place.dp_count,),
            [
                pl.BlockSpec(
                    (1, place.chips, 1) + b.shape[3:],
                    lambda i, s: (i, 0, s[place.core_at + 1], 0, 0),
                )
                for b in blocks
            ],
            pl.BlockSpec((1,) + shape[1:], lambda i, s: (i, 0, 0, 0)),
            jax.ShapeDtypeStruct(shape, BF),
            "exchange",
        )(place.spots, *blocks)
        self.sent = sent
        self.other = place.across_cores(sent)
        self.got = []

    def call(self, kernel, grid, in_specs, out_specs, out_shape, name):
        return pl.pallas_call(
            kernel,
            grid_spec=pltpu.PrefetchScalarGridSpec(
                num_scalar_prefetch=1, grid=grid, in_specs=in_specs, out_specs=out_specs
            ),
            out_shape=out_shape,
            compiler_params=pltpu.CompilerParams(vmem_limit_bytes=24 << 20),
            cost_estimate=QUICK,
            name=name,
        )

    def leave(self, step, *earlier):
        place = self.place
        if step == 0:
            self.other = after(self.other, *earlier)
        else:
            self.got[-1] = after(self.got[-1], *earlier)
        count = 1 << (place.bits - 1 - step)
        chips, core = place.chips, place.core_at

        def spot(i, s):
            return s[(1 << step) + i * (2 << step)]

        shape = (count, chips, self.rows, self.cols)
        specs = [
            pl.BlockSpec(
                (1, chips, 1) + b.shape[3:], lambda i, s: (spot(i, s), 0, s[core], 0, 0)
            )
            for b in self.blocks
        ]
        specs.append(pl.BlockSpec((1,) + shape[1:], lambda i, s: (spot(i, s), 0, 0, 0)))
        for t in range(step):
            specs.append(
                pl.BlockSpec(
                    (1,) + shape[1:],
                    lambda i, s, t=t: ((1 << (step - t - 1)) + i * (1 << (step - t)), 0, 0, 0),
                )
            )
        sent = self.call(
            functools.partial(leave_kernel, len(self.blocks)),
            (count,),
            specs,
            pl.BlockSpec((1,) + shape[1:], lambda i, s: (i, 0, 0, 0)),
            jax.ShapeDtypeStruct(shape, BF),
            "leave",
        )(place.spots, *self.blocks, self.other, *self.got)
        self.got.append(place.across_step(sent, step))
        return sent

    def latest(self):
        return self.got[-1]

    def last(self, *earlier):
        place = self.place
        self.got[-1] = after(self.got[-1], *earlier)
        chips, core = place.chips, place.core_at
        specs, ins = [], []
        for k in range(chips):
            up = place.up_at + k
            for b in self.blocks:
                ins.append(b)
                specs.append(
                    pl.BlockSpec(
                        (1, 1, 1) + b.shape[3:],
                        lambda i, s, up=up: (s[0], s[up], s[core], 0, 0),
                    )
                )
            for n, g in enumerate([self.other] + self.got):
                ins.append(g)
                specs.append(
                    pl.BlockSpec(
                        (1, 1, self.rows, self.cols),
                        lambda i, s, up=up, n=n: (s[0] if n == 0 else 0, s[up], 0, 0),
                    )
                )
        own, *sent = self.call(
            functools.partial(last_kernel, len(self.blocks), len(ins) // chips, chips),
            (1,),
            specs,
            [pl.BlockSpec((self.rows, self.cols), lambda i, s: (0, 0))] * chips,
            [
                jax.ShapeDtypeStruct((self.rows, self.cols), F32 if k == 0 else BF)
                for k in range(chips)
            ],
            "last",
        )(place.spots, *ins)
        self.own = own
        self.came = [place.along_chips(v, k + 1) for k, v in enumerate(sent)]
        return own

    def result(self, parts, *earlier):
        self.came = after(self.came, *earlier)
        return cut_sum([self.own] + self.came, parts)


def line_kernel(n, each, chips, spots_ref, *refs):
    outs = refs[2 * chips * each :]
    for k in range(chips):
        for i in range(2):
            at = (2 * k + i) * each
            value = sum_refs(refs[at : at + each], n)
            outs[k][i] = value.astype(outs[k].dtype).reshape(outs[k].shape[1:])


def turn_kernel(own_ref, *refs):
    *came, keep_ref, send_ref = refs
    total = own_ref[...]
    for c in came:
        total = total + c[...].astype(F32)
    keep_ref[...] = total[0]
    send_ref[...] = total[1].astype(BF)


class ReduceHopLast(Reduce):
    def line(self, *earlier):
        place = self.place
        self.got[-1] = after(self.got[-1], *earlier)
        chips, core = place.chips, place.core_at
        specs, ins = [], []
        for k in range(chips):
            up = place.up_at + k
            for i in range(2):
                for b in self.blocks:
                    ins.append(b)
                    specs.append(
                        pl.BlockSpec(
                            (1, 1, 1) + b.shape[3:],
                            lambda _, s, up=up, i=i: (s[2 * i], s[up], s[core], 0, 0),
                        )
                    )
                ins.append(self.other)
                specs.append(
                    pl.BlockSpec(
                        (1, 1, self.rows, self.cols),
                        lambda _, s, up=up, i=i: (s[2 * i], s[up], 0, 0),
                    )
                )
                ins.append(self.got[0])
                specs.append(
                    pl.BlockSpec(
                        (1, 1, self.rows, self.cols),
                        lambda _, s, up=up, i=i: (i, s[up], 0, 0),
                    )
                )
        shape = (2, self.rows, self.cols)
        own, *sent = self.call(
            functools.partial(line_kernel, len(self.blocks), len(ins) // chips // 2, chips),
            (1,),
            specs,
            [pl.BlockSpec(shape, lambda _, s: (0, 0, 0))] * chips,
            [jax.ShapeDtypeStruct(shape, F32 if k == 0 else BF) for k in range(chips)],
            "line",
        )(place.spots, *ins)
        self.own = own
        self.came = [place.along_chips(v, k + 1) for k, v in enumerate(sent)]
        return own

    def turn(self, *earlier):
        came = after(self.came, *earlier)
        shape = (self.rows, self.cols)
        self.own, sent = pl.pallas_call(
            turn_kernel,
            out_shape=[jax.ShapeDtypeStruct(shape, F32), jax.ShapeDtypeStruct(shape, BF)],
            compiler_params=pltpu.CompilerParams(vmem_limit_bytes=8 << 20),
            cost_estimate=QUICK,
            name="turn",
        )(self.own, *came)
        self.came = [self.place.across_step(sent, 1)]
        return sent


def owner_blocks(place, gradient):
    rows = gradient.shape[0] // (place.dp_count * place.inner)
    return gradient.reshape(
        place.dp_count, place.chips, 2, rows, gradient.shape[-1]
    )


class PlainReduce:
    def __init__(self, place, blocks):
        devices = place.dp_count * place.inner
        flat = [b.reshape((devices,) + b.shape[3:]) for b in blocks]
        self.sum = lax.psum_scatter(
            jnp.concatenate(flat, axis=1), AXES, scatter_dimension=0, tiled=False
        )
        self.sent = self.sum

    def leave(self, step, *earlier):
        return self.sum

    def last(self, *earlier):
        return self.sum

    def latest(self):
        return self.sum

    def line(self, *earlier):
        return self.sum

    def turn(self, *earlier):
        return self.sum

    def result(self, parts, *earlier):
        total = self.sum.astype(F32)
        return [
            total[r : r + int(np.prod(s[:-1])), c : c + s[-1]].reshape(s)
            for s, r, c in parts
        ]


def dot_nt(a, b):
    return lax.dot_general(a, b, (((1,), (1,)), ((), ())), preferred_element_type=F32)


def dot_nn(a, b):
    return jnp.dot(a, b, preferred_element_type=F32)


def dot_tn(a, b):
    return lax.dot_general(a, b, (((0,), (0,)), ((), ())), preferred_element_type=F32)


def head(h):
    return slice(h * HD, (h + 1) * HD)


def attend_kernel(
    masked, start_ref, length_ref, q_ref, k_ref, v_ref, o_ref, p_ref, scores_ref
):
    rows = q_ref.shape[0]
    keys = k_ref.shape[0]
    if masked:
        seq = pl.program_id(0)
        start = start_ref[seq]
        stop = start + length_ref[seq]
        key_at = lax.broadcasted_iota(jnp.int32, (keys, rows), 0)
        row_at = lax.broadcasted_iota(jnp.int32, (keys, rows), 1)
        inside = (key_at >= start) & (key_at < stop) & (row_at >= start) & (row_at < stop)
        hidden = jnp.where((key_at <= row_at) | inside, 0.0, BIG_NEGATIVE).astype(F32)
    for h in range(H):
        scores_ref[h] = dot_nt(k_ref[:, head(h)], q_ref[:, head(h)])
    for h in range(H):
        scores = scores_ref[h]
        if masked:
            scores = scores + hidden
        peak = jnp.max(scores, axis=0, keepdims=True)
        weights = jnp.exp(scores - peak)
        total = jnp.sum(weights, axis=0, keepdims=True)
        p_ref[0, h] = (weights * (1.0 / total)).astype(BF)
    values_t = v_ref[...].T
    pieces = [dot_nn(values_t[head(h)], p_ref[0, h]) for h in range(H)]
    o_ref[...] = jnp.concatenate(pieces, axis=0).T.astype(BF)


def attend(queries, keys, values, start, length, masked, count):
    rows = queries.shape[0] // count
    key_rows = keys.shape[0] // count
    block = lambda n: pl.BlockSpec((n, D), lambda s, *_: (s, 0))
    return pl.pallas_call(
        functools.partial(attend_kernel, masked),
        grid_spec=pltpu.PrefetchScalarGridSpec(
            num_scalar_prefetch=2,
            grid=(count,),
            in_specs=[block(rows), block(key_rows), block(key_rows)],
            out_specs=[
                block(rows),
                pl.BlockSpec((1, H, key_rows, rows), lambda s, *_: (s, 0, 0, 0)),
            ],
            scratch_shapes=[pltpu.VMEM((H, key_rows, rows), F32)],
        ),
        out_shape=[
            jax.ShapeDtypeStruct(queries.shape, BF),
            jax.ShapeDtypeStruct((count, H, key_rows, rows), BF),
        ],
        compiler_params=pltpu.CompilerParams(vmem_limit_bytes=14 << 20),
        cost_estimate=QUICK,
        name="attend",
    )(start, length, queries, keys, values)


def norm_parts(summed):
    centre = summed - jnp.mean(summed, axis=-1, keepdims=True)
    scale = lax.rsqrt(jnp.mean(centre * centre, axis=-1, keepdims=True) + EPS)
    return centre * scale, scale


def row_sum(value):
    return jnp.sum(value.astype(F32), axis=0, keepdims=True)


def norm_back_sums(summed, gain, grad):
    normal, scale = norm_parts(summed)
    inner = grad * gain
    back = scale * (
        inner
        - jnp.mean(inner, axis=-1, keepdims=True)
        - normal * jnp.mean(inner * normal, axis=-1, keepdims=True)
    )
    return back, [row_sum(grad * normal), row_sum(grad)]


def put_rows(ref, rows):
    for i, r in enumerate(rows):
        ref[i : i + 1] = r


def hidden_back_kernel(df_ref, c_ref, slope_ref, du_ref, sum_ref):
    du = (dot_nt(df_ref[...], c_ref[...]) * slope_ref[...].astype(F32)).astype(BF)
    du_ref[...] = du
    sum_ref[...] = row_sum(du)


def hidden_back(df, contract, slope):
    tokens = df.shape[0]
    return pl.pallas_call(
        hidden_back_kernel,
        grid=(FF // D,),
        in_specs=[
            pl.BlockSpec((tokens, D), lambda j: (0, 0)),
            pl.BlockSpec((D, D), lambda j: (j, 0)),
            pl.BlockSpec((tokens, D), lambda j: (0, j)),
        ],
        out_specs=[
            pl.BlockSpec((tokens, D), lambda j: (0, j)),
            pl.BlockSpec((1, D), lambda j: (0, j)),
        ],
        out_shape=[
            jax.ShapeDtypeStruct((tokens, FF), BF),
            jax.ShapeDtypeStruct((1, FF), F32),
        ],
        compiler_params=pltpu.CompilerParams(vmem_limit_bytes=16 << 20),
        cost_estimate=LONG,
        name="hidden_back",
    )(df, contract, slope)


def expand_back_kernel(
    x_ref, du_ref, e_ref, dr3_ref, r2_ref, gain_ref, de_ref, dr2_ref, dc_ref, sum_ref, xt_ref
):
    j = pl.program_id(0)

    @pl.when(j == 0)
    def _():
        xt_ref[...] = x_ref[...].T
        dr2_ref[...] = dr3_ref[...]

    du = du_ref[...]
    de_ref[...] = dot_nn(xt_ref[...], du).astype(BF)
    dr2_ref[...] += dot_nt(du, e_ref[...])

    @pl.when(j == pl.num_programs(0) - 1)
    def _():
        back, sums = norm_back_sums(r2_ref[...], gain_ref[...], dr2_ref[...])
        dc = back.astype(BF)
        dr2_ref[...] = back
        dc_ref[...] = dc
        put_rows(sum_ref, sums + [row_sum(dc)])


def expand_back(x2b, du, expand, dr3, r2, gain):
    tokens = x2b.shape[0]
    still = pl.BlockSpec((tokens, D), lambda j: (0, 0))
    moving = lambda n: pl.BlockSpec((n, D), lambda j: (0, j))
    return pl.pallas_call(
        expand_back_kernel,
        grid=(FF // D,),
        in_specs=[
            still,
            moving(tokens),
            moving(D),
            still,
            still,
            pl.BlockSpec((1, D), lambda j: (0, 0)),
        ],
        out_specs=[moving(D), still, still, pl.BlockSpec((8, D), lambda j: (0, 0))],
        out_shape=[
            jax.ShapeDtypeStruct((D, FF), BF),
            jax.ShapeDtypeStruct((tokens, D), F32),
            jax.ShapeDtypeStruct((tokens, D), BF),
            jax.ShapeDtypeStruct((8, D), F32),
        ],
        scratch_shapes=[pltpu.VMEM((D, tokens), BF)],
        compiler_params=pltpu.CompilerParams(vmem_limit_bytes=24 << 20),
        cost_estimate=LONG,
        name="expand_back",
    )(x2b, du, expand, dr3, r2, gain)


def heads_back(count, q_ref, k_ref, v_ref, p_ref, g_ref, outs, moved_ref, ds_ref):
    rows = q_ref.shape[0] // count
    keys = k_ref.shape[0] // count
    for s in range(count):
        at = slice(s * rows, (s + 1) * rows)
        key_at = slice(s * keys, (s + 1) * keys)
        for h in range(H):
            moved_ref[h] = dot_nt(v_ref[key_at, head(h)], g_ref[at, head(h)])
        for h in range(H):
            weights = p_ref[s, h].astype(F32)
            moved = moved_ref[h]
            centre = jnp.sum(weights * moved, axis=0, keepdims=True)
            ds_ref[h] = (weights * (moved - centre)).astype(BF)
        keys_t = k_ref[key_at].T
        dq, dk, dv = [], [], []
        for h in range(H):
            dk.append(dot_nn(ds_ref[h], q_ref[at, head(h)]))
            dv.append(dot_nn(p_ref[s, h], g_ref[at, head(h)]))
            dq.append(dot_nn(keys_t[head(h)], ds_ref[h]))
        outs[0][at] = (jnp.concatenate(dq, axis=0).T.astype(BF) * 0.125).astype(BF)
        outs[1][key_at] = jnp.concatenate(dk, axis=1).astype(BF)
        outs[2][key_at] = jnp.concatenate(dv, axis=1).astype(BF)


def cross_back_kernel(
    count,
    dc_ref,
    co_ref,
    cq_ref,
    q_ref,
    k_ref,
    v_ref,
    p_ref,
    o_ref,
    x_ref,
    m_ref,
    dr2_ref,
    r1_ref,
    gain_ref,
    os_ref,
    dwq_ref,
    dwk_ref,
    dwv_ref,
    dwo_ref,
    dso_ref,
    dk_ref,
    dv_ref,
    dr1_ref,
    da_ref,
    sum_ref,
    g_ref,
    dq_ref,
    moved_ref,
    ds_ref,
):
    dc = dc_ref[...]
    g_ref[...] = dot_nt(dc, co_ref[...]).astype(BF)
    dwo_ref[...] = dot_tn(o_ref[...], dc).astype(BF)
    heads_back(
        count, q_ref, k_ref, v_ref, p_ref, g_ref, (dq_ref, dk_ref, dv_ref), moved_ref, ds_ref
    )
    dq = dq_ref[...]
    dr1 = dr2_ref[...] + dot_nt(dq, cq_ref[...])
    dwq_ref[...] = dot_tn(x_ref[...], dq).astype(BF)
    mt = m_ref[...].T
    dwk_ref[...] = dot_nn(mt, dk_ref[...]).astype(BF)
    dwv_ref[...] = dot_nn(mt, dv_ref[...]).astype(BF)
    back, sums = norm_back_sums(r1_ref[...], gain_ref[...], dr1)
    da = back.astype(BF)
    dr1_ref[...] = back
    da_ref[...] = da
    dso_ref[...] = dot_tn(os_ref[...], da).astype(BF)
    put_rows(sum_ref, sums + [row_sum(da), row_sum(dq), row_sum(dv_ref[...])])


def cross_back(dc, co, cq, q2, k2, v2, p2, o2, x1b, memory, dr2, r1, gain, o, count):
    tokens, rows = dc.shape[0], dc.shape[0] // count
    keys = memory.shape[0] // count
    square = jax.ShapeDtypeStruct((D, D), BF)
    low = jax.ShapeDtypeStruct((tokens, D), BF)
    return pl.pallas_call(
        functools.partial(cross_back_kernel, count),
        out_shape=[square] * 5
        + [
            jax.ShapeDtypeStruct(memory.shape, BF),
            jax.ShapeDtypeStruct(memory.shape, BF),
            jax.ShapeDtypeStruct((tokens, D), F32),
            low,
            jax.ShapeDtypeStruct((8, D), F32),
        ],
        scratch_shapes=[
            pltpu.VMEM((tokens, D), BF),
            pltpu.VMEM((tokens, D), BF),
            pltpu.VMEM((H, keys, rows), F32),
            pltpu.VMEM((H, keys, rows), BF),
        ],
        compiler_params=pltpu.CompilerParams(vmem_limit_bytes=18 << 20),
        cost_estimate=LONG,
        name="cross_back",
    )(dc, co, cq, q2, k2, v2, p2, o2, x1b, memory, dr2, r1, gain, o)


def self_back_kernel(
    count,
    da_ref,
    wo_ref,
    q_ref,
    k_ref,
    v_ref,
    p_ref,
    x_ref,
    dwq_ref,
    dwk_ref,
    dwv_ref,
    dq_ref,
    dk_ref,
    dv_ref,
    sum_ref,
    g_ref,
    moved_ref,
    ds_ref,
):
    g_ref[...] = dot_nt(da_ref[...], wo_ref[...]).astype(BF)
    heads_back(
        count, q_ref, k_ref, v_ref, p_ref, g_ref, (dq_ref, dk_ref, dv_ref), moved_ref, ds_ref
    )
    xt = x_ref[...].T
    dwq_ref[...] = dot_nn(xt, dq_ref[...]).astype(BF)
    dwk_ref[...] = dot_nn(xt, dk_ref[...]).astype(BF)
    dwv_ref[...] = dot_nn(xt, dv_ref[...]).astype(BF)
    put_rows(sum_ref, [row_sum(dq_ref[...]), row_sum(dv_ref[...])])


def self_back(da, wo, q, k, v, p, x, count):
    tokens, rows = da.shape[0], da.shape[0] // count
    square = jax.ShapeDtypeStruct((D, D), BF)
    low = jax.ShapeDtypeStruct((tokens, D), BF)
    return pl.pallas_call(
        functools.partial(self_back_kernel, count),
        out_shape=[square] * 3 + [low] * 3 + [jax.ShapeDtypeStruct((8, D), F32)],
        scratch_shapes=[
            pltpu.VMEM((tokens, D), BF),
            pltpu.VMEM((H, rows, rows), F32),
            pltpu.VMEM((H, rows, rows), BF),
        ],
        compiler_params=pltpu.CompilerParams(vmem_limit_bytes=14 << 20),
        cost_estimate=LONG,
        name="self_back",
    )(da, wo, q, k, v, p, x)


def inputs_back_kernel(
    dq_ref, dk_ref, dv_ref, wq_ref, wk_ref, wv_ref, dr1_ref, dk2_ref, dv2_ref, ck_ref, cv_ref, dx_ref, de_ref
):
    de_ref[...] = dot_nt(dk2_ref[...], ck_ref[...]) + dot_nt(dv2_ref[...], cv_ref[...])
    dx_ref[...] = (
        dr1_ref[...]
        + dot_nt(dq_ref[...], wq_ref[...])
        + dot_nt(dk_ref[...], wk_ref[...])
        + dot_nt(dv_ref[...], wv_ref[...])
    )


def inputs_back(dq, dk, dv, wq, wk, wv, dr1, dk2, dv2, ck, cv):
    return pl.pallas_call(
        inputs_back_kernel,
        out_shape=[
            jax.ShapeDtypeStruct(dr1.shape, F32),
            jax.ShapeDtypeStruct(dk2.shape, F32),
        ],
        compiler_params=pltpu.CompilerParams(vmem_limit_bytes=10 << 20),
        cost_estimate=LONG,
        name="inputs_back",
    )(dq, dk, dv, wq, wk, wv, dr1, dk2, dv2, ck, cv)


def norm(summed):
    centre = summed - jnp.mean(summed, axis=-1, keepdims=True)
    scale = lax.rsqrt(jnp.mean(centre * centre, axis=-1, keepdims=True) + EPS)
    return centre * scale, scale


def norm_back(normal, scale, gain, grad):
    inner = grad * gain
    back = scale * (
        inner
        - jnp.mean(inner, axis=-1, keepdims=True)
        - normal * jnp.mean(inner * normal, axis=-1, keepdims=True)
    )
    return back, jnp.sum(grad * normal, axis=0), jnp.sum(grad, axis=0)


def column_sum(value):
    return jnp.sum(value.astype(F32), axis=0)


def gelu_and_slope(value):
    spread = 0.5 * (1.0 + lax.erf(value * np.float32(np.sqrt(0.5))))
    density = jnp.exp(-0.5 * value * value) * np.float32(1.0 / np.sqrt(2.0 * np.pi))
    return value * spread, spread + value * density


def pack_kernel(sp_ref, so_ref, ab_ref, eb_ref, cb_ref, ng_ref, ns_ref, out_ref):
    rows, n = so_ref.shape[0], ab_ref.shape[1]
    for i in range(3):
        out_ref[i * rows : (i + 1) * rows] = sp_ref[i]
    out_ref[3 * rows : 4 * rows] = so_ref[...]

    def padded(v, width):
        v = v.astype(F32)
        if v.shape[0] < 8:
            v = jnp.concatenate([v, jnp.zeros((8 - v.shape[0], v.shape[1]), F32)])
        return jnp.concatenate([v, jnp.zeros((8, width - v.shape[1]), F32)], axis=1)

    first = jnp.concatenate([ab_ref[...].astype(F32), cb_ref[...].astype(F32)])
    second = jnp.concatenate([ng_ref[...].astype(F32), ns_ref[...].astype(F32)])
    out_ref[4 * rows :] = jnp.concatenate(
        [padded(first, 128), padded(second, 128), padded(eb_ref[...], D - 256)], axis=1
    ).astype(BF)


def pack_self(sp, so, ab, eb, cb, ng, ns):
    ins = [sp, so, ab, eb.reshape(1, -1), cb.reshape(1, -1), ng, ns]
    ins = [pltpu.with_memory_space_constraint(a, pltpu.HBM) for a in ins]
    return pl.pallas_call(
        pack_kernel,
        grid=(1,),
        in_specs=[
            pl.BlockSpec(a.shape, lambda i, n=a.ndim: (0,) * n) for a in ins
        ],
        out_specs=pl.BlockSpec((4 * so.shape[0] + 8, D), lambda i: (0, 0)),
        out_shape=jax.ShapeDtypeStruct((4 * so.shape[0] + 8, D), BF),
        compiler_params=pltpu.CompilerParams(vmem_limit_bytes=4 << 20),
        cost_estimate=QUICK,
        name="pack_self",
    )(*ins)


def pack_small(ab, eb, cb, ng, ns):
    n, wide = cb.shape[0], eb.shape[0]
    return jnp.concatenate(
        [
            jnp.pad(jnp.concatenate([ab, cb[None]]), ((0, 1), (0, 128 - n))),
            jnp.pad(jnp.concatenate([ng, ns]), ((0, 2), (0, 128 - n))),
            jnp.pad(eb[None], ((0, 7), (0, D - 256 - wide))),
        ],
        axis=1,
    )


def unpack_small_kernel(n, wide, in_ref, rows_ref, eb_ref):
    for d in range(in_ref.shape[0]):
        block = in_ref[d].astype(F32)
        rows_ref[0:8, d * n : (d + 1) * n] = block[:, 0:n]
        rows_ref[8:16, d * n : (d + 1) * n] = block[:, 128 : 128 + n]
        eb_ref[:, d * wide : (d + 1) * wide] = block[0:1, 256 : 256 + wide]


def unpack_small(gathered, n, wide):
    devices = gathered.shape[0]
    return pl.pallas_call(
        functools.partial(unpack_small_kernel, n, wide),
        out_shape=[
            jax.ShapeDtypeStruct((16, devices * n), F32),
            jax.ShapeDtypeStruct((1, devices * wide), F32),
        ],
        compiler_params=pltpu.CompilerParams(vmem_limit_bytes=8 << 20),
        cost_estimate=QUICK,
        name="unpack_small",
    )(gathered)


def split_small_kernel(n, wide, ff_ref, cross_ref, self_ref, db_ref, g3_ref, s3_ref, eb_ref, out_ref):
    zero = jnp.zeros((1, D), F32)
    first = jnp.concatenate(
        [
            self_ref[0:2],
            cross_ref[2:5],
            ff_ref[2:3],
            db_ref[...].reshape(1, D),
            zero,
        ],
        axis=0,
    )
    second = jnp.concatenate(
        [
            cross_ref[0:1],
            ff_ref[0:1],
            g3_ref[...].reshape(1, D),
            cross_ref[1:2],
            ff_ref[1:2],
            s3_ref[...].reshape(1, D),
            zero,
            zero,
        ],
        axis=0,
    )
    tail = jnp.broadcast_to(eb_ref[...], (8, FF))

    def padded(v, width):
        return jnp.concatenate([v, jnp.zeros((8, width - v.shape[1]), F32)], axis=1)

    for d in range(out_ref.shape[0]):
        out_ref[d] = jnp.concatenate(
            [
                padded(first[:, d * n : (d + 1) * n], 128),
                padded(second[:, d * n : (d + 1) * n], 128),
                padded(tail[:, d * wide : (d + 1) * wide], D - 256),
            ],
            axis=1,
        ).astype(BF)


def split_small(ff_sums, cross_sums, self_sums, vectors, eb, n, wide):
    devices = D // n
    return pl.pallas_call(
        functools.partial(split_small_kernel, n, wide),
        out_shape=jax.ShapeDtypeStruct((devices, 8, D), BF),
        compiler_params=pltpu.CompilerParams(vmem_limit_bytes=8 << 20),
        cost_estimate=QUICK,
        name="split_small",
    )(ff_sums, cross_sums, self_sums, *vectors, eb)


def body(
    layer_input,
    encoder_states,
    output_grad,
    span_start,
    span_length,
    self_project,
    self_output,
    cross_project,
    cross_output,
    attend_bias,
    expand_weight,
    expand_bias,
    contract_weight,
    contract_bias,
    norm_gain,
    norm_shift,
):
    place = Place()
    count, length = layer_input.shape[:2]
    shape = layer_input.shape
    rows = self_output.shape[0]
    wide = expand_bias.shape[0]
    fits = rows % 8 == 0 and place.bits == 2
    reduce = Reduce if fits else PlainReduce
    reduce_hop_last = ReduceHopLast if fits else PlainReduce
    x = layer_input.reshape(-1, D)
    memory = encoder_states.reshape(-1, D)
    grad_out = output_grad.reshape(-1, D).astype(F32)

    local_cross = jnp.concatenate([cross_project.reshape(-1, D), cross_output])
    four = [(i * rows, rows) for i in range(4)]
    if fits:
        g_self = Gather(
            place,
            pack_self(
                self_project,
                self_output,
                attend_bias,
                expand_bias,
                contract_bias,
                norm_gain,
                norm_shift,
            ),
        )
        line = g_self.column()
        g_self.hop(0, 0)
        g_self.hop(1, 0)
        g_cross = Gather(place, after(local_cross, line))
        g_self.blocks, g_cross.got = lax.optimization_barrier((g_self.blocks, g_cross.got))
        g_self.hop(1, 1)
        line = g_cross.column()
        g_cross.hop(0, 0)
        g_cross.hop(1, 0)
        g_expand = Gather(place, after(expand_weight, line))
        g_self.blocks, g_cross.blocks, g_expand.got = lax.optimization_barrier(
            (g_self.blocks, g_cross.blocks, g_expand.got)
        )
        g_cross.hop(1, 1)
        line = g_expand.column()
        g_expand.hop(0, 0)
        g_expand.hop(1, 0)
        g_contract = Gather(place, after(contract_weight, line))
        g_self.half(line)
        *w_self, smalls = g_self.spread(four + [(4 * rows, 8)])
        smalls = smalls.reshape(-1, 8, D)
    else:
        whole = lax.all_gather(
            jnp.concatenate(
                [
                    self_project.reshape(-1, D),
                    self_output,
                    pack_small(
                        attend_bias, expand_bias, contract_bias, norm_gain, norm_shift
                    ),
                    local_cross,
                    contract_weight,
                ]
            ),
            AXES,
            axis=0,
        )
        squares = [
            whole[:, a : a + rows].reshape(D, D)
            for a in [i * rows for i in range(4)]
            + [4 * rows + 8 + i * rows for i in range(4)]
        ]
        w_self, w_cross = squares[:4], squares[4:]
        contract = whole[:, 8 * rows + 8 :].reshape(FF, D)
        smalls = whole[:, 4 * rows : 4 * rows + 8]
        expand = lax.all_gather(expand_weight, AXES, axis=0, tiled=True)
    wq, wk, wv, wo = w_self
    small_rows, expand_b = unpack_small(smalls, rows, wide)
    biases = [small_rows[i : i + 1] for i in range(6)]
    contract_b = small_rows[6:7]
    gains = [small_rows[8 + i : 9 + i] for i in range(3)]
    shifts = [small_rows[11 + i : 12 + i] for i in range(3)]

    q = ((dot_nn(x, wq) + biases[0]) * 0.125).astype(BF)
    k = dot_nn(x, wk).astype(BF)
    v = (dot_nn(x, wv) + biases[1]).astype(BF)
    o, p = attend(q, k, v, span_start, span_length, True, count)
    if fits:
        g_cross.blocks, g_expand.blocks, g_contract.got, o = lax.optimization_barrier(
            (g_cross.blocks, g_expand.blocks, g_contract.got, o)
        )
        g_expand.hop(1, 1)
        line = g_contract.column()
        g_contract.hop(0, 0)
        g_contract.hop(1, 0)
        g_cross.half(line)
        w_cross = g_cross.spread(four)
    r1 = x.astype(F32) + (dot_nn(o, wo) + biases[2])
    n1, s1 = norm(r1)
    x1 = n1 * gains[0] + shifts[0]
    x1b = x1.astype(BF)
    cq, ck, cv, co = w_cross
    q2 = ((dot_nn(x1b, cq) + biases[3]) * 0.125).astype(BF)
    k2 = dot_nn(memory, ck).astype(BF)
    v2 = (dot_nn(memory, cv) + biases[4]).astype(BF)
    o2, p2 = attend(q2, k2, v2, span_start, span_length, False, count)
    if fits:
        g_expand.blocks, g_contract.blocks, o2 = lax.optimization_barrier(
            (g_expand.blocks, g_contract.blocks, o2)
        )
        g_contract.hop(1, 1)
        g_expand.half()
        (expand,) = g_expand.spread([(0, rows)])
    r2 = x1 + (dot_nn(o2, co) + biases[5])
    n2, s2 = norm(r2)
    x2 = n2 * gains[1] + shifts[1]
    x2b = x2.astype(BF)
    act, slope = gelu_and_slope(dot_nn(x2b, expand) + expand_b)
    act = act.astype(BF)
    slope = slope.astype(BF)
    if fits:
        g_contract.blocks[3] = after(g_contract.blocks[3], act)
        (contract,) = g_contract.spread([(0, 4 * rows)])
    n3, s3 = norm(x2 + (dot_nn(act, contract) + contract_b))
    output = (n3 * gains[2] + shifts[2]).astype(BF)

    dr3, gain3, shift3 = norm_back(n3, s3, gains[2], grad_out)
    df = dr3.astype(BF)
    d_contract = dot_tn(act, df).astype(BF)
    r_contract = reduce_hop_last(place, [owner_blocks(place, d_contract)])
    d_contract_b = column_sum(df)
    du, d_expand_b = hidden_back(after(df, d_contract), contract, slope)
    sent = r_contract.leave(0, du)
    d_expand, dr2, dc, ff_sums = expand_back(
        x2b, after(du, sent), expand, dr3, r2, gains[1]
    )
    sent = r_contract.line(dc)
    r_expand = reduce(place, [owner_blocks(place, after(d_expand, sent))])
    sent = r_expand.leave(0, dc)
    *d_cross, dk2, dv2, dr1, da, cross_sums = cross_back(
        after(dc, sent), co, cq, q2, k2, v2, p2, o2, x1b, memory, dr2, r1, gains[0], o, count
    )
    r_cross = reduce(place, [owner_blocks(place, d) for d in d_cross])
    *d_self, dq, dk, dv, self_sums = self_back(
        after(da, r_cross.sent), wo, q, k, v, p, x, count
    )
    sent = r_expand.leave(1, self_sums)
    sent = r_cross.leave(0, sent)
    small_blocks = split_small(
        ff_sums,
        cross_sums,
        self_sums,
        [d_contract_b, gain3, shift3],
        d_expand_b,
        rows,
        wide,
    )
    small_blocks = small_blocks.reshape(place.dp_count, place.chips, 2, 8, D)
    r_self = reduce(
        place,
        [owner_blocks(place, d) for d in after(d_self, sent)] + [small_blocks],
    )
    sent = r_contract.turn(r_self.sent)
    dq, dk, dv, dk2, dv2 = after((dq, dk, dv, dk2, dv2), sent)
    input_grad, encoder_grad = inputs_back(
        dq, dk, dv, wq, wk, wv, dr1, dk2, dv2, ck, cv
    )
    (own_contract,) = r_contract.result([((4 * rows, D), 0, 0)], input_grad)
    sent = r_expand.last(own_contract)
    sent = r_cross.leave(1, fence(place, sent))
    (own_expand,) = r_expand.result([((rows, FF), 0, 0)], sent)
    fence(place, own_expand)
    sent = r_self.leave(0, r_cross.latest())
    sent = r_cross.last(sent)
    sent = r_self.leave(1, fence(place, sent))
    projects = ((3, rows, D), 0, 0)
    square = (rows, D)
    own_cross = r_cross.result(
        [projects, (square, 3 * rows, 0), (square, 4 * rows, 0)], sent
    )
    r_self.last(fence(place, own_cross[0]))
    at = 3 * rows
    own_self = r_self.result(
        [
            projects,
            ((6, rows), at, 0),
            ((1, wide), at, 256),
            ((1, rows), at + 6, 0),
            ((3, rows), at, 128),
            ((3, rows), at + 3, 128),
        ]
    )
    own_self = [own_self[0], own_cross[2], *own_self[1:]]
    return (
        output.reshape(shape),
        input_grad.reshape(shape),
        encoder_grad.reshape(encoder_states.shape),
        own_self[0],
        own_self[1],
        own_cross[0],
        own_cross[1],
        own_self[2],
        own_expand,
        own_self[3].reshape(-1),
        own_contract,
        own_self[4].reshape(-1),
        own_self[5],
        own_self[6],
    )


def solution(mesh):
    rows = P(AXES)
    return jax.shard_map(
        body,
        mesh=mesh,
        in_specs=(
            P(AXES, None, None),
            P(AXES, None, None),
            P(AXES, None, None),
            P(AXES),
            P(AXES),
            P(None, AXES, None),
            P(AXES, None),
            P(None, AXES, None),
            P(AXES, None),
            P(None, AXES),
            P(AXES, None),
            P(AXES),
            P(AXES, None),
            P(AXES),
            P(None, AXES),
            P(None, AXES),
        ),
        out_specs=(
            P(AXES, None, None),
            P(AXES, None, None),
            P(AXES, None, None),
            P(None, AXES, None),
            P(AXES, None),
            P(None, AXES, None),
            P(AXES, None),
            P(None, AXES),
            P(AXES, None),
            P(AXES),
            P(AXES, None),
            P(AXES),
            P(None, AXES),
            P(None, AXES),
        ),
        check_vma=False,
    )
```

```python
import functools

import jax
import jax.numpy as jnp
import numpy as np
from jax import lax
from jax.experimental import pallas as pl
from jax.experimental.pallas import tpu as pltpu
from jax.sharding import PartitionSpec as P

D = 768
H = 12
HD = 64
FF = 3072
AXES = ("dp", "fsdp")

EPS = 1e-05
BIG_NEGATIVE = -1000000000.0
BF = jnp.bfloat16
F32 = jnp.float32
QUICK = pl.CostEstimate(flops=1000, bytes_accessed=1000, transcendentals=0)
LONG = pl.CostEstimate(flops=4 * 10**10, bytes_accessed=10**6, transcendentals=0)


class Place:
    def __init__(self):
        self.dp_count = lax.axis_size("dp")
        self.inner = lax.axis_size("fsdp")
        self.chips = self.inner // 2
        self.bits = int(np.log2(self.dp_count))
        self.dp = lax.axis_index("dp")
        inner = lax.axis_index("fsdp")
        self.chip = inner // 2
        self.core = inner % 2
        table = []
        for dp in range(self.dp_count):
            for chip in range(self.chips):
                for core in range(2):
                    table.append(
                        [dp ^ self.mask(core, m) for m in range(self.dp_count)]
                        + [dp ^ self.mask(1 - core, m) for m in range(self.dp_count)]
                        + [(chip + k) % self.chips for k in range(self.chips)]
                        + [(chip - k) % self.chips for k in range(self.chips)]
                        + [core, 1 - core]
                    )
        index = self.dp * self.inner + inner
        self.spots = lax.dynamic_index_in_dim(
            jnp.asarray(np.array(table, np.int32)), index, 0, keepdims=False
        )
        self.theirs_at = self.dp_count
        self.up_at = 2 * self.dp_count
        self.down_at = self.up_at + self.chips
        self.core_at = self.down_at + self.chips

    def bit(self, core, step):
        return 1 << (self.bits - 1 - step if core == 0 else step)

    def mask(self, core, relative):
        return sum(self.bit(core, s) for s in range(self.bits) if relative >> s & 1)

    def permute(self, value, target):
        pairs = []
        for dp in range(self.dp_count):
            for chip in range(self.chips):
                for core in range(2):
                    to = target(dp, chip, core)
                    pairs.append(
                        (
                            dp * self.inner + chip * 2 + core,
                            to[0] * self.inner + to[1] * 2 + to[2],
                        )
                    )
        return lax.ppermute(value, AXES, pairs)

    def across_cores(self, value):
        return self.permute(value, lambda d, z, c: (d, z, 1 - c))

    def across_step(self, value, step):
        return self.permute(value, lambda d, z, c: (d ^ self.bit(c, step), z, c))

    def along_chips(self, value, shift):
        return self.permute(value, lambda d, z, c: (d, (z + shift) % self.chips, c))


def after(values, *earlier):
    return lax.optimization_barrier((values, earlier))[0]


def copy_kernel(plan, n_in, spots_ref, *refs):
    ins, outs, sems = refs[:n_in], refs[n_in:-1], refs[-1]
    copies = []
    for i, (source, source_at, target, target_at) in enumerate(plan):
        copies.append(
            pltpu.make_async_copy(
                ins[source].at[source_at(spots_ref)],
                outs[target].at[target_at(spots_ref)],
                sems.at[i],
            )
        )
    for c in copies:
        c.start()
    for c in copies:
        c.wait()


def copy_call(place, plan, ins, outs, name):
    anywhere = pl.BlockSpec(memory_space=pl.ANY)
    return pl.pallas_call(
        functools.partial(copy_kernel, plan, len(ins)),
        grid_spec=pltpu.PrefetchScalarGridSpec(
            num_scalar_prefetch=1,
            grid=(1,),
            in_specs=[anywhere] * len(ins),
            out_specs=[anywhere] * len(outs),
            scratch_shapes=[pltpu.SemaphoreType.DMA((len(plan),))],
        ),
        out_shape=outs,
        compiler_params=pltpu.CompilerParams(vmem_limit_bytes=1 << 20),
        cost_estimate=QUICK,
        name=name,
    )(place.spots, *ins)


def fence_kernel(in_ref, out_ref):
    for i in range(in_ref.shape[0]):
        out_ref[i] = in_ref[i]


def fence(place, *values):
    spots = place.spots
    scalars = pl.BlockSpec(memory_space=pltpu.SMEM)
    place.spots = pl.pallas_call(
        fence_kernel,
        in_specs=[scalars],
        out_specs=scalars,
        out_shape=jax.ShapeDtypeStruct(spots.shape, spots.dtype),
        compiler_params=pltpu.CompilerParams(vmem_limit_bytes=1 << 20),
        cost_estimate=LONG,
        name="fence",
    )(after(spots, *values))
    return place.spots


class Gather:
    def __init__(self, place, local):
        self.place = place
        self.local = local
        self.got = [local] + [
            place.along_chips(local, k) for k in range(1, place.chips)
        ]

    def column(self, *earlier):
        place = self.place
        self.got = after(self.got, *earlier)
        plan = [
            (
                k,
                lambda s: (slice(None),),
                0,
                lambda s, k=k: (s[place.down_at + k],),
            )
            for k in range(place.chips)
        ]
        shape = jax.ShapeDtypeStruct((place.chips,) + self.local.shape, BF)
        self.blocks = {0: copy_call(place, plan, self.got, [shape], "column")[0]}
        return self.blocks[0]

    def meet(self, later):
        self.blocks, later.got = lax.optimization_barrier((self.blocks, later.got))

    def hop(self, step, held, *earlier):
        self.blocks[held] = after(self.blocks[held], *earlier)
        self.blocks[held | 1 << step] = self.place.across_step(self.blocks[held], step)

    def share(self, held):
        return self.place.across_cores(self.blocks[held])

    def half(self, *earlier):
        place = self.place
        ins = after([self.blocks[m] for m in range(place.dp_count)], *earlier)
        plan = [
            (m, lambda s: (slice(None),), 0, lambda s, m=m: (s[m],))
            for m in range(place.dp_count)
        ]
        shape = jax.ShapeDtypeStruct((place.dp_count,) + ins[0].shape, BF)
        self.own_half = copy_call(place, plan, ins, [shape], "half")[0]
        self.other_half = place.across_cores(self.own_half)
        return self.own_half

    def spread(self, parts, *earlier):
        place = self.place
        cols = self.local.shape[1]
        whole = slice(None)
        if hasattr(self, "other_half"):
            ins = [self.own_half, self.other_half]
            places = [lambda s: (whole,), lambda s: (whole,)]
        else:
            ins = [self.blocks[m] for m in range(place.dp_count)]
            ins += [self.share(m) for m in range(place.dp_count)]
            places = [lambda s, m=m: (s[m],) for m in range(2 * place.dp_count)]
        ins = after(ins, *earlier)
        plan, outs = [], []
        for out, (first, rows) in enumerate(parts):
            outs.append(
                jax.ShapeDtypeStruct((place.dp_count, place.chips, 2, rows, cols), BF)
            )
            for m, where in enumerate(places):
                core = place.core_at + (m >= len(places) // 2)
                lead = (whole,) * (ins[m].ndim - 2)
                plan.append(
                    (
                        m,
                        lambda s, a=first, n=rows, lead=lead: lead + (pl.ds(a, n),),
                        out,
                        lambda s, where=where, core=core: where(s) + (whole, s[core]),
                    )
                )
        full = copy_call(place, plan, ins, outs, "spread")
        return [w.reshape(-1, cols) for w in full]


def side_by_side(refs):
    parts = [r[...].reshape(r.shape[1:2] + r.shape[-2:]) for r in refs]
    return parts[0] if len(parts) == 1 else jnp.concatenate(parts, axis=1)


def exchange_kernel(spots_ref, *refs):
    out = refs[-1]
    out[...] = side_by_side(refs[:-1]).reshape(out.shape)


def sum_refs(refs, n):
    value = side_by_side(refs[:n]).astype(F32)
    for a in refs[n:]:
        value = value + a[...].astype(F32).reshape(value.shape)
    return value


def leave_kernel(n, spots_ref, *refs):
    out = refs[-1]
    out[...] = sum_refs(refs[:-1], n).astype(BF).reshape(out.shape)


def last_kernel(n, each, chips, spots_ref, *refs):
    outs = refs[chips * each :]
    for k in range(chips):
        value = sum_refs(refs[k * each : (k + 1) * each], n)
        outs[k][...] = value.astype(outs[k].dtype).reshape(outs[k].shape)


def cut_kernel(parts, count, *refs):
    total = refs[0][...].astype(F32)
    for r in refs[1:count]:
        total = total + r[...].astype(F32)
    for (shape, row, col), out in zip(parts, refs[count:]):
        piece = total[row : row + int(np.prod(shape[:-1])), col : col + shape[-1]]
        out[...] = piece.reshape(shape)


def cut_sum(terms, parts):
    return pl.pallas_call(
        functools.partial(cut_kernel, parts, len(terms)),
        out_shape=[jax.ShapeDtypeStruct(s, F32) for s, _, _ in parts],
        compiler_params=pltpu.CompilerParams(vmem_limit_bytes=8 << 20),
        cost_estimate=QUICK,
        name="cut_sum",
    )(*terms)


class Reduce:
    def __init__(self, place, blocks):
        self.place = place
        self.blocks = blocks
        self.rows = sum(b.shape[3] for b in blocks)
        self.cols = blocks[0].shape[4]
        shape = (place.dp_count, place.chips, self.rows, self.cols)
        sent = self.call(
            exchange_kernel,
            (place.dp_count,),
            [
                pl.BlockSpec(
                    (1, place.chips, 1) + b.shape[3:],
                    lambda i, s: (i, 0, s[place.core_at + 1], 0, 0),
                )
                for b in blocks
            ],
            pl.BlockSpec((1,) + shape[1:], lambda i, s: (i, 0, 0, 0)),
            jax.ShapeDtypeStruct(shape, BF),
            "exchange",
        )(place.spots, *blocks)
        self.sent = sent
        self.other = place.across_cores(sent)
        self.got = []

    def call(self, kernel, grid, in_specs, out_specs, out_shape, name):
        return pl.pallas_call(
            kernel,
            grid_spec=pltpu.PrefetchScalarGridSpec(
                num_scalar_prefetch=1, grid=grid, in_specs=in_specs, out_specs=out_specs
            ),
            out_shape=out_shape,
            compiler_params=pltpu.CompilerParams(vmem_limit_bytes=24 << 20),
            cost_estimate=QUICK,
            name=name,
        )

    def leave(self, step, *earlier):
        place = self.place
        if step == 0:
            self.other = after(self.other, *earlier)
        else:
            self.got[-1] = after(self.got[-1], *earlier)
        count = 1 << (place.bits - 1 - step)
        chips, core = place.chips, place.core_at

        def spot(i, s):
            return s[(1 << step) + i * (2 << step)]

        shape = (count, chips, self.rows, self.cols)
        specs = [
            pl.BlockSpec(
                (1, chips, 1) + b.shape[3:], lambda i, s: (spot(i, s), 0, s[core], 0, 0)
            )
            for b in self.blocks
        ]
        specs.append(pl.BlockSpec((1,) + shape[1:], lambda i, s: (spot(i, s), 0, 0, 0)))
        for t in range(step):
            specs.append(
                pl.BlockSpec(
                    (1,) + shape[1:],
                    lambda i, s, t=t: ((1 << (step - t - 1)) + i * (1 << (step - t)), 0, 0, 0),
                )
            )
        sent = self.call(
            functools.partial(leave_kernel, len(self.blocks)),
            (count,),
            specs,
            pl.BlockSpec((1,) + shape[1:], lambda i, s: (i, 0, 0, 0)),
            jax.ShapeDtypeStruct(shape, BF),
            "leave",
        )(place.spots, *self.blocks, self.other, *self.got)
        self.got.append(place.across_step(sent, step))
        return sent

    def latest(self):
        return self.got[-1]

    def last(self, *earlier):
        place = self.place
        self.got[-1] = after(self.got[-1], *earlier)
        chips, core = place.chips, place.core_at
        specs, ins = [], []
        for k in range(chips):
            up = place.up_at + k
            for b in self.blocks:
                ins.append(b)
                specs.append(
                    pl.BlockSpec(
                        (1, 1, 1) + b.shape[3:],
                        lambda i, s, up=up: (s[0], s[up], s[core], 0, 0),
                    )
                )
            for n, g in enumerate([self.other] + self.got):
                ins.append(g)
                specs.append(
                    pl.BlockSpec(
                        (1, 1, self.rows, self.cols),
                        lambda i, s, up=up, n=n: (s[0] if n == 0 else 0, s[up], 0, 0),
                    )
                )
        own, *sent = self.call(
            functools.partial(last_kernel, len(self.blocks), len(ins) // chips, chips),
            (1,),
            specs,
            [pl.BlockSpec((self.rows, self.cols), lambda i, s: (0, 0))] * chips,
            [
                jax.ShapeDtypeStruct((self.rows, self.cols), F32 if k == 0 else BF)
                for k in range(chips)
            ],
            "last",
        )(place.spots, *ins)
        self.own = own
        self.came = [place.along_chips(v, k + 1) for k, v in enumerate(sent)]
        return own

    def result(self, parts, *earlier):
        self.came = after(self.came, *earlier)
        return cut_sum([self.own] + self.came, parts)


def line_kernel(n, each, chips, spots_ref, *refs):
    outs = refs[2 * chips * each :]
    for k in range(chips):
        for i in range(2):
            at = (2 * k + i) * each
            value = sum_refs(refs[at : at + each], n)
            outs[k][i] = value.astype(outs[k].dtype).reshape(outs[k].shape[1:])


def turn_kernel(own_ref, *refs):
    *came, keep_ref, send_ref = refs
    total = own_ref[...]
    for c in came:
        total = total + c[...].astype(F32)
    keep_ref[...] = total[0]
    send_ref[...] = total[1].astype(BF)


class ReduceHopLast(Reduce):
    def line(self, *earlier):
        place = self.place
        self.got[-1] = after(self.got[-1], *earlier)
        chips, core = place.chips, place.core_at
        specs, ins = [], []
        for k in range(chips):
            up = place.up_at + k
            for i in range(2):
                for b in self.blocks:
                    ins.append(b)
                    specs.append(
                        pl.BlockSpec(
                            (1, 1, 1) + b.shape[3:],
                            lambda _, s, up=up, i=i: (s[2 * i], s[up], s[core], 0, 0),
                        )
                    )
                ins.append(self.other)
                specs.append(
                    pl.BlockSpec(
                        (1, 1, self.rows, self.cols),
                        lambda _, s, up=up, i=i: (s[2 * i], s[up], 0, 0),
                    )
                )
                ins.append(self.got[0])
                specs.append(
                    pl.BlockSpec(
                        (1, 1, self.rows, self.cols),
                        lambda _, s, up=up, i=i: (i, s[up], 0, 0),
                    )
                )
        shape = (2, self.rows, self.cols)
        own, *sent = self.call(
            functools.partial(line_kernel, len(self.blocks), len(ins) // chips // 2, chips),
            (1,),
            specs,
            [pl.BlockSpec(shape, lambda _, s: (0, 0, 0))] * chips,
            [jax.ShapeDtypeStruct(shape, F32 if k == 0 else BF) for k in range(chips)],
            "line",
        )(place.spots, *ins)
        self.own = own
        self.came = [place.along_chips(v, k + 1) for k, v in enumerate(sent)]
        return own

    def turn(self, *earlier):
        came = after(self.came, *earlier)
        shape = (self.rows, self.cols)
        self.own, sent = pl.pallas_call(
            turn_kernel,
            out_shape=[jax.ShapeDtypeStruct(shape, F32), jax.ShapeDtypeStruct(shape, BF)],
            compiler_params=pltpu.CompilerParams(vmem_limit_bytes=8 << 20),
            cost_estimate=QUICK,
            name="turn",
        )(self.own, *came)
        self.came = [self.place.across_step(sent, 1)]
        return sent


def owner_blocks(place, gradient):
    rows = gradient.shape[0] // (place.dp_count * place.inner)
    return gradient.reshape(
        place.dp_count, place.chips, 2, rows, gradient.shape[-1]
    )


class PlainReduce:
    def __init__(self, place, blocks):
        devices = place.dp_count * place.inner
        flat = [b.reshape((devices,) + b.shape[3:]) for b in blocks]
        self.sum = lax.psum_scatter(
            jnp.concatenate(flat, axis=1), AXES, scatter_dimension=0, tiled=False
        )
        self.sent = self.sum

    def leave(self, step, *earlier):
        return self.sum

    def last(self, *earlier):
        return self.sum

    def latest(self):
        return self.sum

    got = [None]

    def line(self, *earlier):
        return self.sum

    def turn(self, *earlier):
        return self.sum

    def result(self, parts, *earlier):
        total = self.sum.astype(F32)
        return [
            total[r : r + int(np.prod(s[:-1])), c : c + s[-1]].reshape(s)
            for s, r, c in parts
        ]


def dot_nt(a, b):
    return lax.dot_general(a, b, (((1,), (1,)), ((), ())), preferred_element_type=F32)


def dot_nn(a, b):
    return jnp.dot(a, b, preferred_element_type=F32)


def dot_tn(a, b):
    return lax.dot_general(a, b, (((0,), (0,)), ((), ())), preferred_element_type=F32)


def head(h):
    return slice(h * HD, (h + 1) * HD)


def attend_kernel(
    masked, start_ref, length_ref, q_ref, k_ref, v_ref, o_ref, p_ref, scores_ref
):
    rows = q_ref.shape[0]
    keys = k_ref.shape[0]
    if masked:
        seq = pl.program_id(0)
        start = start_ref[seq]
        stop = start + length_ref[seq]
        key_at = lax.broadcasted_iota(jnp.int32, (keys, rows), 0)
        row_at = lax.broadcasted_iota(jnp.int32, (keys, rows), 1)
        inside = (key_at >= start) & (key_at < stop) & (row_at >= start) & (row_at < stop)
        hidden = jnp.where((key_at <= row_at) | inside, 0.0, BIG_NEGATIVE).astype(F32)
    for h in range(H):
        scores_ref[h] = dot_nt(k_ref[:, head(h)], q_ref[:, head(h)])
    for h in range(H):
        scores = scores_ref[h]
        if masked:
            scores = scores + hidden
        peak = jnp.max(scores, axis=0, keepdims=True)
        weights = jnp.exp(scores - peak)
        total = jnp.sum(weights, axis=0, keepdims=True)
        p_ref[0, h] = (weights * (1.0 / total)).astype(BF)
    values_t = v_ref[...].T
    pieces = [dot_nn(values_t[head(h)], p_ref[0, h]) for h in range(H)]
    o_ref[...] = jnp.concatenate(pieces, axis=0).T.astype(BF)


def attend(queries, keys, values, start, length, masked, count):
    rows = queries.shape[0] // count
    key_rows = keys.shape[0] // count
    block = lambda n: pl.BlockSpec((n, D), lambda s, *_: (s, 0))
    return pl.pallas_call(
        functools.partial(attend_kernel, masked),
        grid_spec=pltpu.PrefetchScalarGridSpec(
            num_scalar_prefetch=2,
            grid=(count,),
            in_specs=[block(rows), block(key_rows), block(key_rows)],
            out_specs=[
                block(rows),
                pl.BlockSpec((1, H, key_rows, rows), lambda s, *_: (s, 0, 0, 0)),
            ],
            scratch_shapes=[pltpu.VMEM((H, key_rows, rows), F32)],
        ),
        out_shape=[
            jax.ShapeDtypeStruct(queries.shape, BF),
            jax.ShapeDtypeStruct((count, H, key_rows, rows), BF),
        ],
        compiler_params=pltpu.CompilerParams(vmem_limit_bytes=14 << 20),
        cost_estimate=QUICK,
        name="attend",
    )(start, length, queries, keys, values)


def norm_parts(summed):
    centre = summed - jnp.mean(summed, axis=-1, keepdims=True)
    scale = lax.rsqrt(jnp.mean(centre * centre, axis=-1, keepdims=True) + EPS)
    return centre * scale, scale


def row_sum(value):
    return jnp.sum(value.astype(F32), axis=0, keepdims=True)


def norm_back_sums(summed, gain, grad):
    normal, scale = norm_parts(summed)
    inner = grad * gain
    back = scale * (
        inner
        - jnp.mean(inner, axis=-1, keepdims=True)
        - normal * jnp.mean(inner * normal, axis=-1, keepdims=True)
    )
    return back, [row_sum(grad * normal), row_sum(grad)]


def put_rows(ref, rows):
    for i, r in enumerate(rows):
        ref[i : i + 1] = r


def hidden_back_kernel(df_ref, c_ref, slope_ref, du_ref, sum_ref):
    du = (dot_nt(df_ref[...], c_ref[...]) * slope_ref[...].astype(F32)).astype(BF)
    du_ref[...] = du
    sum_ref[...] = row_sum(du)


def hidden_back(df, contract, slope):
    tokens = df.shape[0]
    return pl.pallas_call(
        hidden_back_kernel,
        grid=(FF // D,),
        in_specs=[
            pl.BlockSpec((tokens, D), lambda j: (0, 0)),
            pl.BlockSpec((D, D), lambda j: (j, 0)),
            pl.BlockSpec((tokens, D), lambda j: (0, j)),
        ],
        out_specs=[
            pl.BlockSpec((tokens, D), lambda j: (0, j)),
            pl.BlockSpec((1, D), lambda j: (0, j)),
        ],
        out_shape=[
            jax.ShapeDtypeStruct((tokens, FF), BF),
            jax.ShapeDtypeStruct((1, FF), F32),
        ],
        compiler_params=pltpu.CompilerParams(vmem_limit_bytes=16 << 20),
        cost_estimate=LONG,
        name="hidden_back",
    )(df, contract, slope)


def expand_back_kernel(
    du_ref, e_ref, dr3_ref, r2_ref, gain_ref, dr2_ref, dc_ref, sum_ref
):
    j = pl.program_id(0)

    @pl.when(j == 0)
    def _():
        dr2_ref[...] = dr3_ref[...]

    dr2_ref[...] += dot_nt(du_ref[...], e_ref[...])

    @pl.when(j == pl.num_programs(0) - 1)
    def _():
        back, sums = norm_back_sums(r2_ref[...], gain_ref[...], dr2_ref[...])
        dc = back.astype(BF)
        dr2_ref[...] = back
        dc_ref[...] = dc
        put_rows(sum_ref, sums + [row_sum(dc)])


def expand_back(du, expand, dr3, r2, gain):
    tokens = du.shape[0]
    still = pl.BlockSpec((tokens, D), lambda j: (0, 0))
    moving = lambda n: pl.BlockSpec((n, D), lambda j: (0, j))
    return pl.pallas_call(
        expand_back_kernel,
        grid=(FF // D,),
        in_specs=[
            moving(tokens),
            moving(D),
            still,
            still,
            pl.BlockSpec((1, D), lambda j: (0, 0)),
        ],
        out_specs=[still, still, pl.BlockSpec((8, D), lambda j: (0, 0))],
        out_shape=[
            jax.ShapeDtypeStruct((tokens, D), F32),
            jax.ShapeDtypeStruct((tokens, D), BF),
            jax.ShapeDtypeStruct((8, D), F32),
        ],
        compiler_params=pltpu.CompilerParams(vmem_limit_bytes=20 << 20),
        cost_estimate=LONG,
        name="expand_back",
    )(du, expand, dr3, r2, gain)


def heads_back(count, q_ref, k_ref, v_ref, p_ref, g_ref, outs, moved_ref, ds_ref):
    rows = q_ref.shape[0] // count
    keys = k_ref.shape[0] // count
    for s in range(count):
        at = slice(s * rows, (s + 1) * rows)
        key_at = slice(s * keys, (s + 1) * keys)
        for h in range(H):
            moved_ref[h] = dot_nt(v_ref[key_at, head(h)], g_ref[at, head(h)])
        for h in range(H):
            weights = p_ref[s, h].astype(F32)
            moved = moved_ref[h]
            centre = jnp.sum(weights * moved, axis=0, keepdims=True)
            ds_ref[h] = (weights * (moved - centre)).astype(BF)
        keys_t = k_ref[key_at].T
        dq, dk, dv = [], [], []
        for h in range(H):
            dk.append(dot_nn(ds_ref[h], q_ref[at, head(h)]))
            dv.append(dot_nn(p_ref[s, h], g_ref[at, head(h)]))
            dq.append(dot_nn(keys_t[head(h)], ds_ref[h]))
        outs[0][at] = (jnp.concatenate(dq, axis=0).T.astype(BF) * 0.125).astype(BF)
        outs[1][key_at] = jnp.concatenate(dk, axis=1).astype(BF)
        outs[2][key_at] = jnp.concatenate(dv, axis=1).astype(BF)


def cross_back_kernel(
    count,
    dc_ref,
    co_ref,
    cq_ref,
    q_ref,
    k_ref,
    v_ref,
    p_ref,
    o_ref,
    x_ref,
    m_ref,
    dr2_ref,
    r1_ref,
    gain_ref,
    os_ref,
    dwq_ref,
    dwk_ref,
    dwv_ref,
    dwo_ref,
    dso_ref,
    dk_ref,
    dv_ref,
    dr1_ref,
    da_ref,
    sum_ref,
    g_ref,
    dq_ref,
    moved_ref,
    ds_ref,
):
    dc = dc_ref[...]
    g_ref[...] = dot_nt(dc, co_ref[...]).astype(BF)
    dwo_ref[...] = dot_tn(o_ref[...], dc).astype(BF)
    heads_back(
        count, q_ref, k_ref, v_ref, p_ref, g_ref, (dq_ref, dk_ref, dv_ref), moved_ref, ds_ref
    )
    dq = dq_ref[...]
    dr1 = dr2_ref[...] + dot_nt(dq, cq_ref[...])
    dwq_ref[...] = dot_tn(x_ref[...], dq).astype(BF)
    mt = m_ref[...].T
    dwk_ref[...] = dot_nn(mt, dk_ref[...]).astype(BF)
    dwv_ref[...] = dot_nn(mt, dv_ref[...]).astype(BF)
    back, sums = norm_back_sums(r1_ref[...], gain_ref[...], dr1)
    da = back.astype(BF)
    dr1_ref[...] = back
    da_ref[...] = da
    dso_ref[...] = dot_tn(os_ref[...], da).astype(BF)
    put_rows(sum_ref, sums + [row_sum(da), row_sum(dq), row_sum(dv_ref[...])])


def cross_back(dc, co, cq, q2, k2, v2, p2, o2, x1b, memory, dr2, r1, gain, o, count):
    tokens, rows = dc.shape[0], dc.shape[0] // count
    keys = memory.shape[0] // count
    square = jax.ShapeDtypeStruct((D, D), BF)
    low = jax.ShapeDtypeStruct((tokens, D), BF)
    return pl.pallas_call(
        functools.partial(cross_back_kernel, count),
        out_shape=[square] * 5
        + [
            jax.ShapeDtypeStruct(memory.shape, BF),
            jax.ShapeDtypeStruct(memory.shape, BF),
            jax.ShapeDtypeStruct((tokens, D), F32),
            low,
            jax.ShapeDtypeStruct((8, D), F32),
        ],
        scratch_shapes=[
            pltpu.VMEM((tokens, D), BF),
            pltpu.VMEM((tokens, D), BF),
            pltpu.VMEM((H, keys, rows), F32),
            pltpu.VMEM((H, keys, rows), BF),
        ],
        compiler_params=pltpu.CompilerParams(vmem_limit_bytes=18 << 20),
        cost_estimate=LONG,
        name="cross_back",
    )(dc, co, cq, q2, k2, v2, p2, o2, x1b, memory, dr2, r1, gain, o)


def self_back_kernel(
    count,
    da_ref,
    wo_ref,
    q_ref,
    k_ref,
    v_ref,
    p_ref,
    x_ref,
    dwq_ref,
    dwk_ref,
    dwv_ref,
    dq_ref,
    dk_ref,
    dv_ref,
    sum_ref,
    g_ref,
    moved_ref,
    ds_ref,
):
    g_ref[...] = dot_nt(da_ref[...], wo_ref[...]).astype(BF)
    heads_back(
        count, q_ref, k_ref, v_ref, p_ref, g_ref, (dq_ref, dk_ref, dv_ref), moved_ref, ds_ref
    )
    xt = x_ref[...].T
    dwq_ref[...] = dot_nn(xt, dq_ref[...]).astype(BF)
    dwk_ref[...] = dot_nn(xt, dk_ref[...]).astype(BF)
    dwv_ref[...] = dot_nn(xt, dv_ref[...]).astype(BF)
    put_rows(sum_ref, [row_sum(dq_ref[...]), row_sum(dv_ref[...])])


def self_back(da, wo, q, k, v, p, x, count):
    tokens, rows = da.shape[0], da.shape[0] // count
    square = jax.ShapeDtypeStruct((D, D), BF)
    low = jax.ShapeDtypeStruct((tokens, D), BF)
    return pl.pallas_call(
        functools.partial(self_back_kernel, count),
        out_shape=[square] * 3 + [low] * 3 + [jax.ShapeDtypeStruct((8, D), F32)],
        scratch_shapes=[
            pltpu.VMEM((tokens, D), BF),
            pltpu.VMEM((H, rows, rows), F32),
            pltpu.VMEM((H, rows, rows), BF),
        ],
        compiler_params=pltpu.CompilerParams(vmem_limit_bytes=14 << 20),
        cost_estimate=LONG,
        name="self_back",
    )(da, wo, q, k, v, p, x)


def rows_back_kernel(n, *refs):
    total = None if len(refs) == 2 * n + 1 else refs[2 * n][...]
    for g, w in zip(refs[:n], refs[n : 2 * n]):
        part = dot_nt(g[...], w[...])
        total = part if total is None else total + part
    refs[-1][...] = total


def rows_back(grads, weights, start=()):
    return pl.pallas_call(
        functools.partial(rows_back_kernel, len(grads)),
        out_shape=jax.ShapeDtypeStruct(grads[0].shape, F32),
        compiler_params=pltpu.CompilerParams(vmem_limit_bytes=10 << 20),
        cost_estimate=LONG,
        name="rows_back",
    )(*grads, *weights, *start)


def norm(summed):
    centre = summed - jnp.mean(summed, axis=-1, keepdims=True)
    scale = lax.rsqrt(jnp.mean(centre * centre, axis=-1, keepdims=True) + EPS)
    return centre * scale, scale


def norm_back(normal, scale, gain, grad):
    inner = grad * gain
    back = scale * (
        inner
        - jnp.mean(inner, axis=-1, keepdims=True)
        - normal * jnp.mean(inner * normal, axis=-1, keepdims=True)
    )
    return back, jnp.sum(grad * normal, axis=0), jnp.sum(grad, axis=0)


def column_sum(value):
    return jnp.sum(value.astype(F32), axis=0)


def gelu_and_slope(value):
    spread = 0.5 * (1.0 + lax.erf(value * np.float32(np.sqrt(0.5))))
    density = jnp.exp(-0.5 * value * value) * np.float32(1.0 / np.sqrt(2.0 * np.pi))
    return value * spread, spread + value * density


def pack_kernel(sp_ref, so_ref, ab_ref, eb_ref, cb_ref, ng_ref, ns_ref, out_ref):
    rows, n = so_ref.shape[0], ab_ref.shape[1]
    for i in range(3):
        out_ref[i * rows : (i + 1) * rows] = sp_ref[i]
    out_ref[3 * rows : 4 * rows] = so_ref[...]

    def padded(v, width):
        v = v.astype(F32)
        if v.shape[0] < 8:
            v = jnp.concatenate([v, jnp.zeros((8 - v.shape[0], v.shape[1]), F32)])
        return jnp.concatenate([v, jnp.zeros((8, width - v.shape[1]), F32)], axis=1)

    first = jnp.concatenate([ab_ref[...].astype(F32), cb_ref[...].astype(F32)])
    second = jnp.concatenate([ng_ref[...].astype(F32), ns_ref[...].astype(F32)])
    out_ref[4 * rows :] = jnp.concatenate(
        [padded(first, 128), padded(second, 128), padded(eb_ref[...], D - 256)], axis=1
    ).astype(BF)


def pack_self(sp, so, ab, eb, cb, ng, ns):
    ins = [sp, so, ab, eb.reshape(1, -1), cb.reshape(1, -1), ng, ns]
    ins = [pltpu.with_memory_space_constraint(a, pltpu.HBM) for a in ins]
    return pl.pallas_call(
        pack_kernel,
        grid=(1,),
        in_specs=[
            pl.BlockSpec(a.shape, lambda i, n=a.ndim: (0,) * n) for a in ins
        ],
        out_specs=pl.BlockSpec((4 * so.shape[0] + 8, D), lambda i: (0, 0)),
        out_shape=jax.ShapeDtypeStruct((4 * so.shape[0] + 8, D), BF),
        compiler_params=pltpu.CompilerParams(vmem_limit_bytes=4 << 20),
        cost_estimate=QUICK,
        name="pack_self",
    )(*ins)


def pack_small(ab, eb, cb, ng, ns):
    n, wide = cb.shape[0], eb.shape[0]
    return jnp.concatenate(
        [
            jnp.pad(jnp.concatenate([ab, cb[None]]), ((0, 1), (0, 128 - n))),
            jnp.pad(jnp.concatenate([ng, ns]), ((0, 2), (0, 128 - n))),
            jnp.pad(eb[None], ((0, 7), (0, D - 256 - wide))),
        ],
        axis=1,
    )


def unpack_small_kernel(n, wide, in_ref, rows_ref, eb_ref):
    for d in range(in_ref.shape[0]):
        block = in_ref[d].astype(F32)
        rows_ref[0:8, d * n : (d + 1) * n] = block[:, 0:n]
        rows_ref[8:16, d * n : (d + 1) * n] = block[:, 128 : 128 + n]
        eb_ref[:, d * wide : (d + 1) * wide] = block[0:1, 256 : 256 + wide]


def unpack_small(gathered, n, wide):
    devices = gathered.shape[0]
    return pl.pallas_call(
        functools.partial(unpack_small_kernel, n, wide),
        out_shape=[
            jax.ShapeDtypeStruct((16, devices * n), F32),
            jax.ShapeDtypeStruct((1, devices * wide), F32),
        ],
        compiler_params=pltpu.CompilerParams(vmem_limit_bytes=8 << 20),
        cost_estimate=QUICK,
        name="unpack_small",
    )(gathered)


def split_small_kernel(n, wide, ff_ref, cross_ref, self_ref, db_ref, g3_ref, s3_ref, eb_ref, out_ref):
    zero = jnp.zeros((1, D), F32)
    first = jnp.concatenate(
        [
            self_ref[0:2],
            cross_ref[2:5],
            ff_ref[2:3],
            db_ref[...].reshape(1, D),
            zero,
        ],
        axis=0,
    )
    second = jnp.concatenate(
        [
            cross_ref[0:1],
            ff_ref[0:1],
            g3_ref[...].reshape(1, D),
            cross_ref[1:2],
            ff_ref[1:2],
            s3_ref[...].reshape(1, D),
            zero,
            zero,
        ],
        axis=0,
    )
    tail = jnp.broadcast_to(eb_ref[...], (8, FF))

    def padded(v, width):
        return jnp.concatenate([v, jnp.zeros((8, width - v.shape[1]), F32)], axis=1)

    for d in range(out_ref.shape[0]):
        out_ref[d] = jnp.concatenate(
            [
                padded(first[:, d * n : (d + 1) * n], 128),
                padded(second[:, d * n : (d + 1) * n], 128),
                padded(tail[:, d * wide : (d + 1) * wide], D - 256),
            ],
            axis=1,
        ).astype(BF)


def split_small(ff_sums, cross_sums, self_sums, vectors, eb, n, wide):
    devices = D // n
    return pl.pallas_call(
        functools.partial(split_small_kernel, n, wide),
        out_shape=jax.ShapeDtypeStruct((devices, 8, D), BF),
        compiler_params=pltpu.CompilerParams(vmem_limit_bytes=8 << 20),
        cost_estimate=QUICK,
        name="split_small",
    )(ff_sums, cross_sums, self_sums, *vectors, eb)


def body(
    layer_input,
    encoder_states,
    output_grad,
    span_start,
    span_length,
    self_project,
    self_output,
    cross_project,
    cross_output,
    attend_bias,
    expand_weight,
    expand_bias,
    contract_weight,
    contract_bias,
    norm_gain,
    norm_shift,
):
    place = Place()
    count, length = layer_input.shape[:2]
    shape = layer_input.shape
    rows = self_output.shape[0]
    wide = expand_bias.shape[0]
    fits = rows % 8 == 0 and place.bits == 2
    reduce = Reduce if fits else PlainReduce
    reduce_hop_last = ReduceHopLast if fits else PlainReduce
    x = layer_input.reshape(-1, D)
    memory = encoder_states.reshape(-1, D)
    grad_out = output_grad.reshape(-1, D).astype(F32)

    local_cross = jnp.concatenate([cross_project.reshape(-1, D), cross_output])
    four = [(i * rows, rows) for i in range(4)]
    if fits:
        g_self = Gather(
            place,
            pack_self(
                self_project,
                self_output,
                attend_bias,
                expand_bias,
                contract_bias,
                norm_gain,
                norm_shift,
            ),
        )
        line = g_self.column()
        g_self.hop(0, 0)
        g_self.hop(1, 0)
        g_cross = Gather(place, after(local_cross, line))
        g_self.blocks, g_cross.got = lax.optimization_barrier((g_self.blocks, g_cross.got))
        g_self.hop(1, 1)
        line = g_cross.column()
        g_cross.hop(0, 0)
        g_cross.hop(1, 0)
        g_expand = Gather(place, after(expand_weight, line))
        g_self.blocks, g_cross.blocks, g_expand.got = lax.optimization_barrier(
            (g_self.blocks, g_cross.blocks, g_expand.got)
        )
        g_cross.hop(1, 1)
        line = g_expand.column()
        g_expand.hop(0, 0)
        g_expand.hop(1, 0)
        g_contract = Gather(place, after(contract_weight, line))
        g_self.half(line)
        *w_self, smalls = g_self.spread(four + [(4 * rows, 8)])
        smalls = smalls.reshape(-1, 8, D)
    else:
        whole = lax.all_gather(
            jnp.concatenate(
                [
                    self_project.reshape(-1, D),
                    self_output,
                    pack_small(
                        attend_bias, expand_bias, contract_bias, norm_gain, norm_shift
                    ),
                    local_cross,
                    contract_weight,
                ]
            ),
            AXES,
            axis=0,
        )
        squares = [
            whole[:, a : a + rows].reshape(D, D)
            for a in [i * rows for i in range(4)]
            + [4 * rows + 8 + i * rows for i in range(4)]
        ]
        w_self, w_cross = squares[:4], squares[4:]
        contract = whole[:, 8 * rows + 8 :].reshape(FF, D)
        smalls = whole[:, 4 * rows : 4 * rows + 8]
        expand = lax.all_gather(expand_weight, AXES, axis=0, tiled=True)
    wq, wk, wv, wo = w_self
    small_rows, expand_b = unpack_small(smalls, rows, wide)
    biases = [small_rows[i : i + 1] for i in range(6)]
    contract_b = small_rows[6:7]
    gains = [small_rows[8 + i : 9 + i] for i in range(3)]
    shifts = [small_rows[11 + i : 12 + i] for i in range(3)]

    q = ((dot_nn(x, wq) + biases[0]) * 0.125).astype(BF)
    k = dot_nn(x, wk).astype(BF)
    v = (dot_nn(x, wv) + biases[1]).astype(BF)
    o, p = attend(q, k, v, span_start, span_length, True, count)
    if fits:
        g_cross.blocks, g_expand.blocks, g_contract.got, o = lax.optimization_barrier(
            (g_cross.blocks, g_expand.blocks, g_contract.got, o)
        )
        g_expand.hop(1, 1)
        line = g_contract.column()
        g_contract.hop(0, 0)
        g_contract.hop(1, 0)
        g_cross.half(line)
        w_cross = g_cross.spread(four)
    r1 = x.astype(F32) + (dot_nn(o, wo) + biases[2])
    n1, s1 = norm(r1)
    x1 = n1 * gains[0] + shifts[0]
    x1b = x1.astype(BF)
    cq, ck, cv, co = w_cross
    q2 = ((dot_nn(x1b, cq) + biases[3]) * 0.125).astype(BF)
    k2 = dot_nn(memory, ck).astype(BF)
    v2 = (dot_nn(memory, cv) + biases[4]).astype(BF)
    o2, p2 = attend(q2, k2, v2, span_start, span_length, False, count)
    if fits:
        g_expand.blocks, g_contract.blocks, o2 = lax.optimization_barrier(
            (g_expand.blocks, g_contract.blocks, o2)
        )
        g_contract.hop(1, 1)
        g_expand.half()
        (expand,) = g_expand.spread([(0, rows)])
    r2 = x1 + (dot_nn(o2, co) + biases[5])
    n2, s2 = norm(r2)
    x2 = n2 * gains[1] + shifts[1]
    x2b = x2.astype(BF)
    act, slope = gelu_and_slope(dot_nn(x2b, expand) + expand_b)
    act = act.astype(BF)
    slope = slope.astype(BF)
    if fits:
        g_contract.blocks[3] = after(g_contract.blocks[3], act)
        (contract,) = g_contract.spread([(0, 4 * rows)])
    n3, s3 = norm(x2 + (dot_nn(act, contract) + contract_b))
    output = (n3 * gains[2] + shifts[2]).astype(BF)

    dr3, gain3, shift3 = norm_back(n3, s3, gains[2], grad_out)
    df = dr3.astype(BF)
    d_contract = dot_tn(act, df).astype(BF)
    r_contract = reduce_hop_last(place, [owner_blocks(place, d_contract)])
    d_contract_b = column_sum(df)
    du, d_expand_b = hidden_back(after(df, d_contract), contract, slope)
    sent = r_contract.leave(0, du)
    d_expand = dot_tn(x2b, after(du, sent)).astype(BF)
    r_expand = reduce(place, [owner_blocks(place, d_expand)])
    dr2, dc, ff_sums = expand_back(
        after(du, r_expand.sent), expand, dr3, r2, gains[1]
    )
    sent = r_expand.leave(0, dc)
    sent = r_contract.line(sent)
    *d_cross, dk2, dv2, dr1, da, cross_sums = cross_back(
        after(dc, sent), co, cq, q2, k2, v2, p2, o2, x1b, memory, dr2, r1, gains[0], o, count
    )
    r_cross = reduce(place, [owner_blocks(place, d) for d in d_cross])
    sent = r_expand.leave(1, r_cross.sent)
    fence(place, sent)
    sent = r_cross.leave(0, place.spots)
    *d_self, dq, dk, dv, self_sums = self_back(after(da, sent), wo, q, k, v, p, x, count)
    sent = r_expand.last(self_sums)
    small_blocks = split_small(
        ff_sums,
        cross_sums,
        self_sums,
        [d_contract_b, gain3, shift3],
        d_expand_b,
        rows,
        wide,
    )
    small_blocks = small_blocks.reshape(place.dp_count, place.chips, 2, 8, D)
    r_self = reduce(
        place,
        [owner_blocks(place, d) for d in after(d_self, sent)] + [small_blocks],
    )
    sent = r_contract.turn(r_self.sent)
    encoder_grad = rows_back(after([dk2, dv2], sent), [ck, cv])
    sent = r_cross.leave(1, encoder_grad)
    (own_expand,) = r_expand.result([((rows, FF), 0, 0)], sent)
    (own_contract,) = r_contract.result([((4 * rows, D), 0, 0)], own_expand)
    input_grad = rows_back(after([dq, dk, dv], own_contract), [wq, wk, wv], [dr1])
    r_cross.got[-1] = after(r_cross.latest(), input_grad)
    sent = r_self.leave(0, r_cross.latest())
    sent = r_cross.last(sent)
    sent = r_self.leave(1, fence(place, sent))
    projects = ((3, rows, D), 0, 0)
    square = (rows, D)
    own_cross = r_cross.result(
        [projects, (square, 3 * rows, 0), (square, 4 * rows, 0)], sent
    )
    r_self.last(fence(place, own_cross[0]))
    at = 3 * rows
    own_self = r_self.result(
        [
            projects,
            ((6, rows), at, 0),
            ((1, wide), at, 256),
            ((1, rows), at + 6, 0),
            ((3, rows), at, 128),
            ((3, rows), at + 3, 128),
        ]
    )
    own_self = [own_self[0], own_cross[2], *own_self[1:]]
    return (
        output.reshape(shape),
        input_grad.reshape(shape),
        encoder_grad.reshape(encoder_states.shape),
        own_self[0],
        own_self[1],
        own_cross[0],
        own_cross[1],
        own_self[2],
        own_expand,
        own_self[3].reshape(-1),
        own_contract,
        own_self[4].reshape(-1),
        own_self[5],
        own_self[6],
    )


def solution(mesh):
    rows = P(AXES)
    return jax.shard_map(
        body,
        mesh=mesh,
        in_specs=(
            P(AXES, None, None),
            P(AXES, None, None),
            P(AXES, None, None),
            P(AXES),
            P(AXES),
            P(None, AXES, None),
            P(AXES, None),
            P(None, AXES, None),
            P(AXES, None),
            P(None, AXES),
            P(AXES, None),
            P(AXES),
            P(AXES, None),
            P(AXES),
            P(None, AXES),
            P(None, AXES),
        ),
        out_specs=(
            P(AXES, None, None),
            P(AXES, None, None),
            P(AXES, None, None),
            P(None, AXES, None),
            P(AXES, None),
            P(None, AXES, None),
            P(AXES, None),
            P(None, AXES),
            P(AXES, None),
            P(AXES),
            P(AXES, None),
            P(AXES),
            P(None, AXES),
            P(None, AXES),
        ),
        check_vma=False,
    )
```

```python
import functools

import jax
import jax.numpy as jnp
import numpy as np
from jax import lax
from jax.experimental import pallas as pl
from jax.experimental.pallas import tpu as pltpu
from jax.sharding import PartitionSpec as P

D = 768
H = 12
HD = 64
FF = 3072
AXES = ("dp", "fsdp")

EPS = 1e-05
BIG_NEGATIVE = -1000000000.0
BF = jnp.bfloat16
F32 = jnp.float32
QUICK = pl.CostEstimate(flops=1000, bytes_accessed=1000, transcendentals=0)
LONG = pl.CostEstimate(flops=4 * 10**10, bytes_accessed=10**6, transcendentals=0)


class Place:
    def __init__(self):
        self.dp_count = lax.axis_size("dp")
        self.inner = lax.axis_size("fsdp")
        self.chips = self.inner // 2
        self.bits = int(np.log2(self.dp_count))
        self.dp = lax.axis_index("dp")
        inner = lax.axis_index("fsdp")
        self.chip = inner // 2
        self.core = inner % 2
        table = []
        for dp in range(self.dp_count):
            for chip in range(self.chips):
                for core in range(2):
                    table.append(
                        [dp ^ self.mask(core, m) for m in range(self.dp_count)]
                        + [dp ^ self.mask(1 - core, m) for m in range(self.dp_count)]
                        + [(chip + k) % self.chips for k in range(self.chips)]
                        + [(chip - k) % self.chips for k in range(self.chips)]
                        + [core, 1 - core]
                    )
        index = self.dp * self.inner + inner
        self.spots = lax.dynamic_index_in_dim(
            jnp.asarray(np.array(table, np.int32)), index, 0, keepdims=False
        )
        self.theirs_at = self.dp_count
        self.up_at = 2 * self.dp_count
        self.down_at = self.up_at + self.chips
        self.core_at = self.down_at + self.chips

    def bit(self, core, step):
        return 1 << (self.bits - 1 - step if core == 0 else step)

    def mask(self, core, relative):
        return sum(self.bit(core, s) for s in range(self.bits) if relative >> s & 1)

    def permute(self, value, target):
        pairs = []
        for dp in range(self.dp_count):
            for chip in range(self.chips):
                for core in range(2):
                    to = target(dp, chip, core)
                    pairs.append(
                        (
                            dp * self.inner + chip * 2 + core,
                            to[0] * self.inner + to[1] * 2 + to[2],
                        )
                    )
        return lax.ppermute(value, AXES, pairs)

    def across_cores(self, value):
        return self.permute(value, lambda d, z, c: (d, z, 1 - c))

    def across_step(self, value, step):
        return self.permute(value, lambda d, z, c: (d ^ self.bit(c, step), z, c))

    def along_chips(self, value, shift):
        return self.permute(value, lambda d, z, c: (d, (z + shift) % self.chips, c))


def after(values, *earlier):
    return lax.optimization_barrier((values, earlier))[0]


def copy_kernel(plan, n_in, spots_ref, *refs):
    ins, outs, sems = refs[:n_in], refs[n_in:-1], refs[-1]
    copies = []
    for i, (source, source_at, target, target_at) in enumerate(plan):
        copies.append(
            pltpu.make_async_copy(
                ins[source].at[source_at(spots_ref)],
                outs[target].at[target_at(spots_ref)],
                sems.at[i],
            )
        )
    for c in copies:
        c.start()
    for c in copies:
        c.wait()


def copy_call(place, plan, ins, outs, name):
    anywhere = pl.BlockSpec(memory_space=pl.ANY)
    return pl.pallas_call(
        functools.partial(copy_kernel, plan, len(ins)),
        grid_spec=pltpu.PrefetchScalarGridSpec(
            num_scalar_prefetch=1,
            grid=(1,),
            in_specs=[anywhere] * len(ins),
            out_specs=[anywhere] * len(outs),
            scratch_shapes=[pltpu.SemaphoreType.DMA((len(plan),))],
        ),
        out_shape=outs,
        compiler_params=pltpu.CompilerParams(vmem_limit_bytes=1 << 20),
        cost_estimate=QUICK,
        name=name,
    )(place.spots, *ins)


def fence_kernel(in_ref, out_ref):
    for i in range(in_ref.shape[0]):
        out_ref[i] = in_ref[i]


def fence(place, *values):
    spots = place.spots
    scalars = pl.BlockSpec(memory_space=pltpu.SMEM)
    place.spots = pl.pallas_call(
        fence_kernel,
        in_specs=[scalars],
        out_specs=scalars,
        out_shape=jax.ShapeDtypeStruct(spots.shape, spots.dtype),
        compiler_params=pltpu.CompilerParams(vmem_limit_bytes=1 << 20),
        cost_estimate=LONG,
        name="fence",
    )(after(spots, *values))
    return place.spots


class Gather:
    def __init__(self, place, local):
        self.place = place
        self.local = local
        self.got = [local] + [
            place.along_chips(local, k) for k in range(1, place.chips)
        ]

    def column(self, *earlier):
        place = self.place
        self.got = after(self.got, *earlier)
        plan = [
            (
                k,
                lambda s: (slice(None),),
                0,
                lambda s, k=k: (s[place.down_at + k],),
            )
            for k in range(place.chips)
        ]
        shape = jax.ShapeDtypeStruct((place.chips,) + self.local.shape, BF)
        self.blocks = {0: copy_call(place, plan, self.got, [shape], "column")[0]}
        return self.blocks[0]

    def meet(self, later):
        self.blocks, later.got = lax.optimization_barrier((self.blocks, later.got))

    def hop(self, step, held, *earlier):
        self.blocks[held] = after(self.blocks[held], *earlier)
        self.blocks[held | 1 << step] = self.place.across_step(self.blocks[held], step)

    def share(self, held):
        return self.place.across_cores(self.blocks[held])

    def half(self, *earlier):
        place = self.place
        ins = after([self.blocks[m] for m in range(place.dp_count)], *earlier)
        plan = [
            (m, lambda s: (slice(None),), 0, lambda s, m=m: (s[m],))
            for m in range(place.dp_count)
        ]
        shape = jax.ShapeDtypeStruct((place.dp_count,) + ins[0].shape, BF)
        self.own_half = copy_call(place, plan, ins, [shape], "half")[0]
        self.other_half = place.across_cores(self.own_half)
        return self.own_half

    def spread(self, parts, *earlier):
        place = self.place
        cols = self.local.shape[1]
        whole = slice(None)
        if hasattr(self, "other_half"):
            ins = [self.own_half, self.other_half]
            places = [lambda s: (whole,), lambda s: (whole,)]
        else:
            ins = [self.blocks[m] for m in range(place.dp_count)]
            ins += [self.share(m) for m in range(place.dp_count)]
            places = [lambda s, m=m: (s[m],) for m in range(2 * place.dp_count)]
        ins = after(ins, *earlier)
        plan, outs = [], []
        for out, (first, rows) in enumerate(parts):
            outs.append(
                jax.ShapeDtypeStruct((place.dp_count, place.chips, 2, rows, cols), BF)
            )
            for m, where in enumerate(places):
                core = place.core_at + (m >= len(places) // 2)
                lead = (whole,) * (ins[m].ndim - 2)
                plan.append(
                    (
                        m,
                        lambda s, a=first, n=rows, lead=lead: lead + (pl.ds(a, n),),
                        out,
                        lambda s, where=where, core=core: where(s) + (whole, s[core]),
                    )
                )
        full = copy_call(place, plan, ins, outs, "spread")
        return [w.reshape(-1, cols) for w in full]


def side_by_side(refs):
    parts = [r[...].reshape(r.shape[1:2] + r.shape[-2:]) for r in refs]
    return parts[0] if len(parts) == 1 else jnp.concatenate(parts, axis=1)


def exchange_kernel(spots_ref, *refs):
    out = refs[-1]
    out[...] = side_by_side(refs[:-1]).reshape(out.shape)


def sum_refs(refs, n):
    value = side_by_side(refs[:n]).astype(F32)
    for a in refs[n:]:
        value = value + a[...].astype(F32).reshape(value.shape)
    return value


def leave_kernel(n, spots_ref, *refs):
    out = refs[-1]
    out[...] = sum_refs(refs[:-1], n).astype(BF).reshape(out.shape)


def last_kernel(n, each, chips, spots_ref, *refs):
    outs = refs[chips * each :]
    for k in range(chips):
        value = sum_refs(refs[k * each : (k + 1) * each], n)
        outs[k][...] = value.astype(outs[k].dtype).reshape(outs[k].shape)


def cut_kernel(parts, count, *refs):
    total = refs[0][...].astype(F32)
    for r in refs[1:count]:
        total = total + r[...].astype(F32)
    for (shape, row, col), out in zip(parts, refs[count:]):
        piece = total[row : row + int(np.prod(shape[:-1])), col : col + shape[-1]]
        out[...] = piece.reshape(shape)


def cut_sum(terms, parts):
    return pl.pallas_call(
        functools.partial(cut_kernel, parts, len(terms)),
        out_shape=[jax.ShapeDtypeStruct(s, F32) for s, _, _ in parts],
        compiler_params=pltpu.CompilerParams(vmem_limit_bytes=8 << 20),
        cost_estimate=QUICK,
        name="cut_sum",
    )(*terms)


class Reduce:
    def __init__(self, place, blocks):
        self.place = place
        self.blocks = blocks
        self.rows = sum(b.shape[3] for b in blocks)
        self.cols = blocks[0].shape[4]
        shape = (place.dp_count, place.chips, self.rows, self.cols)
        sent = self.call(
            exchange_kernel,
            (place.dp_count,),
            [
                pl.BlockSpec(
                    (1, place.chips, 1) + b.shape[3:],
                    lambda i, s: (i, 0, s[place.core_at + 1], 0, 0),
                )
                for b in blocks
            ],
            pl.BlockSpec((1,) + shape[1:], lambda i, s: (i, 0, 0, 0)),
            jax.ShapeDtypeStruct(shape, BF),
            "exchange",
        )(place.spots, *blocks)
        self.sent = sent
        self.other = place.across_cores(sent)
        self.got = []

    def call(self, kernel, grid, in_specs, out_specs, out_shape, name):
        return pl.pallas_call(
            kernel,
            grid_spec=pltpu.PrefetchScalarGridSpec(
                num_scalar_prefetch=1, grid=grid, in_specs=in_specs, out_specs=out_specs
            ),
            out_shape=out_shape,
            compiler_params=pltpu.CompilerParams(
                vmem_limit_bytes=(14 if name == "line" else 8) << 20
            ),
            cost_estimate=QUICK,
            name=name,
        )

    def leave(self, step, *earlier):
        place = self.place
        if step == 0:
            self.other = after(self.other, *earlier)
        else:
            self.got[-1] = after(self.got[-1], *earlier)
        count = 1 << (place.bits - 1 - step)
        chips, core = place.chips, place.core_at

        def spot(i, s):
            return s[(1 << step) + i * (2 << step)]

        shape = (count, chips, self.rows, self.cols)
        specs = [
            pl.BlockSpec(
                (1, chips, 1) + b.shape[3:], lambda i, s: (spot(i, s), 0, s[core], 0, 0)
            )
            for b in self.blocks
        ]
        specs.append(pl.BlockSpec((1,) + shape[1:], lambda i, s: (spot(i, s), 0, 0, 0)))
        for t in range(step):
            specs.append(
                pl.BlockSpec(
                    (1,) + shape[1:],
                    lambda i, s, t=t: ((1 << (step - t - 1)) + i * (1 << (step - t)), 0, 0, 0),
                )
            )
        sent = self.call(
            functools.partial(leave_kernel, len(self.blocks)),
            (count,),
            specs,
            pl.BlockSpec((1,) + shape[1:], lambda i, s: (i, 0, 0, 0)),
            jax.ShapeDtypeStruct(shape, BF),
            "leave",
        )(place.spots, *self.blocks, self.other, *self.got)
        self.got.append(place.across_step(sent, step))
        return sent

    def latest(self):
        return self.got[-1]

    def last(self, *earlier):
        place = self.place
        self.got[-1] = after(self.got[-1], *earlier)
        chips, core = place.chips, place.core_at
        specs, ins = [], []
        for k in range(chips):
            up = place.up_at + k
            for b in self.blocks:
                ins.append(b)
                specs.append(
                    pl.BlockSpec(
                        (1, 1, 1) + b.shape[3:],
                        lambda i, s, up=up: (s[0], s[up], s[core], 0, 0),
                    )
                )
            for n, g in enumerate([self.other] + self.got):
                ins.append(g)
                specs.append(
                    pl.BlockSpec(
                        (1, 1, self.rows, self.cols),
                        lambda i, s, up=up, n=n: (s[0] if n == 0 else 0, s[up], 0, 0),
                    )
                )
        own, *sent = self.call(
            functools.partial(last_kernel, len(self.blocks), len(ins) // chips, chips),
            (1,),
            specs,
            [pl.BlockSpec((self.rows, self.cols), lambda i, s: (0, 0))] * chips,
            [
                jax.ShapeDtypeStruct((self.rows, self.cols), F32 if k == 0 else BF)
                for k in range(chips)
            ],
            "last",
        )(place.spots, *ins)
        self.own = own
        self.came = [place.along_chips(v, k + 1) for k, v in enumerate(sent)]
        return own

    def result(self, parts, *earlier):
        self.came = after(self.came, *earlier)
        return cut_sum([self.own] + self.came, parts)


def line_kernel(n, each, chips, spots_ref, *refs):
    outs = refs[2 * chips * each :]
    for k in range(chips):
        for i in range(2):
            at = (2 * k + i) * each
            value = sum_refs(refs[at : at + each], n)
            outs[k][i] = value.astype(outs[k].dtype).reshape(outs[k].shape[1:])


def turn_kernel(own_ref, *refs):
    *came, keep_ref, send_ref = refs
    total = own_ref[...]
    for c in came:
        total = total + c[...].astype(F32)
    keep_ref[...] = total[0]
    send_ref[...] = total[1].astype(BF)


class ReduceHopLast(Reduce):
    def line(self, *earlier):
        place = self.place
        self.got[-1] = after(self.got[-1], *earlier)
        chips, core = place.chips, place.core_at
        specs, ins = [], []
        for k in range(chips):
            up = place.up_at + k
            for i in range(2):
                for b in self.blocks:
                    ins.append(b)
                    specs.append(
                        pl.BlockSpec(
                            (1, 1, 1) + b.shape[3:],
                            lambda _, s, up=up, i=i: (s[2 * i], s[up], s[core], 0, 0),
                        )
                    )
                ins.append(self.other)
                specs.append(
                    pl.BlockSpec(
                        (1, 1, self.rows, self.cols),
                        lambda _, s, up=up, i=i: (s[2 * i], s[up], 0, 0),
                    )
                )
                ins.append(self.got[0])
                specs.append(
                    pl.BlockSpec(
                        (1, 1, self.rows, self.cols),
                        lambda _, s, up=up, i=i: (i, s[up], 0, 0),
                    )
                )
        shape = (2, self.rows, self.cols)
        own, *sent = self.call(
            functools.partial(line_kernel, len(self.blocks), len(ins) // chips // 2, chips),
            (1,),
            specs,
            [pl.BlockSpec(shape, lambda _, s: (0, 0, 0))] * chips,
            [jax.ShapeDtypeStruct(shape, F32 if k == 0 else BF) for k in range(chips)],
            "line",
        )(place.spots, *ins)
        self.own = own
        self.came = [place.along_chips(v, k + 1) for k, v in enumerate(sent)]
        return own

    def turn(self, *earlier):
        came = after(self.came, *earlier)
        shape = (self.rows, self.cols)
        self.own, sent = pl.pallas_call(
            turn_kernel,
            out_shape=[jax.ShapeDtypeStruct(shape, F32), jax.ShapeDtypeStruct(shape, BF)],
            compiler_params=pltpu.CompilerParams(vmem_limit_bytes=8 << 20),
            cost_estimate=QUICK,
            name="turn",
        )(self.own, *came)
        self.came = [self.place.across_step(sent, 1)]
        return sent


def owner_blocks(place, gradient):
    rows = gradient.shape[0] // (place.dp_count * place.inner)
    return gradient.reshape(
        place.dp_count, place.chips, 2, rows, gradient.shape[-1]
    )


class PlainReduce:
    def __init__(self, place, blocks):
        devices = place.dp_count * place.inner
        flat = [b.reshape((devices,) + b.shape[3:]) for b in blocks]
        self.sum = lax.psum_scatter(
            jnp.concatenate(flat, axis=1), AXES, scatter_dimension=0, tiled=False
        )
        self.sent = self.sum

    def leave(self, step, *earlier):
        return self.sum

    def last(self, *earlier):
        return self.sum

    def latest(self):
        return self.sum

    got = [None]

    def line(self, *earlier):
        return self.sum

    def turn(self, *earlier):
        return self.sum

    def result(self, parts, *earlier):
        total = self.sum.astype(F32)
        return [
            total[r : r + int(np.prod(s[:-1])), c : c + s[-1]].reshape(s)
            for s, r, c in parts
        ]


def dot_nt(a, b):
    return lax.dot_general(a, b, (((1,), (1,)), ((), ())), preferred_element_type=F32)


def dot_nn(a, b):
    return jnp.dot(a, b, preferred_element_type=F32)


def dot_tn(a, b):
    return lax.dot_general(a, b, (((0,), (0,)), ((), ())), preferred_element_type=F32)


def head(h):
    return slice(h * HD, (h + 1) * HD)


def attend_kernel(
    masked, start_ref, length_ref, q_ref, k_ref, v_ref, o_ref, p_ref, scores_ref
):
    rows = q_ref.shape[0]
    keys = k_ref.shape[0]
    if masked:
        seq = pl.program_id(0)
        start = start_ref[seq]
        stop = start + length_ref[seq]
        key_at = lax.broadcasted_iota(jnp.int32, (keys, rows), 0)
        row_at = lax.broadcasted_iota(jnp.int32, (keys, rows), 1)
        inside = (key_at >= start) & (key_at < stop) & (row_at >= start) & (row_at < stop)
        hidden = jnp.where((key_at <= row_at) | inside, 0.0, BIG_NEGATIVE).astype(F32)
    for h in range(H):
        scores_ref[h] = dot_nt(k_ref[:, head(h)], q_ref[:, head(h)])
    for h in range(H):
        scores = scores_ref[h]
        if masked:
            scores = scores + hidden
        peak = jnp.max(scores, axis=0, keepdims=True)
        weights = jnp.exp(scores - peak)
        total = jnp.sum(weights, axis=0, keepdims=True)
        p_ref[0, h] = (weights * (1.0 / total)).astype(BF)
    values_t = v_ref[...].T
    pieces = [dot_nn(values_t[head(h)], p_ref[0, h]) for h in range(H)]
    o_ref[...] = jnp.concatenate(pieces, axis=0).T.astype(BF)


def attend(queries, keys, values, start, length, masked, count):
    rows = queries.shape[0] // count
    key_rows = keys.shape[0] // count
    block = lambda n: pl.BlockSpec((n, D), lambda s, *_: (s, 0))
    return pl.pallas_call(
        functools.partial(attend_kernel, masked),
        grid_spec=pltpu.PrefetchScalarGridSpec(
            num_scalar_prefetch=2,
            grid=(count,),
            in_specs=[block(rows), block(key_rows), block(key_rows)],
            out_specs=[
                block(rows),
                pl.BlockSpec((1, H, key_rows, rows), lambda s, *_: (s, 0, 0, 0)),
            ],
            scratch_shapes=[pltpu.VMEM((H, key_rows, rows), F32)],
        ),
        out_shape=[
            jax.ShapeDtypeStruct(queries.shape, BF),
            jax.ShapeDtypeStruct((count, H, key_rows, rows), BF),
        ],
        compiler_params=pltpu.CompilerParams(vmem_limit_bytes=14 << 20),
        cost_estimate=QUICK,
        name="attend",
    )(start, length, queries, keys, values)


def norm_parts(summed):
    centre = summed - jnp.mean(summed, axis=-1, keepdims=True)
    scale = lax.rsqrt(jnp.mean(centre * centre, axis=-1, keepdims=True) + EPS)
    return centre * scale, scale


def row_sum(value):
    return jnp.sum(value.astype(F32), axis=0, keepdims=True)


def norm_back_sums(summed, gain, grad):
    normal, scale = norm_parts(summed)
    inner = grad * gain
    back = scale * (
        inner
        - jnp.mean(inner, axis=-1, keepdims=True)
        - normal * jnp.mean(inner * normal, axis=-1, keepdims=True)
    )
    return back, [row_sum(grad * normal), row_sum(grad)]


def put_rows(ref, rows):
    for i, r in enumerate(rows):
        ref[i : i + 1] = r


def hidden_back_kernel(df_ref, c_ref, slope_ref, du_ref, sum_ref):
    du = (dot_nt(df_ref[...], c_ref[...]) * slope_ref[...].astype(F32)).astype(BF)
    du_ref[...] = du
    sum_ref[...] = row_sum(du)


def hidden_back(df, contract, slope):
    tokens = df.shape[0]
    return pl.pallas_call(
        hidden_back_kernel,
        grid=(FF // D,),
        in_specs=[
            pl.BlockSpec((tokens, D), lambda j: (0, 0)),
            pl.BlockSpec((D, D), lambda j: (j, 0)),
            pl.BlockSpec((tokens, D), lambda j: (0, j)),
        ],
        out_specs=[
            pl.BlockSpec((tokens, D), lambda j: (0, j)),
            pl.BlockSpec((1, D), lambda j: (0, j)),
        ],
        out_shape=[
            jax.ShapeDtypeStruct((tokens, FF), BF),
            jax.ShapeDtypeStruct((1, FF), F32),
        ],
        compiler_params=pltpu.CompilerParams(vmem_limit_bytes=16 << 20),
        cost_estimate=LONG,
        name="hidden_back",
    )(df, contract, slope)


def expand_back_kernel(
    du_ref, e_ref, dr3_ref, r2_ref, gain_ref, dr2_ref, dc_ref, sum_ref
):
    j = pl.program_id(0)

    @pl.when(j == 0)
    def _():
        dr2_ref[...] = dr3_ref[...]

    dr2_ref[...] += dot_nt(du_ref[...], e_ref[...])

    @pl.when(j == pl.num_programs(0) - 1)
    def _():
        back, sums = norm_back_sums(r2_ref[...], gain_ref[...], dr2_ref[...])
        dc = back.astype(BF)
        dr2_ref[...] = back
        dc_ref[...] = dc
        put_rows(sum_ref, sums + [row_sum(dc)])


def expand_back(du, expand, dr3, r2, gain):
    tokens = du.shape[0]
    still = pl.BlockSpec((tokens, D), lambda j: (0, 0))
    moving = lambda n: pl.BlockSpec((n, D), lambda j: (0, j))
    return pl.pallas_call(
        expand_back_kernel,
        grid=(FF // D,),
        in_specs=[
            moving(tokens),
            moving(D),
            still,
            still,
            pl.BlockSpec((1, D), lambda j: (0, 0)),
        ],
        out_specs=[still, still, pl.BlockSpec((8, D), lambda j: (0, 0))],
        out_shape=[
            jax.ShapeDtypeStruct((tokens, D), F32),
            jax.ShapeDtypeStruct((tokens, D), BF),
            jax.ShapeDtypeStruct((8, D), F32),
        ],
        compiler_params=pltpu.CompilerParams(vmem_limit_bytes=20 << 20),
        cost_estimate=LONG,
        name="expand_back",
    )(du, expand, dr3, r2, gain)


def heads_back(count, q_ref, k_ref, v_ref, p_ref, g_ref, outs, moved_ref, ds_ref):
    rows = q_ref.shape[0] // count
    keys = k_ref.shape[0] // count
    for s in range(count):
        at = slice(s * rows, (s + 1) * rows)
        key_at = slice(s * keys, (s + 1) * keys)
        for h in range(H):
            moved_ref[h] = dot_nt(v_ref[key_at, head(h)], g_ref[at, head(h)])
        for h in range(H):
            weights = p_ref[s, h].astype(F32)
            moved = moved_ref[h]
            centre = jnp.sum(weights * moved, axis=0, keepdims=True)
            ds_ref[h] = (weights * (moved - centre)).astype(BF)
        keys_t = k_ref[key_at].T
        dq, dk, dv = [], [], []
        for h in range(H):
            dk.append(dot_nn(ds_ref[h], q_ref[at, head(h)]))
            dv.append(dot_nn(p_ref[s, h], g_ref[at, head(h)]))
            dq.append(dot_nn(keys_t[head(h)], ds_ref[h]))
        outs[0][at] = (jnp.concatenate(dq, axis=0).T.astype(BF) * 0.125).astype(BF)
        outs[1][key_at] = jnp.concatenate(dk, axis=1).astype(BF)
        outs[2][key_at] = jnp.concatenate(dv, axis=1).astype(BF)


def cross_back_kernel(
    count,
    dc_ref,
    co_ref,
    cq_ref,
    q_ref,
    k_ref,
    v_ref,
    p_ref,
    o_ref,
    x_ref,
    m_ref,
    dr2_ref,
    r1_ref,
    gain_ref,
    os_ref,
    dwq_ref,
    dwk_ref,
    dwv_ref,
    dwo_ref,
    dso_ref,
    dk_ref,
    dv_ref,
    dr1_ref,
    da_ref,
    sum_ref,
    g_ref,
    dq_ref,
    moved_ref,
    ds_ref,
):
    dc = dc_ref[...]
    g_ref[...] = dot_nt(dc, co_ref[...]).astype(BF)
    dwo_ref[...] = dot_tn(o_ref[...], dc).astype(BF)
    heads_back(
        count, q_ref, k_ref, v_ref, p_ref, g_ref, (dq_ref, dk_ref, dv_ref), moved_ref, ds_ref
    )
    dq = dq_ref[...]
    dr1 = dr2_ref[...] + dot_nt(dq, cq_ref[...])
    dwq_ref[...] = dot_tn(x_ref[...], dq).astype(BF)
    mt = m_ref[...].T
    dwk_ref[...] = dot_nn(mt, dk_ref[...]).astype(BF)
    dwv_ref[...] = dot_nn(mt, dv_ref[...]).astype(BF)
    back, sums = norm_back_sums(r1_ref[...], gain_ref[...], dr1)
    da = back.astype(BF)
    dr1_ref[...] = back
    da_ref[...] = da
    dso_ref[...] = dot_tn(os_ref[...], da).astype(BF)
    put_rows(sum_ref, sums + [row_sum(da), row_sum(dq), row_sum(dv_ref[...])])


def cross_back(dc, co, cq, q2, k2, v2, p2, o2, x1b, memory, dr2, r1, gain, o, count):
    tokens, rows = dc.shape[0], dc.shape[0] // count
    keys = memory.shape[0] // count
    square = jax.ShapeDtypeStruct((D, D), BF)
    low = jax.ShapeDtypeStruct((tokens, D), BF)
    return pl.pallas_call(
        functools.partial(cross_back_kernel, count),
        out_shape=[square] * 5
        + [
            jax.ShapeDtypeStruct(memory.shape, BF),
            jax.ShapeDtypeStruct(memory.shape, BF),
            jax.ShapeDtypeStruct((tokens, D), F32),
            low,
            jax.ShapeDtypeStruct((8, D), F32),
        ],
        scratch_shapes=[
            pltpu.VMEM((tokens, D), BF),
            pltpu.VMEM((tokens, D), BF),
            pltpu.VMEM((H, keys, rows), F32),
            pltpu.VMEM((H, keys, rows), BF),
        ],
        compiler_params=pltpu.CompilerParams(vmem_limit_bytes=14 << 20),
        cost_estimate=LONG,
        name="cross_back",
    )(dc, co, cq, q2, k2, v2, p2, o2, x1b, memory, dr2, r1, gain, o)


def self_back_kernel(
    count,
    da_ref,
    wo_ref,
    q_ref,
    k_ref,
    v_ref,
    p_ref,
    x_ref,
    dwq_ref,
    dwk_ref,
    dwv_ref,
    dq_ref,
    dk_ref,
    dv_ref,
    sum_ref,
    g_ref,
    moved_ref,
    ds_ref,
):
    g_ref[...] = dot_nt(da_ref[...], wo_ref[...]).astype(BF)
    heads_back(
        count, q_ref, k_ref, v_ref, p_ref, g_ref, (dq_ref, dk_ref, dv_ref), moved_ref, ds_ref
    )
    xt = x_ref[...].T
    dwq_ref[...] = dot_nn(xt, dq_ref[...]).astype(BF)
    dwk_ref[...] = dot_nn(xt, dk_ref[...]).astype(BF)
    dwv_ref[...] = dot_nn(xt, dv_ref[...]).astype(BF)
    put_rows(sum_ref, [row_sum(dq_ref[...]), row_sum(dv_ref[...])])


def self_back(da, wo, q, k, v, p, x, count):
    tokens, rows = da.shape[0], da.shape[0] // count
    square = jax.ShapeDtypeStruct((D, D), BF)
    low = jax.ShapeDtypeStruct((tokens, D), BF)
    return pl.pallas_call(
        functools.partial(self_back_kernel, count),
        out_shape=[square] * 3 + [low] * 3 + [jax.ShapeDtypeStruct((8, D), F32)],
        scratch_shapes=[
            pltpu.VMEM((tokens, D), BF),
            pltpu.VMEM((H, rows, rows), F32),
            pltpu.VMEM((H, rows, rows), BF),
        ],
        compiler_params=pltpu.CompilerParams(vmem_limit_bytes=10 << 20),
        cost_estimate=LONG,
        name="self_back",
    )(da, wo, q, k, v, p, x)


def rows_back_kernel(n, *refs):
    total = None if len(refs) == 2 * n + 1 else refs[2 * n][...]
    for g, w in zip(refs[:n], refs[n : 2 * n]):
        part = dot_nt(g[...], w[...])
        total = part if total is None else total + part
    refs[-1][...] = total


def rows_back(grads, weights, start=()):
    return pl.pallas_call(
        functools.partial(rows_back_kernel, len(grads)),
        out_shape=jax.ShapeDtypeStruct(grads[0].shape, F32),
        compiler_params=pltpu.CompilerParams(vmem_limit_bytes=10 << 20),
        cost_estimate=LONG,
        name="rows_back",
    )(*grads, *weights, *start)


def norm(summed):
    centre = summed - jnp.mean(summed, axis=-1, keepdims=True)
    scale = lax.rsqrt(jnp.mean(centre * centre, axis=-1, keepdims=True) + EPS)
    return centre * scale, scale


def norm_back(normal, scale, gain, grad):
    inner = grad * gain
    back = scale * (
        inner
        - jnp.mean(inner, axis=-1, keepdims=True)
        - normal * jnp.mean(inner * normal, axis=-1, keepdims=True)
    )
    return back, jnp.sum(grad * normal, axis=0), jnp.sum(grad, axis=0)


def column_sum(value):
    return jnp.sum(value.astype(F32), axis=0)


def gelu_and_slope(value):
    spread = 0.5 * (1.0 + lax.erf(value * np.float32(np.sqrt(0.5))))
    density = jnp.exp(-0.5 * value * value) * np.float32(1.0 / np.sqrt(2.0 * np.pi))
    return value * spread, spread + value * density


def pack_kernel(sp_ref, so_ref, ab_ref, eb_ref, cb_ref, ng_ref, ns_ref, out_ref):
    rows, n = so_ref.shape[0], ab_ref.shape[1]
    for i in range(3):
        out_ref[i * rows : (i + 1) * rows] = sp_ref[i]
    out_ref[3 * rows : 4 * rows] = so_ref[...]

    def padded(v, width):
        v = v.astype(F32)
        if v.shape[0] < 8:
            v = jnp.concatenate([v, jnp.zeros((8 - v.shape[0], v.shape[1]), F32)])
        return jnp.concatenate([v, jnp.zeros((8, width - v.shape[1]), F32)], axis=1)

    first = jnp.concatenate([ab_ref[...].astype(F32), cb_ref[...].astype(F32)])
    second = jnp.concatenate([ng_ref[...].astype(F32), ns_ref[...].astype(F32)])
    out_ref[4 * rows :] = jnp.concatenate(
        [padded(first, 128), padded(second, 128), padded(eb_ref[...], D - 256)], axis=1
    ).astype(BF)


def pack_self(sp, so, ab, eb, cb, ng, ns):
    ins = [sp, so, ab, eb.reshape(1, -1), cb.reshape(1, -1), ng, ns]
    ins = [pltpu.with_memory_space_constraint(a, pltpu.HBM) for a in ins]
    return pl.pallas_call(
        pack_kernel,
        grid=(1,),
        in_specs=[
            pl.BlockSpec(a.shape, lambda i, n=a.ndim: (0,) * n) for a in ins
        ],
        out_specs=pl.BlockSpec((4 * so.shape[0] + 8, D), lambda i: (0, 0)),
        out_shape=jax.ShapeDtypeStruct((4 * so.shape[0] + 8, D), BF),
        compiler_params=pltpu.CompilerParams(vmem_limit_bytes=4 << 20),
        cost_estimate=QUICK,
        name="pack_self",
    )(*ins)


def pack_small(ab, eb, cb, ng, ns):
    n, wide = cb.shape[0], eb.shape[0]
    return jnp.concatenate(
        [
            jnp.pad(jnp.concatenate([ab, cb[None]]), ((0, 1), (0, 128 - n))),
            jnp.pad(jnp.concatenate([ng, ns]), ((0, 2), (0, 128 - n))),
            jnp.pad(eb[None], ((0, 7), (0, D - 256 - wide))),
        ],
        axis=1,
    )


def unpack_small_kernel(n, wide, in_ref, rows_ref, eb_ref):
    for d in range(in_ref.shape[0]):
        block = in_ref[d].astype(F32)
        rows_ref[0:8, d * n : (d + 1) * n] = block[:, 0:n]
        rows_ref[8:16, d * n : (d + 1) * n] = block[:, 128 : 128 + n]
        eb_ref[:, d * wide : (d + 1) * wide] = block[0:1, 256 : 256 + wide]


def unpack_small(gathered, n, wide):
    devices = gathered.shape[0]
    return pl.pallas_call(
        functools.partial(unpack_small_kernel, n, wide),
        out_shape=[
            jax.ShapeDtypeStruct((16, devices * n), F32),
            jax.ShapeDtypeStruct((1, devices * wide), F32),
        ],
        compiler_params=pltpu.CompilerParams(vmem_limit_bytes=8 << 20),
        cost_estimate=QUICK,
        name="unpack_small",
    )(gathered)


def split_small_kernel(n, wide, ff_ref, cross_ref, self_ref, db_ref, g3_ref, s3_ref, eb_ref, out_ref):
    zero = jnp.zeros((1, D), F32)
    first = jnp.concatenate(
        [
            self_ref[0:2],
            cross_ref[2:5],
            ff_ref[2:3],
            db_ref[...].reshape(1, D),
            zero,
        ],
        axis=0,
    )
    second = jnp.concatenate(
        [
            cross_ref[0:1],
            ff_ref[0:1],
            g3_ref[...].reshape(1, D),
            cross_ref[1:2],
            ff_ref[1:2],
            s3_ref[...].reshape(1, D),
            zero,
            zero,
        ],
        axis=0,
    )
    tail = jnp.broadcast_to(eb_ref[...], (8, FF))

    def padded(v, width):
        return jnp.concatenate([v, jnp.zeros((8, width - v.shape[1]), F32)], axis=1)

    for d in range(out_ref.shape[0]):
        out_ref[d] = jnp.concatenate(
            [
                padded(first[:, d * n : (d + 1) * n], 128),
                padded(second[:, d * n : (d + 1) * n], 128),
                padded(tail[:, d * wide : (d + 1) * wide], D - 256),
            ],
            axis=1,
        ).astype(BF)


def split_small(ff_sums, cross_sums, self_sums, vectors, eb, n, wide):
    devices = D // n
    return pl.pallas_call(
        functools.partial(split_small_kernel, n, wide),
        out_shape=jax.ShapeDtypeStruct((devices, 8, D), BF),
        compiler_params=pltpu.CompilerParams(vmem_limit_bytes=8 << 20),
        cost_estimate=QUICK,
        name="split_small",
    )(ff_sums, cross_sums, self_sums, *vectors, eb)


def body(
    layer_input,
    encoder_states,
    output_grad,
    span_start,
    span_length,
    self_project,
    self_output,
    cross_project,
    cross_output,
    attend_bias,
    expand_weight,
    expand_bias,
    contract_weight,
    contract_bias,
    norm_gain,
    norm_shift,
):
    place = Place()
    count, length = layer_input.shape[:2]
    shape = layer_input.shape
    rows = self_output.shape[0]
    wide = expand_bias.shape[0]
    fits = rows % 8 == 0 and place.bits == 2
    reduce = Reduce if fits else PlainReduce
    reduce_hop_last = ReduceHopLast if fits else PlainReduce
    x = layer_input.reshape(-1, D)
    memory = encoder_states.reshape(-1, D)
    grad_out = output_grad.reshape(-1, D).astype(F32)

    local_cross = jnp.concatenate([cross_project.reshape(-1, D), cross_output])
    four = [(i * rows, rows) for i in range(4)]
    if fits:
        g_self = Gather(
            place,
            pack_self(
                self_project,
                self_output,
                attend_bias,
                expand_bias,
                contract_bias,
                norm_gain,
                norm_shift,
            ),
        )
        line = g_self.column()
        g_self.hop(0, 0)
        g_self.hop(1, 0)
        g_cross = Gather(place, after(local_cross, line))
        g_self.blocks, g_cross.got = lax.optimization_barrier((g_self.blocks, g_cross.got))
        g_self.hop(1, 1)
        line = g_cross.column()
        g_cross.hop(0, 0)
        g_cross.hop(1, 0)
        g_expand = Gather(place, after(expand_weight, line))
        g_self.blocks, g_cross.blocks, g_expand.got = lax.optimization_barrier(
            (g_self.blocks, g_cross.blocks, g_expand.got)
        )
        g_cross.hop(1, 1)
        line = g_expand.column()
        g_expand.hop(0, 0)
        g_expand.hop(1, 0)
        g_contract = Gather(place, after(contract_weight, line))
        g_self.half(line)
        *w_self, smalls = g_self.spread(four + [(4 * rows, 8)])
        smalls = smalls.reshape(-1, 8, D)
    else:
        whole = lax.all_gather(
            jnp.concatenate(
                [
                    self_project.reshape(-1, D),
                    self_output,
                    pack_small(
                        attend_bias, expand_bias, contract_bias, norm_gain, norm_shift
                    ),
                    local_cross,
                    contract_weight,
                ]
            ),
            AXES,
            axis=0,
        )
        squares = [
            whole[:, a : a + rows].reshape(D, D)
            for a in [i * rows for i in range(4)]
            + [4 * rows + 8 + i * rows for i in range(4)]
        ]
        w_self, w_cross = squares[:4], squares[4:]
        contract = whole[:, 8 * rows + 8 :].reshape(FF, D)
        smalls = whole[:, 4 * rows : 4 * rows + 8]
        expand = lax.all_gather(expand_weight, AXES, axis=0, tiled=True)
    wq, wk, wv, wo = w_self
    small_rows, expand_b = unpack_small(smalls, rows, wide)
    biases = [small_rows[i : i + 1] for i in range(6)]
    contract_b = small_rows[6:7]
    gains = [small_rows[8 + i : 9 + i] for i in range(3)]
    shifts = [small_rows[11 + i : 12 + i] for i in range(3)]

    q = ((dot_nn(x, wq) + biases[0]) * 0.125).astype(BF)
    k = dot_nn(x, wk).astype(BF)
    v = (dot_nn(x, wv) + biases[1]).astype(BF)
    o, p = attend(q, k, v, span_start, span_length, True, count)
    if fits:
        g_cross.blocks, g_expand.blocks, g_contract.got, o = lax.optimization_barrier(
            (g_cross.blocks, g_expand.blocks, g_contract.got, o)
        )
        g_expand.hop(1, 1)
        line = g_contract.column()
        g_contract.hop(0, 0)
        g_contract.hop(1, 0)
        g_cross.half(line)
        w_cross = g_cross.spread(four)
    r1 = x.astype(F32) + (dot_nn(o, wo) + biases[2])
    n1, s1 = norm(r1)
    x1 = n1 * gains[0] + shifts[0]
    x1b = x1.astype(BF)
    cq, ck, cv, co = w_cross
    q2 = ((dot_nn(x1b, cq) + biases[3]) * 0.125).astype(BF)
    k2 = dot_nn(memory, ck).astype(BF)
    v2 = (dot_nn(memory, cv) + biases[4]).astype(BF)
    o2, p2 = attend(q2, k2, v2, span_start, span_length, False, count)
    if fits:
        g_expand.blocks, g_contract.blocks, o2 = lax.optimization_barrier(
            (g_expand.blocks, g_contract.blocks, o2)
        )
        g_contract.hop(1, 1)
        g_expand.half()
        (expand,) = g_expand.spread([(0, rows)])
    r2 = x1 + (dot_nn(o2, co) + biases[5])
    n2, s2 = norm(r2)
    x2 = n2 * gains[1] + shifts[1]
    x2b = x2.astype(BF)
    act, slope = gelu_and_slope(dot_nn(x2b, expand) + expand_b)
    act = act.astype(BF)
    slope = slope.astype(BF)
    if fits:
        g_contract.blocks[3] = after(g_contract.blocks[3], act)
        (contract,) = g_contract.spread([(0, 4 * rows)])
    n3, s3 = norm(x2 + (dot_nn(act, contract) + contract_b))
    output = (n3 * gains[2] + shifts[2]).astype(BF)

    dr3, gain3, shift3 = norm_back(n3, s3, gains[2], grad_out)
    df = dr3.astype(BF)
    d_contract = dot_tn(act, df).astype(BF)
    r_contract = reduce_hop_last(place, [owner_blocks(place, d_contract)])
    d_contract_b = column_sum(df)
    du, d_expand_b = hidden_back(after(df, d_contract), contract, slope)
    sent = r_contract.leave(0, du)
    d_expand = dot_tn(x2b, after(du, sent)).astype(BF)
    r_expand = reduce(place, [owner_blocks(place, d_expand)])
    dr2, dc, ff_sums = expand_back(
        after(du, r_expand.sent), expand, dr3, r2, gains[1]
    )
    sent = r_expand.leave(0, dc)
    sent = r_contract.line(sent)
    *d_cross, dk2, dv2, dr1, da, cross_sums = cross_back(
        after(dc, sent), co, cq, q2, k2, v2, p2, o2, x1b, memory, dr2, r1, gains[0], o, count
    )
    r_cross = reduce(place, [owner_blocks(place, d) for d in d_cross])
    sent = r_expand.leave(1, r_cross.sent)
    fence(place, sent)
    sent = r_cross.leave(0, place.spots)
    *d_self, dq, dk, dv, self_sums = self_back(after(da, sent), wo, q, k, v, p, x, count)
    sent = r_expand.last(self_sums)
    small_blocks = split_small(
        ff_sums,
        cross_sums,
        self_sums,
        [d_contract_b, gain3, shift3],
        d_expand_b,
        rows,
        wide,
    )
    small_blocks = small_blocks.reshape(place.dp_count, place.chips, 2, 8, D)
    r_self = reduce(
        place,
        [owner_blocks(place, d) for d in after(d_self, sent)] + [small_blocks],
    )
    sent = r_contract.turn(r_self.sent)
    encoder_grad = rows_back(after([dk2, dv2], sent), [ck, cv])
    sent = r_cross.leave(1, encoder_grad)
    (own_expand,) = r_expand.result([((rows, FF), 0, 0)], sent)
    (own_contract,) = r_contract.result([((4 * rows, D), 0, 0)], own_expand)
    input_grad = rows_back(after([dq, dk, dv], own_contract), [wq, wk, wv], [dr1])
    r_cross.got[-1] = after(r_cross.latest(), input_grad)
    sent = r_self.leave(0, r_cross.latest())
    sent = r_cross.last(sent)
    sent = r_self.leave(1, fence(place, sent))
    projects = ((3, rows, D), 0, 0)
    square = (rows, D)
    own_cross = r_cross.result(
        [projects, (square, 3 * rows, 0), (square, 4 * rows, 0)], sent
    )
    r_self.last(fence(place, own_cross[0]))
    at = 3 * rows
    own_self = r_self.result(
        [
            projects,
            ((6, rows), at, 0),
            ((1, wide), at, 256),
            ((1, rows), at + 6, 0),
            ((3, rows), at, 128),
            ((3, rows), at + 3, 128),
        ]
    )
    own_self = [own_self[0], own_cross[2], *own_self[1:]]
    return (
        output.reshape(shape),
        input_grad.reshape(shape),
        encoder_grad.reshape(encoder_states.shape),
        own_self[0],
        own_self[1],
        own_cross[0],
        own_cross[1],
        own_self[2],
        own_expand,
        own_self[3].reshape(-1),
        own_contract,
        own_self[4].reshape(-1),
        own_self[5],
        own_self[6],
    )


def solution(mesh):
    rows = P(AXES)
    return jax.shard_map(
        body,
        mesh=mesh,
        in_specs=(
            P(AXES, None, None),
            P(AXES, None, None),
            P(AXES, None, None),
            P(AXES),
            P(AXES),
            P(None, AXES, None),
            P(AXES, None),
            P(None, AXES, None),
            P(AXES, None),
            P(None, AXES),
            P(AXES, None),
            P(AXES),
            P(AXES, None),
            P(AXES),
            P(None, AXES),
            P(None, AXES),
        ),
        out_specs=(
            P(AXES, None, None),
            P(AXES, None, None),
            P(AXES, None, None),
            P(None, AXES, None),
            P(AXES, None),
            P(None, AXES, None),
            P(AXES, None),
            P(None, AXES),
            P(AXES, None),
            P(AXES),
            P(AXES, None),
            P(AXES),
            P(None, AXES),
            P(None, AXES),
        ),
        check_vma=False,
    )
```

```python
import functools

import jax
import jax.numpy as jnp
import numpy as np
from jax import lax
from jax.experimental import pallas as pl
from jax.experimental.pallas import tpu as pltpu
from jax.sharding import PartitionSpec as P

D = 768
H = 12
HD = 64
FF = 3072
AXES = ("dp", "fsdp")

EPS = 1e-05
BIG_NEGATIVE = -1000000000.0
BF = jnp.bfloat16
F32 = jnp.float32
QUICK = pl.CostEstimate(flops=1000, bytes_accessed=1000, transcendentals=0)
LONG = pl.CostEstimate(flops=4 * 10**10, bytes_accessed=10**6, transcendentals=0)


class Place:
    def __init__(self):
        self.dp_count = lax.axis_size("dp")
        self.inner = lax.axis_size("fsdp")
        self.chips = self.inner // 2
        self.bits = int(np.log2(self.dp_count))
        self.dp = lax.axis_index("dp")
        inner = lax.axis_index("fsdp")
        self.chip = inner // 2
        self.core = inner % 2
        table = []
        for dp in range(self.dp_count):
            for chip in range(self.chips):
                for core in range(2):
                    table.append(
                        [dp ^ self.mask(core, m) for m in range(self.dp_count)]
                        + [dp ^ self.mask(1 - core, m) for m in range(self.dp_count)]
                        + [(chip + k) % self.chips for k in range(self.chips)]
                        + [(chip - k) % self.chips for k in range(self.chips)]
                        + [core, 1 - core]
                    )
        index = self.dp * self.inner + inner
        self.spots = lax.dynamic_index_in_dim(
            jnp.asarray(np.array(table, np.int32)), index, 0, keepdims=False
        )
        self.theirs_at = self.dp_count
        self.up_at = 2 * self.dp_count
        self.down_at = self.up_at + self.chips
        self.core_at = self.down_at + self.chips

    def bit(self, core, step):
        return 1 << (self.bits - 1 - step if core == 0 else step)

    def mask(self, core, relative):
        return sum(self.bit(core, s) for s in range(self.bits) if relative >> s & 1)

    def permute(self, value, target):
        pairs = []
        for dp in range(self.dp_count):
            for chip in range(self.chips):
                for core in range(2):
                    to = target(dp, chip, core)
                    pairs.append(
                        (
                            dp * self.inner + chip * 2 + core,
                            to[0] * self.inner + to[1] * 2 + to[2],
                        )
                    )
        return lax.ppermute(value, AXES, pairs)

    def across_cores(self, value):
        return self.permute(value, lambda d, z, c: (d, z, 1 - c))

    def across_step(self, value, step):
        return self.permute(value, lambda d, z, c: (d ^ self.bit(c, step), z, c))

    def along_chips(self, value, shift):
        return self.permute(value, lambda d, z, c: (d, (z + shift) % self.chips, c))


def after(values, *earlier):
    return lax.optimization_barrier((values, earlier))[0]


def copy_kernel(plan, n_in, spots_ref, *refs):
    ins, outs, sems = refs[:n_in], refs[n_in:-1], refs[-1]
    copies = []
    for i, (source, source_at, target, target_at) in enumerate(plan):
        copies.append(
            pltpu.make_async_copy(
                ins[source].at[source_at(spots_ref)],
                outs[target].at[target_at(spots_ref)],
                sems.at[i],
            )
        )
    for c in copies:
        c.start()
    for c in copies:
        c.wait()


def copy_call(place, plan, ins, outs, name):
    anywhere = pl.BlockSpec(memory_space=pl.ANY)
    return pl.pallas_call(
        functools.partial(copy_kernel, plan, len(ins)),
        grid_spec=pltpu.PrefetchScalarGridSpec(
            num_scalar_prefetch=1,
            grid=(1,),
            in_specs=[anywhere] * len(ins),
            out_specs=[anywhere] * len(outs),
            scratch_shapes=[pltpu.SemaphoreType.DMA((len(plan),))],
        ),
        out_shape=outs,
        compiler_params=pltpu.CompilerParams(vmem_limit_bytes=1 << 20),
        cost_estimate=QUICK,
        name=name,
    )(place.spots, *ins)


def fence_kernel(in_ref, out_ref):
    for i in range(in_ref.shape[0]):
        out_ref[i] = in_ref[i]


def fence(place, *values):
    spots = place.spots
    scalars = pl.BlockSpec(memory_space=pltpu.SMEM)
    place.spots = pl.pallas_call(
        fence_kernel,
        in_specs=[scalars],
        out_specs=scalars,
        out_shape=jax.ShapeDtypeStruct(spots.shape, spots.dtype),
        compiler_params=pltpu.CompilerParams(vmem_limit_bytes=1 << 20),
        cost_estimate=LONG,
        name="fence",
    )(after(spots, *values))
    return place.spots


class Gather:
    def __init__(self, place, local):
        self.place = place
        self.local = local
        self.got = [local] + [
            place.along_chips(local, k) for k in range(1, place.chips)
        ]

    def column(self, *earlier):
        place = self.place
        self.got = after(self.got, *earlier)
        plan = [
            (
                k,
                lambda s: (slice(None),),
                0,
                lambda s, k=k: (s[place.down_at + k],),
            )
            for k in range(place.chips)
        ]
        shape = jax.ShapeDtypeStruct((place.chips,) + self.local.shape, BF)
        self.blocks = {0: copy_call(place, plan, self.got, [shape], "column")[0]}
        return self.blocks[0]

    def meet(self, later):
        self.blocks, later.got = lax.optimization_barrier((self.blocks, later.got))

    def hop(self, step, held, *earlier):
        self.blocks[held] = after(self.blocks[held], *earlier)
        self.blocks[held | 1 << step] = self.place.across_step(self.blocks[held], step)

    def share(self, held):
        return self.place.across_cores(self.blocks[held])

    def half(self, *earlier):
        place = self.place
        ins = after([self.blocks[m] for m in range(place.dp_count)], *earlier)
        plan = [
            (m, lambda s: (slice(None),), 0, lambda s, m=m: (s[m],))
            for m in range(place.dp_count)
        ]
        shape = jax.ShapeDtypeStruct((place.dp_count,) + ins[0].shape, BF)
        self.own_half = copy_call(place, plan, ins, [shape], "half")[0]
        self.other_half = place.across_cores(self.own_half)
        return self.own_half

    def spread(self, parts, *earlier):
        place = self.place
        cols = self.local.shape[1]
        whole = slice(None)
        if hasattr(self, "other_half"):
            ins = [self.own_half, self.other_half]
            places = [lambda s: (whole,), lambda s: (whole,)]
        else:
            ins = [self.blocks[m] for m in range(place.dp_count)]
            ins += [self.share(m) for m in range(place.dp_count)]
            places = [lambda s, m=m: (s[m],) for m in range(2 * place.dp_count)]
        ins = after(ins, *earlier)
        plan, outs = [], []
        for out, (first, rows) in enumerate(parts):
            outs.append(
                jax.ShapeDtypeStruct((place.dp_count, place.chips, 2, rows, cols), BF)
            )
            for m, where in enumerate(places):
                core = place.core_at + (m >= len(places) // 2)
                lead = (whole,) * (ins[m].ndim - 2)
                plan.append(
                    (
                        m,
                        lambda s, a=first, n=rows, lead=lead: lead + (pl.ds(a, n),),
                        out,
                        lambda s, where=where, core=core: where(s) + (whole, s[core]),
                    )
                )
        full = copy_call(place, plan, ins, outs, "spread")
        return [w.reshape(-1, cols) for w in full]


def side_by_side(refs):
    parts = [r[...].reshape(r.shape[1:2] + r.shape[-2:]) for r in refs]
    return parts[0] if len(parts) == 1 else jnp.concatenate(parts, axis=1)


def exchange_kernel(spots_ref, *refs):
    out = refs[-1]
    out[...] = side_by_side(refs[:-1]).reshape(out.shape)


def sum_refs(refs, n):
    value = side_by_side(refs[:n]).astype(F32)
    for a in refs[n:]:
        value = value + a[...].astype(F32).reshape(value.shape)
    return value


def leave_kernel(n, spots_ref, *refs):
    out = refs[-1]
    out[...] = sum_refs(refs[:-1], n).astype(BF).reshape(out.shape)


def last_kernel(n, each, chips, spots_ref, *refs):
    outs = refs[chips * each :]
    for k in range(chips):
        value = sum_refs(refs[k * each : (k + 1) * each], n)
        outs[k][...] = value.astype(outs[k].dtype).reshape(outs[k].shape)


def cut_kernel(parts, count, *refs):
    total = refs[0][...].astype(F32)
    for r in refs[1:count]:
        total = total + r[...].astype(F32)
    for (shape, row, col), out in zip(parts, refs[count:]):
        piece = total[row : row + int(np.prod(shape[:-1])), col : col + shape[-1]]
        out[...] = piece.reshape(shape)


def cut_sum(terms, parts):
    return pl.pallas_call(
        functools.partial(cut_kernel, parts, len(terms)),
        out_shape=[jax.ShapeDtypeStruct(s, F32) for s, _, _ in parts],
        compiler_params=pltpu.CompilerParams(vmem_limit_bytes=8 << 20),
        cost_estimate=QUICK,
        name="cut_sum",
    )(*terms)


class Reduce:
    def __init__(self, place, blocks):
        self.place = place
        self.blocks = blocks
        self.rows = sum(b.shape[3] for b in blocks)
        self.cols = blocks[0].shape[4]
        shape = (place.dp_count, place.chips, self.rows, self.cols)
        sent = self.call(
            exchange_kernel,
            (place.dp_count,),
            [
                pl.BlockSpec(
                    (1, place.chips, 1) + b.shape[3:],
                    lambda i, s: (i, 0, s[place.core_at + 1], 0, 0),
                )
                for b in blocks
            ],
            pl.BlockSpec((1,) + shape[1:], lambda i, s: (i, 0, 0, 0)),
            jax.ShapeDtypeStruct(shape, BF),
            "exchange",
        )(place.spots, *blocks)
        self.sent = sent
        self.other = place.across_cores(sent)
        self.got = []

    def call(self, kernel, grid, in_specs, out_specs, out_shape, name):
        return pl.pallas_call(
            kernel,
            grid_spec=pltpu.PrefetchScalarGridSpec(
                num_scalar_prefetch=1, grid=grid, in_specs=in_specs, out_specs=out_specs
            ),
            out_shape=out_shape,
            compiler_params=pltpu.CompilerParams(
                vmem_limit_bytes=(14 if name == "line" else 8) << 20
            ),
            cost_estimate=QUICK,
            name=name,
        )

    def leave(self, step, *earlier):
        place = self.place
        if step == 0:
            self.other = after(self.other, *earlier)
        else:
            self.got[-1] = after(self.got[-1], *earlier)
        count = 1 << (place.bits - 1 - step)
        chips, core = place.chips, place.core_at

        def spot(i, s):
            return s[(1 << step) + i * (2 << step)]

        shape = (count, chips, self.rows, self.cols)
        specs = [
            pl.BlockSpec(
                (1, chips, 1) + b.shape[3:], lambda i, s: (spot(i, s), 0, s[core], 0, 0)
            )
            for b in self.blocks
        ]
        specs.append(pl.BlockSpec((1,) + shape[1:], lambda i, s: (spot(i, s), 0, 0, 0)))
        for t in range(step):
            specs.append(
                pl.BlockSpec(
                    (1,) + shape[1:],
                    lambda i, s, t=t: ((1 << (step - t - 1)) + i * (1 << (step - t)), 0, 0, 0),
                )
            )
        sent = self.call(
            functools.partial(leave_kernel, len(self.blocks)),
            (count,),
            specs,
            pl.BlockSpec((1,) + shape[1:], lambda i, s: (i, 0, 0, 0)),
            jax.ShapeDtypeStruct(shape, BF),
            "leave",
        )(place.spots, *self.blocks, self.other, *self.got)
        self.got.append(place.across_step(sent, step))
        return sent

    def latest(self):
        return self.got[-1]

    def last(self, *earlier):
        place = self.place
        self.got[-1] = after(self.got[-1], *earlier)
        chips, core = place.chips, place.core_at
        specs, ins = [], []
        for k in range(chips):
            up = place.up_at + k
            for b in self.blocks:
                ins.append(b)
                specs.append(
                    pl.BlockSpec(
                        (1, 1, 1) + b.shape[3:],
                        lambda i, s, up=up: (s[0], s[up], s[core], 0, 0),
                    )
                )
            for n, g in enumerate([self.other] + self.got):
                ins.append(g)
                specs.append(
                    pl.BlockSpec(
                        (1, 1, self.rows, self.cols),
                        lambda i, s, up=up, n=n: (s[0] if n == 0 else 0, s[up], 0, 0),
                    )
                )
        own, *sent = self.call(
            functools.partial(last_kernel, len(self.blocks), len(ins) // chips, chips),
            (1,),
            specs,
            [pl.BlockSpec((self.rows, self.cols), lambda i, s: (0, 0))] * chips,
            [
                jax.ShapeDtypeStruct((self.rows, self.cols), F32 if k == 0 else BF)
                for k in range(chips)
            ],
            "last",
        )(place.spots, *ins)
        self.own = own
        self.came = [place.along_chips(v, k + 1) for k, v in enumerate(sent)]
        return own

    def result(self, parts, *earlier):
        self.came = after(self.came, *earlier)
        return cut_sum([self.own] + self.came, parts)


def line_kernel(n, each, chips, spots_ref, *refs):
    outs = refs[2 * chips * each :]
    for k in range(chips):
        for i in range(2):
            at = (2 * k + i) * each
            value = sum_refs(refs[at : at + each], n)
            outs[k][i] = value.astype(outs[k].dtype).reshape(outs[k].shape[1:])


def turn_kernel(own_ref, *refs):
    *came, keep_ref, send_ref = refs
    total = own_ref[...]
    for c in came:
        total = total + c[...].astype(F32)
    keep_ref[...] = total[0]
    send_ref[...] = total[1].astype(BF)


class ReduceHopLast(Reduce):
    def line(self, *earlier):
        place = self.place
        self.got[-1] = after(self.got[-1], *earlier)
        chips, core = place.chips, place.core_at
        specs, ins = [], []
        for k in range(chips):
            up = place.up_at + k
            for i in range(2):
                for b in self.blocks:
                    ins.append(b)
                    specs.append(
                        pl.BlockSpec(
                            (1, 1, 1) + b.shape[3:],
                            lambda _, s, up=up, i=i: (s[2 * i], s[up], s[core], 0, 0),
                        )
                    )
                ins.append(self.other)
                specs.append(
                    pl.BlockSpec(
                        (1, 1, self.rows, self.cols),
                        lambda _, s, up=up, i=i: (s[2 * i], s[up], 0, 0),
                    )
                )
                ins.append(self.got[0])
                specs.append(
                    pl.BlockSpec(
                        (1, 1, self.rows, self.cols),
                        lambda _, s, up=up, i=i: (i, s[up], 0, 0),
                    )
                )
        shape = (2, self.rows, self.cols)
        own, *sent = self.call(
            functools.partial(line_kernel, len(self.blocks), len(ins) // chips // 2, chips),
            (1,),
            specs,
            [pl.BlockSpec(shape, lambda _, s: (0, 0, 0))] * chips,
            [jax.ShapeDtypeStruct(shape, F32 if k == 0 else BF) for k in range(chips)],
            "line",
        )(place.spots, *ins)
        self.own = own
        self.came = [place.along_chips(v, k + 1) for k, v in enumerate(sent)]
        return own

    def turn(self, *earlier):
        came = after(self.came, *earlier)
        shape = (self.rows, self.cols)
        self.own, sent = pl.pallas_call(
            turn_kernel,
            out_shape=[jax.ShapeDtypeStruct(shape, F32), jax.ShapeDtypeStruct(shape, BF)],
            compiler_params=pltpu.CompilerParams(vmem_limit_bytes=8 << 20),
            cost_estimate=QUICK,
            name="turn",
        )(self.own, *came)
        self.came = [self.place.across_step(sent, 1)]
        return sent


def owner_blocks(place, gradient):
    rows = gradient.shape[0] // (place.dp_count * place.inner)
    return gradient.reshape(
        place.dp_count, place.chips, 2, rows, gradient.shape[-1]
    )


class PlainReduce:
    def __init__(self, place, blocks):
        devices = place.dp_count * place.inner
        flat = [b.reshape((devices,) + b.shape[3:]) for b in blocks]
        self.sum = lax.psum_scatter(
            jnp.concatenate(flat, axis=1), AXES, scatter_dimension=0, tiled=False
        )
        self.sent = self.sum

    def leave(self, step, *earlier):
        return self.sum

    def last(self, *earlier):
        return self.sum

    def latest(self):
        return self.sum

    got = [None]

    def line(self, *earlier):
        return self.sum

    def turn(self, *earlier):
        return self.sum

    def result(self, parts, *earlier):
        total = self.sum.astype(F32)
        return [
            total[r : r + int(np.prod(s[:-1])), c : c + s[-1]].reshape(s)
            for s, r, c in parts
        ]


def dot_nt(a, b):
    return lax.dot_general(a, b, (((1,), (1,)), ((), ())), preferred_element_type=F32)


def dot_nn(a, b):
    return jnp.dot(a, b, preferred_element_type=F32)


def dot_tn(a, b):
    return lax.dot_general(a, b, (((0,), (0,)), ((), ())), preferred_element_type=F32)


def head(h):
    return slice(h * HD, (h + 1) * HD)


def attend_kernel(
    masked, start_ref, length_ref, q_ref, k_ref, v_ref, o_ref, p_ref, scores_ref
):
    rows = q_ref.shape[0]
    keys = k_ref.shape[0]
    if masked:
        seq = pl.program_id(0)
        start = start_ref[seq]
        stop = start + length_ref[seq]
        key_at = lax.broadcasted_iota(jnp.int32, (keys, rows), 0)
        row_at = lax.broadcasted_iota(jnp.int32, (keys, rows), 1)
        inside = (key_at >= start) & (key_at < stop) & (row_at >= start) & (row_at < stop)
        hidden = jnp.where((key_at <= row_at) | inside, 0.0, BIG_NEGATIVE).astype(F32)
    for h in range(H):
        scores_ref[h] = dot_nt(k_ref[:, head(h)], q_ref[:, head(h)])
    for h in range(H):
        scores = scores_ref[h]
        if masked:
            scores = scores + hidden
        peak = jnp.max(scores, axis=0, keepdims=True)
        weights = jnp.exp(scores - peak)
        total = jnp.sum(weights, axis=0, keepdims=True)
        p_ref[0, h] = (weights * (1.0 / total)).astype(BF)
    values_t = v_ref[...].T
    pieces = [dot_nn(values_t[head(h)], p_ref[0, h]) for h in range(H)]
    o_ref[...] = jnp.concatenate(pieces, axis=0).T.astype(BF)


def attend(queries, keys, values, start, length, masked, count):
    rows = queries.shape[0] // count
    key_rows = keys.shape[0] // count
    block = lambda n: pl.BlockSpec((n, D), lambda s, *_: (s, 0))
    return pl.pallas_call(
        functools.partial(attend_kernel, masked),
        grid_spec=pltpu.PrefetchScalarGridSpec(
            num_scalar_prefetch=2,
            grid=(count,),
            in_specs=[block(rows), block(key_rows), block(key_rows)],
            out_specs=[
                block(rows),
                pl.BlockSpec((1, H, key_rows, rows), lambda s, *_: (s, 0, 0, 0)),
            ],
            scratch_shapes=[pltpu.VMEM((H, key_rows, rows), F32)],
        ),
        out_shape=[
            jax.ShapeDtypeStruct(queries.shape, BF),
            jax.ShapeDtypeStruct((count, H, key_rows, rows), BF),
        ],
        compiler_params=pltpu.CompilerParams(vmem_limit_bytes=14 << 20),
        cost_estimate=QUICK,
        name="attend",
    )(start, length, queries, keys, values)


def norm_parts(summed):
    centre = summed - jnp.mean(summed, axis=-1, keepdims=True)
    scale = lax.rsqrt(jnp.mean(centre * centre, axis=-1, keepdims=True) + EPS)
    return centre * scale, scale


def row_sum(value):
    return jnp.sum(value.astype(F32), axis=0, keepdims=True)


def norm_back_sums(summed, gain, grad):
    normal, scale = norm_parts(summed)
    inner = grad * gain
    back = scale * (
        inner
        - jnp.mean(inner, axis=-1, keepdims=True)
        - normal * jnp.mean(inner * normal, axis=-1, keepdims=True)
    )
    return back, [row_sum(grad * normal), row_sum(grad)]


def put_rows(ref, rows):
    for i, r in enumerate(rows):
        ref[i : i + 1] = r


def hidden_back_kernel(df_ref, c_ref, slope_ref, du_ref, sum_ref):
    du = (dot_nt(df_ref[...], c_ref[...]) * slope_ref[...].astype(F32)).astype(BF)
    du_ref[...] = du
    sum_ref[...] = row_sum(du)


def hidden_back(df, contract, slope):
    tokens = df.shape[0]
    return pl.pallas_call(
        hidden_back_kernel,
        grid=(FF // D,),
        in_specs=[
            pl.BlockSpec((tokens, D), lambda j: (0, 0)),
            pl.BlockSpec((D, D), lambda j: (j, 0)),
            pl.BlockSpec((tokens, D), lambda j: (0, j)),
        ],
        out_specs=[
            pl.BlockSpec((tokens, D), lambda j: (0, j)),
            pl.BlockSpec((1, D), lambda j: (0, j)),
        ],
        out_shape=[
            jax.ShapeDtypeStruct((tokens, FF), BF),
            jax.ShapeDtypeStruct((1, FF), F32),
        ],
        compiler_params=pltpu.CompilerParams(vmem_limit_bytes=16 << 20),
        cost_estimate=LONG,
        name="hidden_back",
    )(df, contract, slope)


def expand_back_kernel(
    du_ref, e_ref, dr3_ref, r2_ref, gain_ref, dr2_ref, dc_ref, sum_ref
):
    j = pl.program_id(0)

    @pl.when(j == 0)
    def _():
        dr2_ref[...] = dr3_ref[...]

    dr2_ref[...] += dot_nt(du_ref[...], e_ref[...])

    @pl.when(j == pl.num_programs(0) - 1)
    def _():
        back, sums = norm_back_sums(r2_ref[...], gain_ref[...], dr2_ref[...])
        dc = back.astype(BF)
        dr2_ref[...] = back
        dc_ref[...] = dc
        put_rows(sum_ref, sums + [row_sum(dc)])


def expand_back(du, expand, dr3, r2, gain):
    tokens = du.shape[0]
    still = pl.BlockSpec((tokens, D), lambda j: (0, 0))
    moving = lambda n: pl.BlockSpec((n, D), lambda j: (0, j))
    return pl.pallas_call(
        expand_back_kernel,
        grid=(FF // D,),
        in_specs=[
            moving(tokens),
            moving(D),
            still,
            still,
            pl.BlockSpec((1, D), lambda j: (0, 0)),
        ],
        out_specs=[still, still, pl.BlockSpec((8, D), lambda j: (0, 0))],
        out_shape=[
            jax.ShapeDtypeStruct((tokens, D), F32),
            jax.ShapeDtypeStruct((tokens, D), BF),
            jax.ShapeDtypeStruct((8, D), F32),
        ],
        compiler_params=pltpu.CompilerParams(vmem_limit_bytes=20 << 20),
        cost_estimate=LONG,
        name="expand_back",
    )(du, expand, dr3, r2, gain)


def heads_back(count, q_ref, k_ref, v_ref, p_ref, g_ref, outs, moved_ref, ds_ref):
    rows = q_ref.shape[0] // count
    keys = k_ref.shape[0] // count
    for s in range(count):
        at = slice(s * rows, (s + 1) * rows)
        key_at = slice(s * keys, (s + 1) * keys)
        for h in range(H):
            moved_ref[h] = dot_nt(v_ref[key_at, head(h)], g_ref[at, head(h)])
        for h in range(H):
            weights = p_ref[s, h].astype(F32)
            moved = moved_ref[h]
            centre = jnp.sum(weights * moved, axis=0, keepdims=True)
            ds_ref[h] = (weights * (moved - centre)).astype(BF)
        keys_t = k_ref[key_at].T
        dq, dk, dv = [], [], []
        for h in range(H):
            dk.append(dot_nn(ds_ref[h], q_ref[at, head(h)]))
            dv.append(dot_nn(p_ref[s, h], g_ref[at, head(h)]))
            dq.append(dot_nn(keys_t[head(h)], ds_ref[h]))
        outs[0][at] = (jnp.concatenate(dq, axis=0).T.astype(BF) * 0.125).astype(BF)
        outs[1][key_at] = jnp.concatenate(dk, axis=1).astype(BF)
        outs[2][key_at] = jnp.concatenate(dv, axis=1).astype(BF)


def cross_back_kernel(
    count,
    dc_ref,
    co_ref,
    cq_ref,
    q_ref,
    k_ref,
    v_ref,
    p_ref,
    o_ref,
    x_ref,
    m_ref,
    dr2_ref,
    r1_ref,
    gain_ref,
    os_ref,
    dwq_ref,
    dwk_ref,
    dwv_ref,
    dwo_ref,
    dso_ref,
    dk_ref,
    dv_ref,
    dr1_ref,
    da_ref,
    sum_ref,
    g_ref,
    dq_ref,
    moved_ref,
    ds_ref,
):
    dc = dc_ref[...]
    g_ref[...] = dot_nt(dc, co_ref[...]).astype(BF)
    dwo_ref[...] = dot_tn(o_ref[...], dc).astype(BF)
    heads_back(
        count, q_ref, k_ref, v_ref, p_ref, g_ref, (dq_ref, dk_ref, dv_ref), moved_ref, ds_ref
    )
    dq = dq_ref[...]
    dr1 = dr2_ref[...] + dot_nt(dq, cq_ref[...])
    dwq_ref[...] = dot_tn(x_ref[...], dq).astype(BF)
    mt = m_ref[...].T
    dwk_ref[...] = dot_nn(mt, dk_ref[...]).astype(BF)
    dwv_ref[...] = dot_nn(mt, dv_ref[...]).astype(BF)
    back, sums = norm_back_sums(r1_ref[...], gain_ref[...], dr1)
    da = back.astype(BF)
    dr1_ref[...] = back
    da_ref[...] = da
    dso_ref[...] = dot_tn(os_ref[...], da).astype(BF)
    put_rows(sum_ref, sums + [row_sum(da), row_sum(dq), row_sum(dv_ref[...])])


def cross_back(dc, co, cq, q2, k2, v2, p2, o2, x1b, memory, dr2, r1, gain, o, count):
    tokens, rows = dc.shape[0], dc.shape[0] // count
    keys = memory.shape[0] // count
    square = jax.ShapeDtypeStruct((D, D), BF)
    low = jax.ShapeDtypeStruct((tokens, D), BF)
    return pl.pallas_call(
        functools.partial(cross_back_kernel, count),
        out_shape=[square] * 5
        + [
            jax.ShapeDtypeStruct(memory.shape, BF),
            jax.ShapeDtypeStruct(memory.shape, BF),
            jax.ShapeDtypeStruct((tokens, D), F32),
            low,
            jax.ShapeDtypeStruct((8, D), F32),
        ],
        scratch_shapes=[
            pltpu.VMEM((tokens, D), BF),
            pltpu.VMEM((tokens, D), BF),
            pltpu.VMEM((H, keys, rows), F32),
            pltpu.VMEM((H, keys, rows), BF),
        ],
        compiler_params=pltpu.CompilerParams(vmem_limit_bytes=14 << 20),
        cost_estimate=LONG,
        name="cross_back",
    )(dc, co, cq, q2, k2, v2, p2, o2, x1b, memory, dr2, r1, gain, o)


def self_back_kernel(
    count,
    da_ref,
    wo_ref,
    q_ref,
    k_ref,
    v_ref,
    p_ref,
    x_ref,
    dwq_ref,
    dwk_ref,
    dwv_ref,
    dq_ref,
    dk_ref,
    dv_ref,
    sum_ref,
    g_ref,
    moved_ref,
    ds_ref,
):
    g_ref[...] = dot_nt(da_ref[...], wo_ref[...]).astype(BF)
    heads_back(
        count, q_ref, k_ref, v_ref, p_ref, g_ref, (dq_ref, dk_ref, dv_ref), moved_ref, ds_ref
    )
    xt = x_ref[...].T
    dwq_ref[...] = dot_nn(xt, dq_ref[...]).astype(BF)
    dwk_ref[...] = dot_nn(xt, dk_ref[...]).astype(BF)
    dwv_ref[...] = dot_nn(xt, dv_ref[...]).astype(BF)
    put_rows(sum_ref, [row_sum(dq_ref[...]), row_sum(dv_ref[...])])


def self_back(da, wo, q, k, v, p, x, count):
    tokens, rows = da.shape[0], da.shape[0] // count
    square = jax.ShapeDtypeStruct((D, D), BF)
    low = jax.ShapeDtypeStruct((tokens, D), BF)
    return pl.pallas_call(
        functools.partial(self_back_kernel, count),
        out_shape=[square] * 3 + [low] * 3 + [jax.ShapeDtypeStruct((8, D), F32)],
        scratch_shapes=[
            pltpu.VMEM((tokens, D), BF),
            pltpu.VMEM((H, rows, rows), F32),
            pltpu.VMEM((H, rows, rows), BF),
        ],
        compiler_params=pltpu.CompilerParams(vmem_limit_bytes=10 << 20),
        cost_estimate=LONG,
        name="self_back",
    )(da, wo, q, k, v, p, x)


def rows_back_kernel(n, *refs):
    total = None if len(refs) == 2 * n + 1 else refs[2 * n][...]
    for g, w in zip(refs[:n], refs[n : 2 * n]):
        part = dot_nt(g[...], w[...])
        total = part if total is None else total + part
    refs[-1][...] = total


def rows_back(grads, weights, start=()):
    return pl.pallas_call(
        functools.partial(rows_back_kernel, len(grads)),
        out_shape=jax.ShapeDtypeStruct(grads[0].shape, F32),
        compiler_params=pltpu.CompilerParams(vmem_limit_bytes=10 << 20),
        cost_estimate=LONG,
        name="rows_back",
    )(*grads, *weights, *start)


def norm(summed):
    centre = summed - jnp.mean(summed, axis=-1, keepdims=True)
    scale = lax.rsqrt(jnp.mean(centre * centre, axis=-1, keepdims=True) + EPS)
    return centre * scale, scale


def norm_back(normal, scale, gain, grad):
    inner = grad * gain
    back = scale * (
        inner
        - jnp.mean(inner, axis=-1, keepdims=True)
        - normal * jnp.mean(inner * normal, axis=-1, keepdims=True)
    )
    return back, jnp.sum(grad * normal, axis=0), jnp.sum(grad, axis=0)


def column_sum(value):
    return jnp.sum(value.astype(F32), axis=0)


def gelu_and_slope(value):
    spread = 0.5 * (1.0 + lax.erf(value * np.float32(np.sqrt(0.5))))
    density = jnp.exp(-0.5 * value * value) * np.float32(1.0 / np.sqrt(2.0 * np.pi))
    return value * spread, spread + value * density


def pack_kernel(sp_ref, so_ref, ab_ref, eb_ref, cb_ref, ng_ref, ns_ref, out_ref):
    rows, n = so_ref.shape[0], ab_ref.shape[1]
    for i in range(3):
        out_ref[i * rows : (i + 1) * rows] = sp_ref[i]
    out_ref[3 * rows : 4 * rows] = so_ref[...]

    def padded(v, width):
        v = v.astype(F32)
        if v.shape[0] < 8:
            v = jnp.concatenate([v, jnp.zeros((8 - v.shape[0], v.shape[1]), F32)])
        return jnp.concatenate([v, jnp.zeros((8, width - v.shape[1]), F32)], axis=1)

    first = jnp.concatenate([ab_ref[...].astype(F32), cb_ref[...].astype(F32)])
    second = jnp.concatenate([ng_ref[...].astype(F32), ns_ref[...].astype(F32)])
    out_ref[4 * rows :] = jnp.concatenate(
        [padded(first, 128), padded(second, 128), padded(eb_ref[...], D - 256)], axis=1
    ).astype(BF)


def pack_self(sp, so, ab, eb, cb, ng, ns):
    ins = [sp, so, ab, eb.reshape(1, -1), cb.reshape(1, -1), ng, ns]
    ins = [pltpu.with_memory_space_constraint(a, pltpu.HBM) for a in ins]
    return pl.pallas_call(
        pack_kernel,
        grid=(1,),
        in_specs=[
            pl.BlockSpec(a.shape, lambda i, n=a.ndim: (0,) * n) for a in ins
        ],
        out_specs=pl.BlockSpec((4 * so.shape[0] + 8, D), lambda i: (0, 0)),
        out_shape=jax.ShapeDtypeStruct((4 * so.shape[0] + 8, D), BF),
        compiler_params=pltpu.CompilerParams(vmem_limit_bytes=4 << 20),
        cost_estimate=QUICK,
        name="pack_self",
    )(*ins)


def pack_small(ab, eb, cb, ng, ns):
    n, wide = cb.shape[0], eb.shape[0]
    return jnp.concatenate(
        [
            jnp.pad(jnp.concatenate([ab, cb[None]]), ((0, 1), (0, 128 - n))),
            jnp.pad(jnp.concatenate([ng, ns]), ((0, 2), (0, 128 - n))),
            jnp.pad(eb[None], ((0, 7), (0, D - 256 - wide))),
        ],
        axis=1,
    )


def unpack_small_kernel(n, wide, in_ref, rows_ref, eb_ref):
    for d in range(in_ref.shape[0]):
        block = in_ref[d].astype(F32)
        rows_ref[0:8, d * n : (d + 1) * n] = block[:, 0:n]
        rows_ref[8:16, d * n : (d + 1) * n] = block[:, 128 : 128 + n]
        eb_ref[:, d * wide : (d + 1) * wide] = block[0:1, 256 : 256 + wide]


def unpack_small(gathered, n, wide):
    devices = gathered.shape[0]
    return pl.pallas_call(
        functools.partial(unpack_small_kernel, n, wide),
        out_shape=[
            jax.ShapeDtypeStruct((16, devices * n), F32),
            jax.ShapeDtypeStruct((1, devices * wide), F32),
        ],
        compiler_params=pltpu.CompilerParams(vmem_limit_bytes=8 << 20),
        cost_estimate=QUICK,
        name="unpack_small",
    )(gathered)


def split_small_kernel(n, wide, ff_ref, cross_ref, self_ref, db_ref, g3_ref, s3_ref, eb_ref, out_ref):
    zero = jnp.zeros((1, D), F32)
    first = jnp.concatenate(
        [
            self_ref[0:2],
            cross_ref[2:5],
            ff_ref[2:3],
            db_ref[...].reshape(1, D),
            zero,
        ],
        axis=0,
    )
    second = jnp.concatenate(
        [
            cross_ref[0:1],
            ff_ref[0:1],
            g3_ref[...].reshape(1, D),
            cross_ref[1:2],
            ff_ref[1:2],
            s3_ref[...].reshape(1, D),
            zero,
            zero,
        ],
        axis=0,
    )
    tail = jnp.broadcast_to(eb_ref[...], (8, FF))

    def padded(v, width):
        return jnp.concatenate([v, jnp.zeros((8, width - v.shape[1]), F32)], axis=1)

    for d in range(out_ref.shape[0]):
        out_ref[d] = jnp.concatenate(
            [
                padded(first[:, d * n : (d + 1) * n], 128),
                padded(second[:, d * n : (d + 1) * n], 128),
                padded(tail[:, d * wide : (d + 1) * wide], D - 256),
            ],
            axis=1,
        ).astype(BF)


def split_small(ff_sums, cross_sums, self_sums, vectors, eb, n, wide):
    devices = D // n
    return pl.pallas_call(
        functools.partial(split_small_kernel, n, wide),
        out_shape=jax.ShapeDtypeStruct((devices, 8, D), BF),
        compiler_params=pltpu.CompilerParams(vmem_limit_bytes=8 << 20),
        cost_estimate=QUICK,
        name="split_small",
    )(ff_sums, cross_sums, self_sums, *vectors, eb)


def body(
    layer_input,
    encoder_states,
    output_grad,
    span_start,
    span_length,
    self_project,
    self_output,
    cross_project,
    cross_output,
    attend_bias,
    expand_weight,
    expand_bias,
    contract_weight,
    contract_bias,
    norm_gain,
    norm_shift,
):
    place = Place()
    count, length = layer_input.shape[:2]
    shape = layer_input.shape
    rows = self_output.shape[0]
    wide = expand_bias.shape[0]
    fits = rows % 8 == 0 and place.bits == 2
    reduce = Reduce if fits else PlainReduce
    reduce_hop_last = ReduceHopLast if fits else PlainReduce
    x = layer_input.reshape(-1, D)
    memory = encoder_states.reshape(-1, D)
    grad_out = output_grad.reshape(-1, D).astype(F32)

    local_cross = jnp.concatenate([cross_project.reshape(-1, D), cross_output])
    four = [(i * rows, rows) for i in range(4)]
    if fits:
        g_self = Gather(
            place,
            pack_self(
                self_project,
                self_output,
                attend_bias,
                expand_bias,
                contract_bias,
                norm_gain,
                norm_shift,
            ),
        )
        line = g_self.column()
        g_self.hop(0, 0)
        g_self.hop(1, 0)
        g_cross = Gather(place, after(local_cross, line))
        g_self.blocks, g_cross.got = lax.optimization_barrier((g_self.blocks, g_cross.got))
        g_self.hop(1, 1)
        line = g_cross.column()
        g_cross.hop(0, 0)
        g_cross.hop(1, 0)
        g_expand = Gather(place, after(expand_weight, line))
        g_self.blocks, g_cross.blocks, g_expand.got = lax.optimization_barrier(
            (g_self.blocks, g_cross.blocks, g_expand.got)
        )
        g_cross.hop(1, 1)
        line = g_expand.column()
        g_expand.hop(0, 0)
        g_expand.hop(1, 0)
        g_self.half(line)
        *w_self, smalls = g_self.spread(four + [(4 * rows, 8)])
        g_contract = Gather(place, after(contract_weight, smalls))
        smalls = smalls.reshape(-1, 8, D)
    else:
        whole = lax.all_gather(
            jnp.concatenate(
                [
                    self_project.reshape(-1, D),
                    self_output,
                    pack_small(
                        attend_bias, expand_bias, contract_bias, norm_gain, norm_shift
                    ),
                    local_cross,
                    contract_weight,
                ]
            ),
            AXES,
            axis=0,
        )
        squares = [
            whole[:, a : a + rows].reshape(D, D)
            for a in [i * rows for i in range(4)]
            + [4 * rows + 8 + i * rows for i in range(4)]
        ]
        w_self, w_cross = squares[:4], squares[4:]
        contract = whole[:, 8 * rows + 8 :].reshape(FF, D)
        smalls = whole[:, 4 * rows : 4 * rows + 8]
        expand = lax.all_gather(expand_weight, AXES, axis=0, tiled=True)
    wq, wk, wv, wo = w_self
    small_rows, expand_b = unpack_small(smalls, rows, wide)
    biases = [small_rows[i : i + 1] for i in range(6)]
    contract_b = small_rows[6:7]
    gains = [small_rows[8 + i : 9 + i] for i in range(3)]
    shifts = [small_rows[11 + i : 12 + i] for i in range(3)]

    q = ((dot_nn(x, wq) + biases[0]) * 0.125).astype(BF)
    k = dot_nn(x, wk).astype(BF)
    v = (dot_nn(x, wv) + biases[1]).astype(BF)
    o, p = attend(q, k, v, span_start, span_length, True, count)
    if fits:
        g_cross.blocks, g_expand.blocks, g_contract.got, o = lax.optimization_barrier(
            (g_cross.blocks, g_expand.blocks, g_contract.got, o)
        )
        g_expand.hop(1, 1)
        line = g_contract.column()
        g_contract.hop(0, 0)
        g_contract.hop(1, 0)
        g_cross.half(line)
        w_cross = g_cross.spread(four)
    r1 = x.astype(F32) + (dot_nn(o, wo) + biases[2])
    n1, s1 = norm(r1)
    x1 = n1 * gains[0] + shifts[0]
    x1b = x1.astype(BF)
    cq, ck, cv, co = w_cross
    q2 = ((dot_nn(x1b, cq) + biases[3]) * 0.125).astype(BF)
    k2 = dot_nn(memory, ck).astype(BF)
    v2 = (dot_nn(memory, cv) + biases[4]).astype(BF)
    o2, p2 = attend(q2, k2, v2, span_start, span_length, False, count)
    if fits:
        g_expand.blocks, g_contract.blocks, o2 = lax.optimization_barrier(
            (g_expand.blocks, g_contract.blocks, o2)
        )
        g_contract.hop(1, 1)
        g_expand.half()
        (expand,) = g_expand.spread([(0, rows)])
    r2 = x1 + (dot_nn(o2, co) + biases[5])
    n2, s2 = norm(r2)
    x2 = n2 * gains[1] + shifts[1]
    x2b = x2.astype(BF)
    act, slope = gelu_and_slope(dot_nn(x2b, expand) + expand_b)
    act = act.astype(BF)
    slope = slope.astype(BF)
    if fits:
        g_contract.blocks[3] = after(g_contract.blocks[3], act)
        (contract,) = g_contract.spread([(0, 4 * rows)])
    n3, s3 = norm(x2 + (dot_nn(act, contract) + contract_b))
    output = (n3 * gains[2] + shifts[2]).astype(BF)

    dr3, gain3, shift3 = norm_back(n3, s3, gains[2], grad_out)
    df = dr3.astype(BF)
    d_contract = dot_tn(act, df).astype(BF)
    r_contract = reduce_hop_last(place, [owner_blocks(place, d_contract)])
    d_contract_b = column_sum(df)
    du, d_expand_b = hidden_back(after(df, d_contract), contract, slope)
    sent = r_contract.leave(0, du)
    d_expand = dot_tn(x2b, after(du, sent)).astype(BF)
    r_expand = reduce(place, [owner_blocks(place, d_expand)])
    dr2, dc, ff_sums = expand_back(
        after(du, r_expand.sent), expand, dr3, r2, gains[1]
    )
    sent = r_expand.leave(0, dc)
    sent = r_contract.line(sent)
    *d_cross, dk2, dv2, dr1, da, cross_sums = cross_back(
        after(dc, sent), co, cq, q2, k2, v2, p2, o2, x1b, memory, dr2, r1, gains[0], o, count
    )
    r_cross = reduce(place, [owner_blocks(place, d) for d in d_cross])
    sent = r_expand.leave(1, r_cross.sent)
    fence(place, sent)
    sent = r_cross.leave(0, place.spots)
    *d_self, dq, dk, dv, self_sums = self_back(after(da, sent), wo, q, k, v, p, x, count)
    sent = r_expand.last(self_sums)
    small_blocks = split_small(
        ff_sums,
        cross_sums,
        self_sums,
        [d_contract_b, gain3, shift3],
        d_expand_b,
        rows,
        wide,
    )
    small_blocks = small_blocks.reshape(place.dp_count, place.chips, 2, 8, D)
    r_self = reduce(
        place,
        [owner_blocks(place, d) for d in after(d_self, sent)] + [small_blocks],
    )
    sent = r_contract.turn(r_self.sent)
    encoder_grad = rows_back(after([dk2, dv2], sent), [ck, cv])
    sent = r_cross.leave(1, encoder_grad)
    (own_expand,) = r_expand.result([((rows, FF), 0, 0)], sent)
    (own_contract,) = r_contract.result([((4 * rows, D), 0, 0)], own_expand)
    input_grad = rows_back(after([dq, dk, dv], own_contract), [wq, wk, wv], [dr1])
    r_cross.got[-1] = after(r_cross.latest(), input_grad)
    sent = r_self.leave(0, r_cross.latest())
    sent = r_cross.last(sent)
    sent = r_self.leave(1, fence(place, sent))
    projects = ((3, rows, D), 0, 0)
    square = (rows, D)
    own_cross = r_cross.result(
        [projects, (square, 3 * rows, 0), (square, 4 * rows, 0)], sent
    )
    r_self.last(fence(place, own_cross[0]))
    at = 3 * rows
    own_self = r_self.result(
        [
            projects,
            ((6, rows), at, 0),
            ((1, wide), at, 256),
            ((1, rows), at + 6, 0),
            ((3, rows), at, 128),
            ((3, rows), at + 3, 128),
        ]
    )
    own_self = [own_self[0], own_cross[2], *own_self[1:]]
    return (
        output.reshape(shape),
        input_grad.reshape(shape),
        encoder_grad.reshape(encoder_states.shape),
        own_self[0],
        own_self[1],
        own_cross[0],
        own_cross[1],
        own_self[2],
        own_expand,
        own_self[3].reshape(-1),
        own_contract,
        own_self[4].reshape(-1),
        own_self[5],
        own_self[6],
    )


def solution(mesh):
    rows = P(AXES)
    return jax.shard_map(
        body,
        mesh=mesh,
        in_specs=(
            P(AXES, None, None),
            P(AXES, None, None),
            P(AXES, None, None),
            P(AXES),
            P(AXES),
            P(None, AXES, None),
            P(AXES, None),
            P(None, AXES, None),
            P(AXES, None),
            P(None, AXES),
            P(AXES, None),
            P(AXES),
            P(AXES, None),
            P(AXES),
            P(None, AXES),
            P(None, AXES),
        ),
        out_specs=(
            P(AXES, None, None),
            P(AXES, None, None),
            P(AXES, None, None),
            P(None, AXES, None),
            P(AXES, None),
            P(None, AXES, None),
            P(AXES, None),
            P(None, AXES),
            P(AXES, None),
            P(AXES),
            P(AXES, None),
            P(AXES),
            P(None, AXES),
            P(None, AXES),
        ),
        check_vma=False,
    )
```
